32 devices in a mesh: lat: 8 (over z, x), section: 4 (over y, core).
Axes of the slice: x: 2, y: 2, z: 4, core: 2. Of those that a mesh axis runs over, the one named last changes fastest.
Arguments:
- saved_input: bfloat16 [4, 2, 4096, 256], P('section', None, 'lat'), may hold values from -6 to 6
- cotangent: bfloat16 [2, 4096, 256], P(None, 'lat'), may hold values from -6 to 6
- quad_values: bfloat16 [3, 64, 5, 64, 64], P(None, 'lat'), may hold values from -0.3125 to 0.3125
- block_index: int32 [64, 5], P('lat'), may hold values from 0 to 63, as said below
- block_mask: int32 [64, 5], P('lat'), may hold values from 0 to 1
- weights: bfloat16 [4, 3, 256, 256], P('section'), may hold values from -0.21875 to 0.21875
Outputs:
- grad_input: bfloat16 [4, 2, 4096, 256], P('section', None, 'lat')
- grad_weight: float32 [4, 3, 256, 256], P('section')
The draws below stay inside these ranges and needn't reach their ends.
Inputs may be any that keep to these rules, and one draw needn't show every extreme that they name: block_index[b, j] lies within 2 blocks of b; entries of one row name distinct blocks where block_mask is 1.
All inputs are finite; a program needn't handle non-finite values.
Results may differ from the reference program's by a relative error of at most 0.0085.
Values may be sent and summed in bfloat16 or wider, within the bound.
No kernel may reach another device: no remote copies, remote signals or barrier semaphores. Data moves between devices by JAX's collectives and lax.ppermute only.
A program may use at most 64 MiB of HBM per device.

```python
import jax
import jax.numpy as jnp
from jax import lax

C = 256
KB = 3
BLK = 64
HALO = 2
NNZ = 5
MB = 2
LAYERS = 4
NBLK = 64
POINTS = 4096


def quad_pattern(key):
    pattern_key = jax.random.fold_in(key, 7)
    scores = jax.random.randint(pattern_key, (NBLK, NNZ), 0, 1 << 20) * NNZ + jnp.arange(NNZ, dtype=jnp.int32)[None, :]
    ranked = jnp.argsort(scores, axis=1).astype(jnp.int32)
    offset = ranked - HALO
    block_rows = jnp.arange(NBLK, dtype=jnp.int32)[:, None]
    target = block_rows + offset
    quarter = max(NBLK // 4, 1)
    distance = jnp.minimum(block_rows, NBLK - 1 - block_rows)
    support = NNZ - (NNZ - 2) * jnp.minimum(distance, quarter) // quarter
    nonzero = (jnp.arange(NNZ, dtype=jnp.int32)[None, :] < support) & (target >= 0) & (target < NBLK)
    return (jnp.clip(target, 0, NBLK - 1).astype(jnp.int32), nonzero.astype(jnp.int32))


def draw_block_index(key, part):
    return quad_pattern(key)[0]


def draw_block_mask(key, part):
    return quad_pattern(key)[1]


def shard_levels(stream_key, dims, shards, least, top_value):
    loudness, own = 1.0, jax.random.fold_in(stream_key, 6)
    for dim, parts in shards:
        draws = jnp.exp(jax.random.uniform(jax.random.fold_in(own, dim), (parts,), jnp.float32, least / len(shards), top_value / len(shards)))
        loudness = loudness * jnp.repeat(draws, dims[dim] // parts).reshape([-1 if axis == dim else 1 for axis in range(len(dims))])
    return loudness


def scatter_about(key, extent, deviation, most, cuts=(), kind=jnp.bfloat16):
    drawn = deviation * jax.random.normal(key, extent, jnp.float32)
    if cuts:
        drawn = drawn * shard_levels(key, extent, cuts, -0.22, 0.18)
    return jnp.clip(drawn, -most, most).astype(kind)


def setup_inputs(seed: int = 0) -> dict:
    key_list = jax.random.split(jax.random.key(seed), 7)
    saved_input = scatter_about(key_list[0], (LAYERS, MB, POINTS, C), 1.0, 6.0, ((0, 4), (2, 8)))
    cotangent = scatter_about(key_list[1], (MB, POINTS, C), 1.0, 6.0, ((1, 8),))
    quad_values = scatter_about(key_list[2], (KB, NBLK, NNZ, BLK, BLK), (NNZ * BLK) ** -0.5, 0.3125, ((1, 8),))
    block_index = draw_block_index(jax.random.fold_in(key_list[6], 71), 0)
    block_mask = draw_block_mask(jax.random.fold_in(key_list[6], 71), 0)
    weights = scatter_about(key_list[5], (LAYERS, KB, C, C), (KB * C) ** -0.5, 0.21875, ((0, 4),))
    return {"saved_input": saved_input, "cotangent": cotangent, "quad_values": quad_values, "block_index": block_index, "block_mask": block_mask, "weights": weights}


def gelu_slope(value):
    return 0.5 * (1.0 + jax.scipy.special.erf(value * 0.7071067811865476)) + value * jnp.exp(-0.5 * value * value) * 0.3989422804014327


def layer_backward(acts, grads, qmat, block_index, weights):
    chosen = acts[block_index]
    hidden = jnp.einsum("kbjpq,bjqc->bpkc", qmat.astype(jnp.float32), chosen.astype(jnp.float32)).astype(jnp.bfloat16)
    flat = hidden.reshape(NBLK * BLK, KB * C)
    w_cat = weights.reshape(KB * C, C)
    mixed = jnp.dot(flat, w_cat, preferred_element_type=jnp.float32)
    slope = (grads.reshape(NBLK * BLK, C).astype(jnp.float32) * gelu_slope(mixed)).astype(jnp.bfloat16)
    w_grad = lax.dot_general(flat, slope, (((0,), (0,)), ((), ())), preferred_element_type=jnp.float32)
    back = jnp.dot(slope, w_cat.T, preferred_element_type=jnp.float32).astype(jnp.bfloat16).reshape(NBLK, BLK, KB, C)
    terms = jnp.einsum("kbjpq,bpkc->bjqc", qmat.astype(jnp.float32), back.astype(jnp.float32))
    summed = jax.ops.segment_sum(terms.reshape(NBLK * NNZ, BLK, C), block_index.reshape(NBLK * NNZ), num_segments=NBLK)
    new_grads = (grads.astype(jnp.float32) + summed).astype(jnp.bfloat16)
    return new_grads, w_grad


def reference(saved_input, cotangent, quad_values, block_index, block_mask, weights):
    qmat = quad_values * block_mask.astype(jnp.bfloat16)[None, :, :, None, None]
    current = cotangent.reshape(MB, NBLK, BLK, C)
    grad_list = []
    weight_list = []
    for layer in reversed(range(LAYERS)):
        acts = saved_input[layer].reshape(MB, NBLK, BLK, C)
        total_w = jnp.zeros((KB * C, C), jnp.float32)
        produced = []
        for micro in range(MB):
            new_grads, w_grad = layer_backward(acts[micro], current[micro], qmat, block_index, weights[layer])
            produced.append(new_grads)
            total_w = total_w + w_grad
        current = jnp.stack(produced)
        grad_list.insert(0, current.reshape(MB, POINTS, C))
        weight_list.insert(0, total_w.reshape(KB, C, C))
    return jnp.stack(grad_list), jnp.stack(weight_list)
```

```python
import functools

import jax
import jax.numpy as jnp
from jax import lax
from jax.experimental import pallas as pl
from jax.experimental.pallas import tpu as pltpu
from jax.sharding import PartitionSpec as P

KB = 3
BLK = 64
HALO = 2
MB = 2
GRP = 4
SPAN = GRP + 2 * HALO
BF = jnp.bfloat16
F32 = jnp.float32
VM = pl.BlockSpec(memory_space=pltpu.VMEM)
ANY = pl.BlockSpec(memory_space=pl.ANY)
SM = pl.BlockSpec(memory_space=pltpu.SMEM)


def gelu_slope(value):
    return (
        0.5 * (1.0 + lax.erf(value * 0.7071067811865476))
        + value * jnp.exp(-0.5 * value * value) * 0.3989422804014327
    )


def params(mib=24):
    return pltpu.CompilerParams(vmem_limit_bytes=mib << 20)


def dot(a, b):
    return jnp.dot(a, b, preferred_element_type=F32)


def band_kernel(blocks, index_ref, mask_ref, quad_ref, band_ref, flip_ref, table_ref):
    first = lax.axis_index("lat") * blocks
    for b in range(blocks):
        for d in range(2 * HALO + 2):
            table_ref[b, d] = 0
        for j in range(index_ref.shape[1]):
            d = index_ref[b, j] - (first + b) + HALO
            table_ref[b, jnp.where(mask_ref[b, j] != 0, d, 2 * HALO + 1)] = j + 1
    empty = jnp.zeros((BLK, BLK), BF)
    for g in range(blocks // GRP):
        for r in range(GRP):
            b = g * GRP + r
            for k in range(KB):
                tiles = [empty] * r
                for d in range(2 * HALO + 1):
                    entry = table_ref[b, d]
                    tile = quad_ref[k, b, jnp.maximum(entry - 1, 0)]
                    tiles.append(jnp.where(entry > 0, tile, empty))
                tiles += [empty] * (GRP - 1 - r)
                row = k * GRP * BLK + r * BLK
                band_ref[g, row : row + BLK, :] = jnp.concatenate(tiles, axis=1)
        flip_ref[g] = band_ref[g].T


def band_call(block_index, block_mask, quad):
    blocks = quad.shape[1]
    groups = blocks // GRP
    return pl.pallas_call(
        functools.partial(band_kernel, blocks),
        out_shape=(
            pltpu.VMEM((groups, KB * GRP * BLK, SPAN * BLK), BF),
            pltpu.VMEM((groups, SPAN * BLK, KB * GRP * BLK), BF),
        ),
        in_specs=[SM, SM, VM],
        out_specs=(VM, VM),
        scratch_shapes=[pltpu.SMEM((blocks, 2 * HALO + 2), jnp.int32)],
        compiler_params=params(),
        name="band",
    )(block_index, block_mask, quad)


def hidden_kernel(x_ref, below_ref, above_ref, band_ref, w_ref, hid_ref, gp_ref, ext_ref, sems):
    rows = x_ref.shape[2]
    edge = HALO * BLK
    copies = [
        pltpu.make_async_copy(below_ref, ext_ref.at[:, pl.ds(0, edge)], sems.at[0]),
        pltpu.make_async_copy(x_ref.at[0], ext_ref.at[:, pl.ds(edge, rows)], sems.at[1]),
        pltpu.make_async_copy(above_ref, ext_ref.at[:, pl.ds(edge + rows, edge)], sems.at[2]),
    ]
    for c in copies:
        c.start()
    for c in copies:
        c.wait()
    size = GRP * BLK
    for m in range(MB):
        for g in range(rows // size):
            window = ext_ref[m, g * size : g * size + SPAN * BLK, :]
            hid = dot(band_ref[g], window).astype(BF)
            hid_ref[m, g] = hid
            z = dot(hid[:size], w_ref[0, 0])
            for k in range(1, KB):
                z += dot(hid[k * size : (k + 1) * size], w_ref[0, k])
            gp_ref[m, g * size : (g + 1) * size, :] = gelu_slope(z)


def hidden_call(x, below, above, band, weights):
    _, mb, rows, ch = x.shape
    groups = band.shape[0]
    return pl.pallas_call(
        hidden_kernel,
        out_shape=(
            pltpu.VMEM((mb, groups, KB * GRP * BLK, ch), BF),
            pltpu.VMEM((mb, rows, ch), F32),
        ),
        in_specs=[ANY, ANY, ANY, VM, VM],
        out_specs=(VM, VM),
        scratch_shapes=[
            pltpu.VMEM((mb, rows + 2 * HALO * BLK, ch), BF),
            pltpu.SemaphoreType.DMA((3,)),
        ],
        compiler_params=params(),
        name="hidden",
    )(x, below, above, band, weights)


def step_kernel(turn, first, main_ref, below_ref, above_ref, gp_ref, flip_ref, w_ref, *rest):
    olds, rest = ((), rest) if first else (rest[:4], rest[4:])
    out_ref, left_ref, right_ref, slope_ref, stack_ref, term_ref = rest
    rows = gp_ref.shape[1]
    size = GRP * BLK
    edge = HALO * BLK
    groups = rows // size

    @pl.when(lax.axis_index("section") == turn)
    def _():
        for m in range(MB):
            for g in range(groups):
                at = pl.ds(g * size, size)
                grad = main_ref[m, at, :].astype(F32)
                if not first:
                    parts = [grad[i * edge : (i + 1) * edge] for i in range(size // edge)]
                    if g == 0:
                        parts[0] += below_ref[m].astype(F32)
                    if g == groups - 1:
                        parts[-1] += above_ref[m].astype(F32)
                    grad = jnp.concatenate(parts, axis=0).astype(BF).astype(F32)
                slope = (grad * gp_ref[m, at, :]).astype(BF)
                slope_ref[m, at, :] = slope
                for k in range(KB):
                    back = lax.dot_general(
                        slope, w_ref[0, k], (((1,), (1,)), ((), ())), preferred_element_type=F32
                    )
                    stack_ref[k * size : (k + 1) * size, :] = back.astype(BF)
                term = dot(flip_ref[g], stack_ref[...])
                lap = 2 * edge
                low = g * size
                if g == 0:
                    left_ref[m] = term[:edge].astype(BF)
                    term_ref[low + edge : low + lap, :] = term[edge:lap] + grad[: lap - edge]
                else:
                    term_ref[low : low + lap, :] += term[:lap]
                    term_ref[low + edge : low + lap, :] += grad[: lap - edge]
                term_ref[low + lap : low + size + edge, :] = (
                    term[lap : size + edge] + grad[lap - edge :]
                )
                if g == groups - 1:
                    right_ref[m] = term[size + edge :].astype(BF)
                else:
                    term_ref[low + size + edge : low + size + lap, :] = term[size + edge :]
            out_ref[m] = term_ref[edge : edge + rows, :].astype(BF)


def step_call(turn, main, below, above, gp, flip, weights, olds):
    mb, rows, ch = gp.shape
    edge = HALO * BLK
    first = olds is None
    shapes = ((mb, rows, ch), (mb, edge, ch), (mb, edge, ch), (mb, rows, ch))
    args = (main, below, above, gp, flip, weights) + (() if first else tuple(olds))
    aliases = {} if first else {6 + i: i for i in range(4)}
    return pl.pallas_call(
        functools.partial(step_kernel, turn, first),
        out_shape=tuple(pltpu.VMEM(s, BF) for s in shapes),
        in_specs=[VM] * len(args),
        out_specs=(VM,) * 4,
        input_output_aliases=aliases,
        scratch_shapes=[
            pltpu.VMEM((KB * GRP * BLK, ch), BF),
            pltpu.VMEM((rows + 2 * edge, ch), F32),
        ],
        compiler_params=params(),
        name=f"step{turn}",
    )(*args)


def weight_kernel(n, hid_ref, slope_ref, *out_refs):
    piece = out_refs[0].shape[0]
    acc_ref = out_refs[-1]
    me = lax.axis_index("lat")
    size = GRP * BLK
    groups = hid_ref.shape[1]
    for k in range(KB):
        total = None
        for m in range(MB):
            for g in range(groups):
                part = lax.dot_general(
                    hid_ref[m, g, k * size : (k + 1) * size, :],
                    slope_ref[m, g * size : (g + 1) * size, :],
                    (((0,), (0,)), ((), ())),
                    preferred_element_type=F32,
                )
                total = part if total is None else total + part
        acc_ref[k * total.shape[0] : (k + 1) * total.shape[0], :] = total
    if n == 1:
        out_refs[0][...] = acc_ref[...]
        return
    out_refs[0][...] = acc_ref[pl.ds(pl.multiple_of(me * piece, piece), piece), :]
    for s in range(1, n):
        other = me ^ s
        out_refs[s][...] = acc_ref[pl.ds(pl.multiple_of(other * piece, piece), piece), :].astype(BF)


def weight_call(n, hid, slope):
    ch = slope.shape[2]
    piece = KB * ch // n
    return pl.pallas_call(
        functools.partial(weight_kernel, n),
        out_shape=(pltpu.VMEM((piece, ch), F32),) + (pltpu.VMEM((piece, ch), BF),) * (n - 1),
        in_specs=[VM] * 2,
        out_specs=(VM,) * n,
        scratch_shapes=[pltpu.VMEM((KB * ch, ch), F32)],
        compiler_params=params(),
        name="weight",
    )(hid, slope)


def sum_kernel(own_ref, *refs):
    total = own_ref[...]
    for ref in refs[:-1]:
        total += ref[...].astype(F32)
    refs[-1][...] = total.astype(BF)


def sum_call(own, others):
    return pl.pallas_call(
        sum_kernel,
        out_shape=pltpu.VMEM(own.shape, BF),
        in_specs=[VM] * (1 + len(others)),
        out_specs=VM,
        compiler_params=params(),
        name="sum",
    )(own, *others)


def close_kernel(n, main_ref, below_ref, above_ref, *refs):
    pieces, grad_ref, weight_ref = refs[:n], refs[n], refs[n + 1 :]
    rows = main_ref.shape[1]
    edge = HALO * BLK
    me = lax.axis_index("lat")
    for s in range(n):
        other, piece = me ^ s, pieces[s].shape[0]
        weight_ref[0][pl.ds(pl.multiple_of(other * piece, piece), piece), :] = pieces[s][...].astype(F32)
    for m in range(MB):
        low = main_ref[m, :edge, :].astype(F32) + below_ref[m].astype(F32)
        grad_ref[0, m, :edge, :] = low.astype(BF)
        grad_ref[0, m, edge : rows - edge, :] = main_ref[m, edge : rows - edge, :]
        high = main_ref[m, rows - edge :, :].astype(F32) + above_ref[m].astype(F32)
        grad_ref[0, m, rows - edge :, :] = high.astype(BF)


def close_call(main, below, above, pieces):
    mb, rows, ch = main.shape
    shapes = (jax.ShapeDtypeStruct((1, mb, rows, ch), BF),)
    if pieces:
        shapes += (jax.ShapeDtypeStruct((KB * ch, ch), F32),)
    return pl.pallas_call(
        functools.partial(close_kernel, len(pieces)),
        out_shape=shapes,
        in_specs=[VM] * (3 + len(pieces)),
        out_specs=(VM,) * len(shapes),
        compiler_params=params(),
        name="close",
    )(main, below, above, *pieces)


def per_device(saved_input, cotangent, quad_values, block_index, block_mask, weights):
    sections = lax.axis_size("section")
    lats = lax.axis_size("lat")
    edge = HALO * BLK
    rows = saved_input.shape[2]
    both = ("lat", "section")
    up = [(i, i + 1) for i in range(lats - 1)]
    down = [(i + 1, i) for i in range(lats - 1)]

    below = lax.ppermute(saved_input[0, :, rows - edge :], "lat", up)
    above = lax.ppermute(saved_input[0, :, :edge], "lat", down)
    band, flip = band_call(block_index, block_mask, quad_values)
    hid, gp = hidden_call(saved_input, below, above, band, weights)

    state, main = None, cotangent
    low = high = jnp.zeros((MB, edge, cotangent.shape[2]), BF)
    for turn in reversed(range(sections)):
        state = step_call(turn, main, low, high, gp, flip, weights, state)
        out, left, right, slope = state
        if turn > 0:
            main = lax.ppermute(out, "section", [(turn, turn - 1)])
            low = lax.ppermute(
                right, both, [(a * sections + turn, b * sections + turn - 1) for a, b in up]
            )
            high = lax.ppermute(
                left, both, [(a * sections + turn, b * sections + turn - 1) for a, b in down]
            )

    if lats & (lats - 1) == 0 and lats <= 8:
        partial_sums = weight_call(lats, hid, slope)
        met = [
            lax.ppermute(partial_sums[s], "lat", [(i, i ^ s) for i in range(lats)])
            for s in range(1, lats)
        ]
        low = lax.ppermute(right, "lat", up)
        high = lax.ppermute(left, "lat", down)
        mine = sum_call(partial_sums[0], met)
        pieces = [mine] + [
            lax.ppermute(mine, "lat", [(i, i ^ s) for i in range(lats)]) for s in range(1, lats)
        ]
    else:
        low = lax.ppermute(right, "lat", up)
        high = lax.ppermute(left, "lat", down)
        pieces = []
        w_sum = [lax.psum(weight_call(1, hid, slope)[0], "lat")]
    grad, *weight = close_call(out, low, high, pieces)
    weight = (weight or w_sum)[0]
    channels = saved_input.shape[3]
    return grad, weight.reshape(1, KB, channels, channels)


def solution(mesh):
    in_specs = (
        P("section", None, "lat", None),
        P(None, "lat", None),
        P(None, "lat", None, None, None),
        P("lat", None),
        P("lat", None),
        P("section", None, None, None),
    )
    out_specs = (P("section", None, "lat", None), P("section", None, None, None))
    return jax.shard_map(
        per_device, mesh=mesh, in_specs=in_specs, out_specs=out_specs, check_vma=False
    )
```

```python
import functools

import jax
import jax.numpy as jnp
from jax import lax
from jax.experimental import pallas as pl
from jax.experimental.pallas import tpu as pltpu
from jax.sharding import PartitionSpec as P

KB = 3
BLK = 64
HALO = 2
MB = 2
GRP = 4
SPAN = GRP + 2 * HALO
BF = jnp.bfloat16
F32 = jnp.float32
VM = pl.BlockSpec(memory_space=pltpu.VMEM)
ANY = pl.BlockSpec(memory_space=pl.ANY)
HB = pl.BlockSpec(memory_space=pltpu.HBM)


def gelu_slope(value):
    return (
        0.5 * (1.0 + lax.erf(value * 0.7071067811865476))
        + value * jnp.exp(-0.5 * value * value) * 0.3989422804014327
    )


def params(mib=24):
    return pltpu.CompilerParams(vmem_limit_bytes=mib << 20)


def matchings(n):
    near = [tuple(i ^ 1 for i in range(n)), tuple((i + 1 if i % 2 else i - 1) % n for i in range(n))]
    used = {(i, m[i]) for m in near for i in range(n)}

    def extend(found, now):
        if None not in now:
            found, now = found + [tuple(now)], [None] * n
        if len(found) == n - 3:
            return found
        i = now.index(None)
        for j in range(n - 1, i, -1):
            taken = any(m[i] == j for m in found)
            if now[j] is None and (i, j) not in used and not taken:
                after = list(now)
                after[i], after[j] = j, i
                result = extend(found, after)
                if result:
                    return result
        return None

    return near + extend([], [None] * n)


def partner_of(match, me):
    return sum((jnp.where(me == i, j, 0) for i, j in enumerate(match)), 0)


def near_pairs(lats, sections, side):
    pairs = []
    for i in range(lats):
        j = i ^ 1 if side == 0 else (i + 1 if i % 2 else i - 1)
        for s in range(sections):
            other = j * sections + s if 0 <= j < lats else i * sections + (s ^ 1)
            pairs.append((i * sections + s, other))
    return pairs


def hop_pairs(sections, turn):
    if turn % 2:
        return [(s, s ^ 1) for s in range(sections)]
    return [(s, (s - 1) % sections) for s in range(sections)]


def slant_pairs(lats, sections, turn, upward):
    last, low = lats - 1, turn - 1
    ways = {(i, turn): (i + 1, low) for i in range(last)}
    ways[last, turn] = (last - 1, turn)
    ways[last, low] = (last, turn)
    ways.update({(i, low): (i - 1, turn) for i in range(2, last)})
    ways[1, low] = (0, low)
    ways[0, low] = (0, turn)
    if not upward:
        ways = {(last - i, s): (last - j, r) for (i, s), (j, r) in ways.items()}
    for i in range(lats):
        for s in range(sections):
            ways.setdefault((i, s), (i, s ^ 1) if turn % 2 else (i ^ 1, s))
    pairs = [(i * sections + s, j * sections + r) for (i, s), (j, r) in ways.items()]
    assert len({b for _, b in pairs}) == lats * sections
    return pairs


def dot(a, b):
    return jnp.dot(a, b, preferred_element_type=F32)


def band_kernel(
    blocks, index_in, mask_in, quad_in, band_ref, flip_ref, index_ref, mask_ref, quad_ref, table_ref, sems
):
    first = lax.axis_index("lat") * blocks
    small = [
        pltpu.make_async_copy(index_in, index_ref, sems.at[KB]),
        pltpu.make_async_copy(mask_in, mask_ref, sems.at[KB + 1]),
    ]
    large = [pltpu.make_async_copy(quad_in.at[k], quad_ref.at[k], sems.at[k]) for k in range(KB)]
    for c in small + large:
        c.start()
    for c in small:
        c.wait()
    for b in range(blocks):
        for d in range(2 * HALO + 2):
            table_ref[b, d] = 0
        for j in range(index_ref.shape[1]):
            d = index_ref[b, j] - (first + b) + HALO
            table_ref[b, jnp.where(mask_ref[b, j] != 0, d, 2 * HALO + 1)] = j + 1
    empty = jnp.zeros((BLK, BLK), BF)
    for k in range(KB):
        large[k].wait()
        for b in range(blocks):
            g, r = b // GRP, b % GRP
            tiles = [empty] * r
            for d in range(2 * HALO + 1):
                entry = table_ref[b, d]
                tile = quad_ref[k, b, jnp.maximum(entry - 1, 0)]
                tiles.append(jnp.where(entry > 0, tile, empty))
            tiles += [empty] * (GRP - 1 - r)
            row = k * GRP * BLK + r * BLK
            band_ref[g, row : row + BLK, :] = jnp.concatenate(tiles, axis=1)
            if r == GRP - 1:
                part = slice(k * GRP * BLK, (k + 1) * GRP * BLK)
                flip_ref[g, :, part] = band_ref[g, part, :].T


def band_call(block_index, block_mask, quad):
    blocks = quad.shape[1]
    groups = blocks // GRP
    return pl.pallas_call(
        functools.partial(band_kernel, blocks),
        out_shape=(
            pltpu.VMEM((groups, KB * GRP * BLK, SPAN * BLK), BF),
            pltpu.VMEM((groups, SPAN * BLK, KB * GRP * BLK), BF),
        ),
        in_specs=[HB] * 3,
        out_specs=(VM, VM),
        scratch_shapes=[
            pltpu.SMEM(block_index.shape, jnp.int32),
            pltpu.SMEM(block_mask.shape, jnp.int32),
            pltpu.VMEM(quad.shape, BF),
            pltpu.SMEM((blocks, 2 * HALO + 2), jnp.int32),
            pltpu.SemaphoreType.DMA((KB + 2,)),
        ],
        compiler_params=params(),
        name="band",
    )(block_index, block_mask, quad)


def hidden_kernel(x_ref, near_ref, far_ref, band_ref, w_ref, hid_ref, gp_ref, ext_ref, sems):
    rows = x_ref.shape[2]
    edge = HALO * BLK
    odd = lax.axis_index("lat") % 2
    ends = [pl.multiple_of(side * (edge + rows), edge) for side in (1 - odd, odd)]
    copies = [
        pltpu.make_async_copy(near_ref, ext_ref.at[:, pl.ds(ends[0], edge)], sems.at[0]),
        pltpu.make_async_copy(x_ref.at[0], ext_ref.at[:, pl.ds(edge, rows)], sems.at[1]),
        pltpu.make_async_copy(far_ref, ext_ref.at[:, pl.ds(ends[1], edge)], sems.at[2]),
    ]
    for c in copies:
        c.start()
    for c in copies:
        c.wait()
    size = GRP * BLK
    for m in range(MB):
        for g in range(rows // size):
            window = ext_ref[m, g * size : g * size + SPAN * BLK, :]
            hid = dot(band_ref[g], window).astype(BF)
            hid_ref[m, g] = hid
            z = dot(hid[:size], w_ref[0, 0])
            for k in range(1, KB):
                z += dot(hid[k * size : (k + 1) * size], w_ref[0, k])
            gp_ref[m, g * size : (g + 1) * size, :] = gelu_slope(z)


def hidden_call(x, near, far, band, weights):
    _, mb, rows, ch = x.shape
    groups = band.shape[0]
    return pl.pallas_call(
        hidden_kernel,
        out_shape=(
            pltpu.VMEM((mb, groups, KB * GRP * BLK, ch), BF),
            pltpu.VMEM((mb, rows, ch), F32),
        ),
        in_specs=[ANY, ANY, ANY, VM, VM],
        out_specs=(VM, VM),
        scratch_shapes=[
            pltpu.VMEM((mb, rows + 2 * HALO * BLK, ch), BF),
            pltpu.SemaphoreType.DMA((3,)),
        ],
        compiler_params=params(),
        name="hidden",
    )(x, near, far, band, weights)


def step_kernel(turn, lats, *refs):
    first = lats is None
    (main_ref, gp_ref, flip_ref, w_ref), rest = refs[:4], refs[4:]
    if not first:
        (below_ref, above_ref), rest = rest[:2], rest[6:]
    lat = lax.axis_index("lat")
    out_ref, left_ref, right_ref, slope_ref, stack_ref, term_ref = rest
    rows = gp_ref.shape[1]
    size = GRP * BLK
    edge = HALO * BLK
    groups = rows // size

    @pl.when(lax.axis_index("section") == turn)
    def _():
        for m in range(MB):
            for g in range(groups):
                at = pl.ds(g * size, size)
                grad = main_ref[m, at, :].astype(F32)
                if not first:
                    parts = [grad[i * edge : (i + 1) * edge] for i in range(size // edge)]
                    if g == 0:
                        parts[0] += jnp.where(lat > 0, below_ref[m].astype(F32), 0.0)
                    if g == groups - 1:
                        parts[-1] += jnp.where(lat < lats - 1, above_ref[m].astype(F32), 0.0)
                    grad = jnp.concatenate(parts, axis=0).astype(BF).astype(F32)
                slope = (grad * gp_ref[m, at, :]).astype(BF)
                slope_ref[m, at, :] = slope
                for k in range(KB):
                    back = lax.dot_general(
                        slope, w_ref[0, k], (((1,), (1,)), ((), ())), preferred_element_type=F32
                    )
                    stack_ref[k * size : (k + 1) * size, :] = back.astype(BF)
                term = dot(flip_ref[g], stack_ref[...])
                lap = 2 * edge
                low = g * size
                if g == 0:
                    left_ref[m] = term[:edge].astype(BF)
                    term_ref[low + edge : low + lap, :] = term[edge:lap] + grad[: lap - edge]
                else:
                    term_ref[low : low + lap, :] += term[:lap]
                    term_ref[low + edge : low + lap, :] += grad[: lap - edge]
                term_ref[low + lap : low + size + edge, :] = (
                    term[lap : size + edge] + grad[lap - edge :]
                )
                if g == groups - 1:
                    right_ref[m] = term[size + edge :].astype(BF)
                else:
                    term_ref[low + size + edge : low + size + lap, :] = term[size + edge :]
            out_ref[m] = term_ref[edge : edge + rows, :].astype(BF)


def step_call(turn, lats, main, sides, gp, flip, weights, olds):
    mb, rows, ch = gp.shape
    edge = HALO * BLK
    shapes = ((mb, rows, ch), (mb, edge, ch), (mb, edge, ch), (mb, rows, ch))
    args = (main, gp, flip, weights) + sides + olds
    aliases = {6 + i: i for i in range(len(olds))}
    return pl.pallas_call(
        functools.partial(step_kernel, turn, lats if olds else None),
        out_shape=tuple(pltpu.VMEM(s, BF) for s in shapes),
        in_specs=[VM] * len(args),
        out_specs=(VM,) * 4,
        input_output_aliases=aliases,
        scratch_shapes=[
            pltpu.VMEM((KB * GRP * BLK, ch), BF),
            pltpu.VMEM((rows + 2 * edge, ch), F32),
        ],
        compiler_params=params(),
        name=f"step{turn}",
    )(*args)


def weight_kernel(ways, hid_ref, slope_ref, left_ref, right_ref, *refs):
    out_refs, acc_ref = refs[:-1], refs[-1]
    n = len(ways) + 1
    me = lax.axis_index("lat")
    size = GRP * BLK
    groups = hid_ref.shape[1]
    for k in range(KB):
        total = None
        for m in range(MB):
            for g in range(groups):
                part = lax.dot_general(
                    hid_ref[m, g, k * size : (k + 1) * size, :],
                    slope_ref[m, g * size : (g + 1) * size, :],
                    (((0,), (0,)), ((), ())),
                    preferred_element_type=F32,
                )
                total = part if total is None else total + part
        acc_ref[k * total.shape[0] : (k + 1) * total.shape[0], :] = total
    piece = acc_ref.shape[0] // n

    def cut(i):
        return acc_ref[pl.ds(pl.multiple_of(i * piece, piece), piece), :]

    if n == 1:
        out_refs[0][...] = acc_ref[...]
        return
    out_refs[0][...] = cut(me)
    odd = me % 2 == 1
    edge = left_ref.shape[1]
    for s, way in enumerate(ways):
        out_refs[s + 1][:piece, :] = cut(partner_of(way, me)).astype(BF)
        if s < 2:
            for m in range(MB):
                rows = slice(piece + m * edge, piece + (m + 1) * edge)
                low, high = (right_ref, left_ref) if s == 0 else (left_ref, right_ref)
                out_refs[s + 1][rows, :] = jnp.where(odd, high[m], low[m])


def weight_call(ways, hid, slope, left, right):
    ch = slope.shape[2]
    piece = KB * ch // (len(ways) + 1)
    extra = MB * left.shape[1]
    return pl.pallas_call(
        functools.partial(weight_kernel, ways),
        out_shape=(pltpu.VMEM((piece, ch), F32),)
        + tuple(pltpu.VMEM((piece + (extra if s < 2 else 0), ch), BF) for s in range(len(ways))),
        in_specs=[VM] * 4,
        out_specs=(VM,) * (len(ways) + 1),
        scratch_shapes=[pltpu.VMEM((KB * ch, ch), F32)],
        compiler_params=params(),
        name="weight",
    )(hid, slope, left, right)


def sum_kernel(own_ref, *refs):
    piece = own_ref.shape[0]
    total = own_ref[...]
    for ref in refs[:-1]:
        total += ref[:piece, :].astype(F32)
    refs[-1][...] = total.astype(BF)


def sum_call(own, others):
    return pl.pallas_call(
        sum_kernel,
        out_shape=pltpu.VMEM(own.shape, BF),
        in_specs=[VM] * (1 + len(others)),
        out_specs=VM,
        compiler_params=params(),
        name="sum",
    )(own, *others)


def grad_kernel(lats, skip, main_ref, near_ref, far_ref, grad_ref):
    rows = main_ref.shape[1]
    edge = HALO * BLK
    me = lax.axis_index("lat")
    odd = me % 2 == 1
    for m in range(MB):
        at = slice(skip + m * edge, skip + (m + 1) * edge)
        near, far = near_ref[at, :].astype(F32), far_ref[at, :].astype(F32)
        below = jnp.where(me > 0, jnp.where(odd, near, far), 0.0)
        above = jnp.where(me < lats - 1, jnp.where(odd, far, near), 0.0)
        grad_ref[0, m, :edge, :] = (main_ref[m, :edge, :].astype(F32) + below).astype(BF)
        grad_ref[0, m, edge : rows - edge, :] = main_ref[m, edge : rows - edge, :]
        grad_ref[0, m, rows - edge :, :] = (main_ref[m, rows - edge :, :].astype(F32) + above).astype(BF)


def grad_call(lats, skip, main, near, far):
    return pl.pallas_call(
        functools.partial(grad_kernel, lats, skip),
        out_shape=jax.ShapeDtypeStruct((1,) + main.shape, BF),
        in_specs=[VM] * 3,
        out_specs=VM,
        compiler_params=params(),
        name="grad",
    )(main, near, far)


def join_kernel(ways, *refs):
    pieces, weight_ref = refs[:-1], refs[-1]
    me = lax.axis_index("lat")
    piece = pieces[0].shape[0]
    for ref, other in zip(pieces, [me] + [partner_of(way, me) for way in ways]):
        weight_ref[pl.ds(pl.multiple_of(other * piece, piece), piece), :] = ref[...].astype(F32)


def join_call(ways, pieces):
    piece, ch = pieces[0].shape
    return pl.pallas_call(
        functools.partial(join_kernel, ways),
        out_shape=jax.ShapeDtypeStruct((piece * len(pieces), ch), F32),
        in_specs=[VM] * len(pieces),
        out_specs=VM,
        compiler_params=params(),
        name="join",
    )(*pieces)


def per_device(saved_input, cotangent, quad_values, block_index, block_mask, weights):
    sections = lax.axis_size("section")
    lats = lax.axis_size("lat")
    edge = HALO * BLK
    rows = saved_input.shape[2]
    both = ("lat", "section")
    odd = lax.axis_index("lat") % 2
    sides = [near_pairs(lats, sections, side) for side in range(2)]

    def rim(high):
        return lax.dynamic_slice_in_dim(saved_input[0], high * (rows - edge), edge, axis=1)

    far = lax.ppermute(rim(odd), both, sides[1])
    near = lax.ppermute(rim(1 - odd), both, sides[0])
    band, flip = band_call(block_index, block_mask, quad_values)
    hid, gp = hidden_call(saved_input, near, far, band, weights)

    state, main, terms = (), cotangent, ()
    for turn in reversed(range(sections)):
        state = step_call(turn, lats, main, terms, gp, flip, weights, state)
        out, left, right, slope = state
        if turn > 0:
            low = lax.ppermute(right, both, slant_pairs(lats, sections, turn, True))
            high = lax.ppermute(left, both, slant_pairs(lats, sections, turn, False))
            main = lax.ppermute(out, "section", hop_pairs(sections, turn))
            terms = (low, high)

    channels = saved_input.shape[3]
    if lats == 8:
        ways = matchings(lats)
        own, *cuts = weight_call(ways, hid, slope, left, right)
        met = [lax.ppermute(cut, "lat", list(enumerate(way))) for cut, way in zip(cuts, ways)]
        mine = sum_call(own, met)
        grad = grad_call(lats, own.shape[0], out, met[0], met[1])
        pieces = [mine] + [lax.ppermute(mine, "lat", list(enumerate(way))) for way in ways]
        weight = join_call(ways, pieces)
    else:
        give = jnp.where(odd == 1, left, right), jnp.where(odd == 1, right, left)
        near, far = (lax.ppermute(g, both, p).reshape(-1, channels) for g, p in zip(give, sides))
        grad = grad_call(lats, 0, out, near, far)
        weight = lax.psum(weight_call([], hid, slope, left, right)[0], "lat")
    return grad, weight.reshape(1, KB, channels, channels)


def solution(mesh):
    in_specs = (
        P("section", None, "lat", None),
        P(None, "lat", None),
        P(None, "lat", None, None, None),
        P("lat", None),
        P("lat", None),
        P("section", None, None, None),
    )
    out_specs = (P("section", None, "lat", None), P("section", None, None, None))
    return jax.shard_map(
        per_device, mesh=mesh, in_specs=in_specs, out_specs=out_specs, check_vma=False
    )
```

```python
import functools

import jax
import jax.numpy as jnp
from jax import lax
from jax.experimental import pallas as pl
from jax.experimental.pallas import tpu as pltpu
from jax.sharding import PartitionSpec as P


KB = 3
BLK = 64
HALO = 2
MB = 2
GRP = 4
SPAN = GRP + 2 * HALO
BF = jnp.bfloat16
F32 = jnp.float32
VM = pl.BlockSpec(memory_space=pltpu.VMEM)
ANY = pl.BlockSpec(memory_space=pl.ANY)
HB = pl.BlockSpec(memory_space=pltpu.HBM)


def gelu_slope(value):
    return (
        0.5 * (1.0 + lax.erf(value * 0.7071067811865476))
        + value * jnp.exp(-0.5 * value * value) * 0.3989422804014327
    )


def params(mib=24):
    return pltpu.CompilerParams(vmem_limit_bytes=mib << 20)


def matchings(n):
    near = [tuple(i ^ 1 for i in range(n)), tuple((i + 1 if i % 2 else i - 1) % n for i in range(n))]
    used = {(i, m[i]) for m in near for i in range(n)}

    def extend(found, now):
        if None not in now:
            found, now = found + [tuple(now)], [None] * n
        if len(found) == n - 3:
            return found
        i = now.index(None)
        for j in range(n - 1, i, -1):
            taken = any(m[i] == j for m in found)
            if now[j] is None and (i, j) not in used and not taken:
                after = list(now)
                after[i], after[j] = j, i
                result = extend(found, after)
                if result:
                    return result
        return None

    return near + extend([], [None] * n)


def partner_of(match, me):
    return sum((jnp.where(me == i, j, 0) for i, j in enumerate(match)), 0)


def near_pairs(lats, sections, side):
    pairs = []
    for i in range(lats):
        j = i ^ 1 if side == 0 else (i + 1 if i % 2 else i - 1)
        for s in range(sections):
            other = j * sections + s if 0 <= j < lats else i * sections + (s ^ 1)
            pairs.append((i * sections + s, other))
    return pairs


def hop_pairs(sections, turn):
    if turn % 2:
        return [(s, s ^ 1) for s in range(sections)]
    return [(s, (s - 1) % sections) for s in range(sections)]


def slant_pairs(lats, sections, turn, upward):
    last, low = lats - 1, turn - 1
    ways = {(i, turn): (i + 1, low) for i in range(last)}
    if turn % 2 and sections > 2:
        aside = (turn - 2) % sections
        ways[last, turn] = (last, aside)
        ways.update({(i, aside): (i - 1, aside) for i in range(1, lats)})
        ways[0, aside] = (0, low)
        ways.update({(i, low): (i, turn) for i in range(lats)})
        for i in range(lats):
            for s in range(sections):
                ways.setdefault((i, s), (i ^ 1, s))
        assert len(set(ways.values())) == lats * sections
    if not upward:
        ways = {(last - i, s): (last - j, r) for (i, s), (j, r) in ways.items()}
    return [(i * sections + s, j * sections + r) for (i, s), (j, r) in ways.items()]


def cost(flops):
    return pl.CostEstimate(flops=flops, bytes_accessed=flops // 256, transcendentals=0)


def dot(a, b):
    return jnp.dot(a, b, preferred_element_type=F32)


def band_kernel(
    blocks, index_in, mask_in, quad_in, band_ref, flip_ref, index_ref, mask_ref, quad_ref, table_ref, sems
):
    first = lax.axis_index("lat") * blocks
    small = [
        pltpu.make_async_copy(index_in, index_ref, sems.at[KB]),
        pltpu.make_async_copy(mask_in, mask_ref, sems.at[KB + 1]),
    ]
    large = [pltpu.make_async_copy(quad_in.at[k], quad_ref.at[k], sems.at[k]) for k in range(KB)]
    for c in small + large:
        c.start()
    for c in small:
        c.wait()
    for b in range(blocks):
        for d in range(2 * HALO + 2):
            table_ref[b, d] = 0
        for j in range(index_ref.shape[1]):
            d = index_ref[b, j] - (first + b) + HALO
            table_ref[b, jnp.where(mask_ref[b, j] != 0, d, 2 * HALO + 1)] = j + 1
    empty = jnp.zeros((BLK, BLK), BF)
    for k in range(KB):
        large[k].wait()
        for b in range(blocks):
            g, r = b // GRP, b % GRP
            tiles = [empty] * r
            for d in range(2 * HALO + 1):
                entry = table_ref[b, d]
                tile = quad_ref[k, b, jnp.maximum(entry - 1, 0)]
                tiles.append(jnp.where(entry > 0, tile, empty))
            tiles += [empty] * (GRP - 1 - r)
            row = k * GRP * BLK + r * BLK
            band_ref[g, row : row + BLK, :] = jnp.concatenate(tiles, axis=1)
            if r == GRP - 1:
                part = slice(k * GRP * BLK, (k + 1) * GRP * BLK)
                flip_ref[g, :, part] = band_ref[g, part, :].T


def band_call(block_index, block_mask, quad):
    blocks = quad.shape[1]
    groups = blocks // GRP
    return pl.pallas_call(
        functools.partial(band_kernel, blocks),
        out_shape=(
            pltpu.VMEM((groups, KB * GRP * BLK, SPAN * BLK), BF),
            pltpu.VMEM((groups, SPAN * BLK, KB * GRP * BLK), BF),
        ),
        in_specs=[HB] * 3,
        out_specs=(VM, VM),
        scratch_shapes=[
            pltpu.SMEM(block_index.shape, jnp.int32),
            pltpu.SMEM(block_mask.shape, jnp.int32),
            pltpu.VMEM(quad.shape, BF),
            pltpu.SMEM((blocks, 2 * HALO + 2), jnp.int32),
            pltpu.SemaphoreType.DMA((KB + 2,)),
        ],
        compiler_params=params(),
        name="band",
    )(*(pltpu.with_memory_space_constraint(a, pltpu.HBM) for a in (block_index, block_mask, quad)))


def hidden_kernel(x_ref, near_ref, far_ref, band_ref, w_ref, hid_ref, gp_ref, ext_ref, sems):
    rows = x_ref.shape[2]
    edge = HALO * BLK
    odd = lax.axis_index("lat") % 2
    ends = [pl.multiple_of(side * (edge + rows), edge) for side in (1 - odd, odd)]
    copies = [
        pltpu.make_async_copy(near_ref, ext_ref.at[:, pl.ds(ends[0], edge)], sems.at[0]),
        pltpu.make_async_copy(x_ref.at[0], ext_ref.at[:, pl.ds(edge, rows)], sems.at[1]),
        pltpu.make_async_copy(far_ref, ext_ref.at[:, pl.ds(ends[1], edge)], sems.at[2]),
    ]
    for c in copies:
        c.start()
    for c in copies:
        c.wait()
    size = GRP * BLK
    for m in range(MB):
        for g in range(rows // size):
            window = ext_ref[m, g * size : g * size + SPAN * BLK, :]
            hid = dot(band_ref[g], window).astype(BF)
            hid_ref[m, g] = hid
            z = dot(hid[:size], w_ref[0, 0])
            for k in range(1, KB):
                z += dot(hid[k * size : (k + 1) * size], w_ref[0, k])
            gp_ref[m, g * size : (g + 1) * size, :] = gelu_slope(z)


def hidden_call(x, near, far, band, weights):
    _, mb, rows, ch = x.shape
    groups = band.shape[0]
    return pl.pallas_call(
        hidden_kernel,
        out_shape=(
            pltpu.VMEM((mb, groups, KB * GRP * BLK, ch), BF),
            pltpu.VMEM((mb, rows, ch), F32),
        ),
        in_specs=[ANY, ANY, ANY, VM, VM],
        out_specs=(VM, VM),
        scratch_shapes=[
            pltpu.VMEM((mb, rows + 2 * HALO * BLK, ch), BF),
            pltpu.SemaphoreType.DMA((3,)),
        ],
        compiler_params=params(),
        name="hidden",
    )(x, near, far, band, weights)


PARTS = {"edge": ("left", "right", "slope"), "bulk": ("out",), "whole": ("left", "right", "slope", "out")}


def back_terms(slope, w_ref, stack_ref):
    size = slope.shape[0]
    for k in range(KB):
        back = lax.dot_general(
            slope, w_ref[0, k], (((1,), (1,)), ((), ())), preferred_element_type=F32
        )
        stack_ref[k * size : (k + 1) * size, :] = back.astype(BF)


def step_kernel(turn, lats, part, *refs):
    first = lats is None
    (main_ref, gp_ref, flip_ref, w_ref), rest = refs[:4], refs[4:]
    if not first:
        (below_ref, above_ref), rest = rest[:2], rest[2 + len(PARTS[part]) :]
    outs, (stack_ref, term_ref) = dict(zip(PARTS[part], rest)), rest[-2:]
    lat = lax.axis_index("lat")
    rows = gp_ref.shape[1]
    size = GRP * BLK
    edge = HALO * BLK
    lap = 2 * edge
    groups = rows // size

    def grad_of(m, g):
        grad = main_ref[m, g * size : (g + 1) * size, :].astype(F32)
        if first:
            return grad
        parts = [grad[i * edge : (i + 1) * edge] for i in range(size // edge)]
        if g == 0:
            parts[0] += jnp.where(lat > 0, below_ref[m].astype(F32), 0.0)
        if g == groups - 1:
            parts[-1] += jnp.where(lat < lats - 1, above_ref[m].astype(F32), 0.0)
        return jnp.concatenate(parts, axis=0).astype(BF).astype(F32)

    def edges(m):
        for name, g, rim, at, low in (
            ("left", 0, 0, 0, 0),
            ("right", groups - 1, size + edge, rows - edge, size - edge),
        ):
            back_terms(outs["slope"][m, at : at + edge, :], w_ref, stack_ref)
            term = None
            for k in range(KB):
                band = flip_ref[g, rim : rim + edge, k * size + low : k * size + low + edge]
                new = dot(band, stack_ref[k * edge : (k + 1) * edge, :])
                term = new if term is None else term + new
            outs[name][m] = term.astype(BF)

    @pl.when(lax.axis_index("section") == turn)
    def _():
        for m in range(MB):
            for g in range(groups):
                grad = grad_of(m, g)
                at = slice(g * size, (g + 1) * size)
                if part == "bulk":
                    slope = gp_ref[m, at, :]
                else:
                    slope = (grad * gp_ref[m, at, :]).astype(BF)
                    outs["slope"][m, at, :] = slope
                if part == "edge":
                    continue
                back_terms(slope, w_ref, stack_ref)
                term = dot(flip_ref[g], stack_ref[...])
                low = g * size
                if g == 0:
                    if part == "whole":
                        outs["left"][m] = term[:edge].astype(BF)
                    term_ref[low + edge : low + lap, :] = term[edge:lap] + grad[: lap - edge]
                else:
                    term_ref[low : low + lap, :] += term[:lap]
                    term_ref[low + edge : low + lap, :] += grad[: lap - edge]
                term_ref[low + lap : low + size + edge, :] = (
                    term[lap : size + edge] + grad[lap - edge :]
                )
                if g < groups - 1:
                    term_ref[low + size + edge : low + size + lap, :] = term[size + edge :]
                elif part == "whole":
                    outs["right"][m] = term[size + edge :].astype(BF)
            if part == "edge":
                edges(m)
            else:
                outs["out"][m] = term_ref[edge : edge + rows, :].astype(BF)


def step_call(turn, lats, part, main, factor, sides, flip, weights, state):
    mb, rows, ch = main.shape
    edge = HALO * BLK
    names = PARTS[part]
    olds = tuple(state[name] for name in names) if sides else ()
    args = (main, factor, flip, weights) + sides + olds
    tall = {"left": edge, "right": edge, "slope": rows, "out": rows}
    outs = pl.pallas_call(
        functools.partial(step_kernel, turn, lats if sides else None, part),
        out_shape=tuple(pltpu.VMEM((mb, tall[name], ch), BF) for name in names),
        in_specs=[VM] * len(args),
        out_specs=(VM,) * len(names),
        input_output_aliases={6 + i: i for i in range(len(olds))},
        scratch_shapes=[
            pltpu.VMEM((KB * GRP * BLK, ch), BF),
            pltpu.VMEM((rows + 2 * edge, ch), F32),
        ],
        compiler_params=params(),
        cost_estimate=cost(3 * MB * rows * KB * ch * ch * 2) if part == "bulk" else None,
    )(*args)
    state.update(zip(names, outs))


def weight_terms(hid_ref, slope_ref, acc_ref):
    size = GRP * BLK
    for k in range(KB):
        total = None
        for m in range(MB):
            for g in range(hid_ref.shape[1]):
                part = lax.dot_general(
                    hid_ref[m, g, k * size : (k + 1) * size, :],
                    slope_ref[m, g * size : (g + 1) * size, :],
                    (((0,), (0,)), ((), ())),
                    preferred_element_type=F32,
                )
                total = part if total is None else total + part
        acc_ref[k * total.shape[0] : (k + 1) * total.shape[0], :] = total


def weight_call(hid, slope):
    ch = slope.shape[2]
    return pl.pallas_call(
        weight_terms,
        out_shape=pltpu.VMEM((KB * ch, ch), F32),
        in_specs=[VM] * 2,
        out_specs=VM,
        compiler_params=params(),
        name="weight",
    )(hid, slope)


def shared(ways, j, own):
    me, second = lax.axis_index("lat"), lax.axis_index("section") % 2 == 1
    ends = [partner_of(ways[2 * j + c], me) for c in range(2)]
    return jnp.where(second == own, ends[1], ends[0])


def lay_edges(out_ref, skip, even_ref, odd_ref):
    odd = lax.axis_index("lat") % 2 == 1
    edge = even_ref.shape[1]
    for m in range(MB):
        out_ref[skip + m * edge : skip + (m + 1) * edge, :] = jnp.where(odd, odd_ref[m], even_ref[m])


def cut_kernel(way, ways, hid_ref, slope_ref, left_ref, right_ref, own_ref, ride_ref, keep_ref, give_ref, acc_ref):
    weight_terms(hid_ref, slope_ref, acc_ref)
    me = lax.axis_index("lat")
    piece = own_ref.shape[0]

    def cut(i):
        return acc_ref[pl.ds(pl.multiple_of(i * piece, piece), piece), :]

    own_ref[...] = cut(me)
    ride_ref[:piece, :] = cut(partner_of(way, me)).astype(BF)
    lay_edges(ride_ref, piece, right_ref, left_ref)
    for j in range(len(ways) // 2):
        keep_ref[j * piece : (j + 1) * piece, :] = cut(shared(ways, j, True)).astype(BF)
        give_ref[j * piece : (j + 1) * piece, :] = cut(shared(ways, j, False)).astype(BF)


def pack_kernel(keep_ref, got_ref, *out_refs):
    piece = out_refs[0].shape[0] // 2
    for j, ref in enumerate(out_refs):
        ref[:piece, :] = keep_ref[j * piece : (j + 1) * piece, :]
        ref[piece:, :] = got_ref[j * piece : (j + 1) * piece, :]


def sum_kernel(own_ref, ride_ref, *refs):
    piece = own_ref.shape[0]
    mine, theirs = own_ref[...] + ride_ref[:piece, :].astype(F32), 0.0
    for ref in refs[:-1]:
        mine += ref[:piece, :].astype(F32)
        theirs += ref[piece:, :].astype(F32)
    refs[-1][:piece, :] = mine.astype(BF)
    refs[-1][piece:, :] = theirs.astype(BF)


def final_kernel(both_ref, got_ref, left_ref, right_ref, pair_ref, ride_ref):
    piece = both_ref.shape[0] // 2
    mine = (both_ref[:piece, :].astype(F32) + got_ref[piece:, :].astype(F32)).astype(BF)
    theirs = (both_ref[piece:, :].astype(F32) + got_ref[:piece, :].astype(F32)).astype(BF)
    pair_ref[:piece, :] = mine
    pair_ref[piece:, :] = theirs
    ride_ref[:piece, :] = mine
    lay_edges(ride_ref, piece, left_ref, right_ref)


def split_kernel(*refs):
    piece = refs[0].shape[0] // 2
    for j, ref in enumerate(refs[:-1]):
        refs[-1][j * piece : (j + 1) * piece, :] = ref[piece:, :]


def join_kernel(way, ways, pair_ref, ride_ref, got_ref, *refs):
    met, weight_ref = refs[:-1], refs[-1]
    me = lax.axis_index("lat")
    piece = pair_ref.shape[0] // 2

    def place(i, value):
        weight_ref[pl.ds(pl.multiple_of(i * piece, piece), piece), :] = value.astype(F32)

    place(me, pair_ref[:piece, :])
    place(partner_of(way, me), ride_ref[:piece, :])
    for j, ref in enumerate(met):
        place(shared(ways, j, True), ref[:piece, :])
        place(shared(ways, j, False), got_ref[j * piece : (j + 1) * piece, :])


def small_call(kernel, shapes, *args, scratch=()):
    return pl.pallas_call(
        kernel,
        out_shape=tuple(shapes),
        in_specs=[VM] * len(args),
        out_specs=(VM,) * len(shapes),
        scratch_shapes=list(scratch),
        compiler_params=params(),
    )(*args)


def reduce_weight(lats, sections, hid, slope, left, right):
    ch = slope.shape[2]
    ways = matchings(lats)
    first, second = ways[1:], ways[:1] + ways[2:]
    count = len(first) // 2
    piece = KB * ch // lats
    ride = piece + MB * left.shape[1]
    swap = [(s, s ^ 1) for s in range(sections)]

    def vmem(rows, dtype=BF):
        return pltpu.VMEM((rows, ch), dtype)

    def meet(arrays, ways):
        return [
            lax.ppermute(
                a,
                ("lat", "section"),
                [
                    (i * sections + s, ways[2 * j + s % 2][i] * sections + s)
                    for i in range(lats)
                    for s in range(sections)
                ],
            )
            for j, a in enumerate(arrays)
        ]

    own, out, keep, give = small_call(
        functools.partial(cut_kernel, ways[0], first),
        (vmem(piece, F32), vmem(ride), vmem(count * piece), vmem(count * piece)),
        hid,
        slope,
        left,
        right,
        scratch=(vmem(KB * ch, F32),),
    )
    got = lax.ppermute(give, "section", swap)
    near = lax.ppermute(out, "lat", list(enumerate(ways[0])))
    packs = small_call(pack_kernel, (vmem(2 * piece),) * count, keep, got)
    (both,) = small_call(sum_kernel, (vmem(2 * piece),), own, near, *meet(packs, first))
    got = lax.ppermute(both, "section", swap)
    pair, out = small_call(final_kernel, (vmem(2 * piece), vmem(ride)), both, got, left, right)
    met = meet([pair] * count, second)
    far = lax.ppermute(out, "lat", list(enumerate(ways[1])))
    (give,) = small_call(split_kernel, (vmem(count * piece),), *met)
    got = lax.ppermute(give, "section", swap)
    (weight,) = small_call(
        functools.partial(join_kernel, ways[1], second),
        (jax.ShapeDtypeStruct((KB * ch, ch), F32),),
        pair,
        far,
        got,
        *met,
    )
    return weight, near, far, piece


def grad_kernel(lats, skip, main_ref, near_ref, far_ref, grad_ref):
    rows = main_ref.shape[1]
    edge = HALO * BLK
    me = lax.axis_index("lat")
    odd = me % 2 == 1
    for m in range(MB):
        at = slice(skip + m * edge, skip + (m + 1) * edge)
        near, far = near_ref[at, :].astype(F32), far_ref[at, :].astype(F32)
        below = jnp.where(me > 0, jnp.where(odd, near, far), 0.0)
        above = jnp.where(me < lats - 1, jnp.where(odd, far, near), 0.0)
        grad_ref[0, m, :edge, :] = (main_ref[m, :edge, :].astype(F32) + below).astype(BF)
        grad_ref[0, m, edge : rows - edge, :] = main_ref[m, edge : rows - edge, :]
        grad_ref[0, m, rows - edge :, :] = (main_ref[m, rows - edge :, :].astype(F32) + above).astype(BF)


def grad_call(lats, skip, main, near, far):
    return pl.pallas_call(
        functools.partial(grad_kernel, lats, skip),
        out_shape=jax.ShapeDtypeStruct((1,) + main.shape, BF),
        in_specs=[VM] * 3,
        out_specs=VM,
        compiler_params=params(),
        name="grad",
    )(main, near, far)


def per_device(saved_input, cotangent, quad_values, block_index, block_mask, weights):
    sections = lax.axis_size("section")
    lats = lax.axis_size("lat")
    edge = HALO * BLK
    rows = saved_input.shape[2]
    both = ("lat", "section")
    odd = lax.axis_index("lat") % 2
    sides = [near_pairs(lats, sections, side) for side in range(2)]

    def rim(high):
        return lax.dynamic_slice_in_dim(saved_input[0], high * (rows - edge), edge, axis=1)

    far = lax.ppermute(rim(odd), both, sides[1])
    near = lax.ppermute(rim(1 - odd), both, sides[0])
    band, flip = band_call(block_index, block_mask, quad_values)
    hid, gp = hidden_call(saved_input, near, far, band, weights)

    state, main, terms = {}, cotangent, ()
    for turn in reversed(range(sections)):
        if turn % 2 or turn == 0:
            step_call(turn, lats, "edge", main, gp, terms, flip, weights, state)
            step_call(turn, lats, "bulk", main, state["slope"], terms, flip, weights, state)
        else:
            step_call(turn, lats, "whole", main, gp, terms, flip, weights, state)
        if turn > 0:
            low = lax.ppermute(state["right"], both, slant_pairs(lats, sections, turn, True))
            high = lax.ppermute(state["left"], both, slant_pairs(lats, sections, turn, False))
            main = lax.ppermute(state["out"], "section", hop_pairs(sections, turn))
            terms = (low, high)

    left, right, slope = (state[name] for name in PARTS["edge"])
    channels = saved_input.shape[3]
    if lats == 8 and sections % 2 == 0:
        weight, near, far, skip = reduce_weight(lats, sections, hid, slope, left, right)
    else:
        give = jnp.where(odd == 1, left, right), jnp.where(odd == 1, right, left)
        near, far = (lax.ppermute(g, both, p).reshape(-1, channels) for g, p in zip(give, sides))
        skip = 0
        weight = lax.psum(weight_call(hid, slope), "lat")
    grad = grad_call(lats, skip, state["out"], near, far)
    return grad, weight.reshape(1, KB, channels, channels)


def solution(mesh):
    in_specs = (
        P("section", None, "lat", None),
        P(None, "lat", None),
        P(None, "lat", None, None, None),
        P("lat", None),
        P("lat", None),
        P("section", None, None, None),
    )
    out_specs = (P("section", None, "lat", None), P("section", None, None, None))
    return jax.shard_map(
        per_device, mesh=mesh, in_specs=in_specs, out_specs=out_specs, check_vma=False
    )
```

```python
import functools

import jax
import jax.numpy as jnp
from jax import lax
from jax.experimental import pallas as pl
from jax.experimental.pallas import tpu as pltpu
from jax.sharding import PartitionSpec as P


KB = 3
BLK = 64
HALO = 2
MB = 2
GRP = 4
SPAN = GRP + 2 * HALO
BF = jnp.bfloat16
F32 = jnp.float32
VM = pl.BlockSpec(memory_space=pltpu.VMEM)
ANY = pl.BlockSpec(memory_space=pl.ANY)
HB = pl.BlockSpec(memory_space=pltpu.HBM)


def gelu_slope(value):
    return (
        0.5 * (1.0 + lax.erf(value * 0.7071067811865476))
        + value * jnp.exp(-0.5 * value * value) * 0.3989422804014327
    )


def params(mib=24):
    return pltpu.CompilerParams(vmem_limit_bytes=mib << 20)


def matchings(n):
    near = [tuple(i ^ 1 for i in range(n)), tuple((i + 1 if i % 2 else i - 1) % n for i in range(n))]
    used = {(i, m[i]) for m in near for i in range(n)}

    def extend(found, now):
        if None not in now:
            found, now = found + [tuple(now)], [None] * n
        if len(found) == n - 3:
            return found
        i = now.index(None)
        for j in range(n - 1, i, -1):
            taken = any(m[i] == j for m in found)
            if now[j] is None and (i, j) not in used and not taken:
                after = list(now)
                after[i], after[j] = j, i
                result = extend(found, after)
                if result:
                    return result
        return None

    return near + extend([], [None] * n)


def partner_of(match, me):
    return sum((jnp.where(me == i, j, 0) for i, j in enumerate(match)), 0)


def near_pairs(lats, sections, side):
    pairs = []
    for i in range(lats):
        j = i ^ 1 if side == 0 else (i + 1 if i % 2 else i - 1)
        for s in range(sections):
            other = j * sections + s if 0 <= j < lats else i * sections + (s ^ 1)
            pairs.append((i * sections + s, other))
    return pairs


def hop_pairs(sections, turn):
    if turn % 2:
        return [(s, s ^ 1) for s in range(sections)]
    return [(s, (s - 1) % sections) for s in range(sections)]


def slant_pairs(lats, sections, turn, upward):
    last, low = lats - 1, turn - 1
    ways = {(i, turn): (i + 1, low) for i in range(last)}
    if turn % 2 and sections > 2:
        aside = (turn - 2) % sections
        ways[last, turn] = (last, aside)
        ways.update({(i, aside): (i - 1, aside) for i in range(1, lats)})
        ways[0, aside] = (0, low)
        ways.update({(i, low): (i, turn) for i in range(lats)})
        for i in range(lats):
            for s in range(sections):
                ways.setdefault((i, s), (i ^ 1, s))
        assert len(set(ways.values())) == lats * sections
    if not upward:
        ways = {(last - i, s): (last - j, r) for (i, s), (j, r) in ways.items()}
    return [(i * sections + s, j * sections + r) for (i, s), (j, r) in ways.items()]


def cost(flops):
    return pl.CostEstimate(flops=flops, bytes_accessed=flops // 256, transcendentals=0)


def dot(a, b):
    return jnp.dot(a, b, preferred_element_type=F32)


def band_kernel(
    blocks, index_in, mask_in, quad_in, band_ref, flip_ref, index_ref, mask_ref, quad_ref, table_ref, sems
):
    first = lax.axis_index("lat") * blocks
    small = [
        pltpu.make_async_copy(index_in, index_ref, sems.at[KB]),
        pltpu.make_async_copy(mask_in, mask_ref, sems.at[KB + 1]),
    ]
    large = [pltpu.make_async_copy(quad_in.at[k], quad_ref.at[k], sems.at[k]) for k in range(KB)]
    for c in small + large:
        c.start()
    for c in small:
        c.wait()
    for b in range(blocks):
        for d in range(2 * HALO + 2):
            table_ref[b, d] = 0
        for j in range(index_ref.shape[1]):
            d = index_ref[b, j] - (first + b) + HALO
            table_ref[b, jnp.where(mask_ref[b, j] != 0, d, 2 * HALO + 1)] = j + 1
    empty = jnp.zeros((BLK, BLK), BF)
    for k in range(KB):
        large[k].wait()
        for b in range(blocks):
            g, r = b // GRP, b % GRP
            tiles = [empty] * r
            for d in range(2 * HALO + 1):
                entry = table_ref[b, d]
                tile = quad_ref[k, b, jnp.maximum(entry - 1, 0)]
                tiles.append(jnp.where(entry > 0, tile, empty))
            tiles += [empty] * (GRP - 1 - r)
            half, rest = divmod(r * BLK, HALO * BLK)
            row = (half * KB + k) * HALO * BLK + rest
            band_ref[g, row : row + BLK, :] = jnp.concatenate(tiles, axis=1)
            if rest + BLK == HALO * BLK:
                part = slice(row - rest, row + BLK)
                flip_ref[g, :, part] = band_ref[g, part, :].T


def band_call(block_index, block_mask, quad):
    blocks = quad.shape[1]
    groups = blocks // GRP
    return pl.pallas_call(
        functools.partial(band_kernel, blocks),
        out_shape=(
            pltpu.VMEM((groups, KB * GRP * BLK, SPAN * BLK), BF),
            pltpu.VMEM((groups, SPAN * BLK, KB * GRP * BLK), BF),
        ),
        in_specs=[HB] * 3,
        out_specs=(VM, VM),
        scratch_shapes=[
            pltpu.SMEM(block_index.shape, jnp.int32),
            pltpu.SMEM(block_mask.shape, jnp.int32),
            pltpu.VMEM(quad.shape, BF),
            pltpu.SMEM((blocks, 2 * HALO + 2), jnp.int32),
            pltpu.SemaphoreType.DMA((KB + 2,)),
        ],
        compiler_params=params(),
        name="band",
    )(*(pltpu.with_memory_space_constraint(a, pltpu.HBM) for a in (block_index, block_mask, quad)))


def hidden_kernel(inner, x_ref, band_ref, w_ref, *refs):
    hid_ref, gp_ref = refs[-2:]
    pair = HALO * BLK
    deep = KB * pair
    groups = band_ref.shape[0]
    spots = [(g, h) for g in range(groups) for h in range(2)]
    spots = spots[1:-1] if inner else [spots[0], spots[-1]]
    odd = lax.axis_index("lat") % 2 == 1
    parts = []
    for m in range(MB):
        for g, h in spots:
            at = (2 * g + h - 1) * pair
            if inner:
                window = x_ref[0, m, at : at + 3 * pair, :]
            elif g == 0:
                rim = jnp.where(odd, refs[0][m], refs[1][m])
                window = jnp.concatenate([rim, x_ref[0, m, : 2 * pair, :]], axis=0)
            else:
                rim = jnp.where(odd, refs[1][m], refs[0][m])
                window = jnp.concatenate([x_ref[0, m, at:, :], rim], axis=0)
            band = band_ref[g, h * deep : (h + 1) * deep, h * pair : h * pair + 3 * pair]
            parts.append(dot(band, window).astype(BF))
            hid_ref[m, g, h * deep : (h + 1) * deep, :] = parts[-1]
    z = None
    for k in range(KB):
        rows = jnp.concatenate([p[k * pair : (k + 1) * pair] for p in parts], axis=0)
        new = dot(rows, w_ref[0, k])
        z = new if z is None else z + new
    gp = gelu_slope(z)
    for i, (m, g, h) in enumerate((m, g, h) for m in range(MB) for g, h in spots):
        gp_ref[m, (2 * g + h) * pair : (2 * g + h + 1) * pair, :] = gp[i * pair : (i + 1) * pair]


def hidden_call(x, band, weights, *rest):
    _, mb, rows, ch = x.shape
    args = (x, band, weights) + rest
    return pl.pallas_call(
        functools.partial(hidden_kernel, not rest),
        out_shape=(
            pltpu.VMEM((mb, band.shape[0], KB * GRP * BLK, ch), BF),
            pltpu.VMEM((mb, rows, ch), F32),
        ),
        in_specs=[VM] * len(args),
        out_specs=(VM, VM),
        input_output_aliases={5: 0, 6: 1} if rest else {},
        compiler_params=params(),
        cost_estimate=None if rest else cost(1 << 30),
        name="outer" if rest else "inner",
    )(*args)


PARTS = {
    "edge": ("left", "right", "slope"),
    "rims": ("left", "right", "slope", "done"),
    "bulk": ("out",),
    "whole": ("left", "right", "slope", "done", "out"),
}


def back_terms(slope, w_ref, stack_ref):
    pair = HALO * BLK
    for k in range(KB):
        back = lax.dot_general(
            slope, w_ref[0, k], (((1,), (1,)), ((), ())), preferred_element_type=F32
        ).astype(BF)
        for h in range(slope.shape[0] // pair):
            stack_ref[(h * KB + k) * pair : (h * KB + k + 1) * pair, :] = back[h * pair : (h + 1) * pair]


def step_kernel(turn, lats, part, *refs):
    first = lats is None
    (main_ref, gp_ref, flip_ref, w_ref), rest = refs[:4], refs[4:]
    if not first:
        below_ref, above_ref = rest[:2]
    outs, (stack_ref, term_ref) = dict(zip(PARTS[part], rest[-2 - len(PARTS[part]) :])), rest[-2:]
    lat = lax.axis_index("lat")
    rows = gp_ref.shape[1]
    size = GRP * BLK
    edge = HALO * BLK
    lap = 2 * edge
    groups = rows // size

    def grad_of(m, g):
        grad = main_ref[m, g * size : (g + 1) * size, :].astype(F32)
        if first:
            return grad
        parts = [grad[i * edge : (i + 1) * edge] for i in range(size // edge)]
        if g == 0:
            parts[0] += jnp.where(lat > 0, below_ref[m].astype(F32), 0.0)
        if g == groups - 1:
            parts[-1] += jnp.where(lat < lats - 1, above_ref[m].astype(F32), 0.0)
        return jnp.concatenate(parts, axis=0).astype(BF).astype(F32)

    def edges():
        slope = outs["slope"]
        rims = [slope[m, at : at + edge, :] for m in range(MB) for at in (0, rows - edge)]
        back_terms(jnp.concatenate(rims, axis=0), w_ref, stack_ref)
        deep = KB * edge
        for m in range(MB):
            low = stack_ref[2 * m * deep : (2 * m + 1) * deep, :]
            outs["left"][m] = dot(flip_ref[0, :edge, :deep], low).astype(BF)
            high = stack_ref[(2 * m + 1) * deep : (2 * m + 2) * deep, :]
            outs["right"][m] = dot(flip_ref[groups - 1, size + edge :, deep:], high).astype(BF)

    @pl.when(lax.axis_index("section") == turn)
    def _():
        for m in range(MB):
            for g in range(groups):
                grad = grad_of(m, g)
                at = slice(g * size, (g + 1) * size)
                if part == "bulk":
                    slope = gp_ref[m, at, :]
                else:
                    slope = (grad * gp_ref[m, at, :]).astype(BF)
                    outs["slope"][m, at, :] = slope
                if "done" in outs and g == 0:
                    outs["done"][m, :edge, :] = grad[:edge].astype(BF)
                if "done" in outs and g == groups - 1:
                    outs["done"][m, edge:, :] = grad[size - edge :].astype(BF)
                if part in ("edge", "rims"):
                    continue
                back_terms(slope, w_ref, stack_ref)
                term = dot(flip_ref[g], stack_ref[: KB * size, :])
                low = g * size
                if g == 0:
                    if part == "whole":
                        outs["left"][m] = term[:edge].astype(BF)
                    term_ref[low + edge : low + lap, :] = term[edge:lap] + grad[: lap - edge]
                else:
                    term_ref[low : low + lap, :] += term[:lap]
                    term_ref[low + edge : low + lap, :] += grad[: lap - edge]
                term_ref[low + lap : low + size + edge, :] = (
                    term[lap : size + edge] + grad[lap - edge :]
                )
                if g < groups - 1:
                    term_ref[low + size + edge : low + size + lap, :] = term[size + edge :]
                elif part == "whole":
                    outs["right"][m] = term[size + edge :].astype(BF)
            if "out" in outs:
                outs["out"][m] = term_ref[edge : edge + rows, :].astype(BF)
        if "out" not in outs:
            edges()


def step_call(turn, lats, part, main, factor, sides, flip, weights, state):
    mb, rows, ch = main.shape
    edge = HALO * BLK
    names = PARTS[part]
    known = [name for name in names if name in state]
    args = (main, factor, flip, weights) + sides + tuple(state[name] for name in known)
    tall = {"left": edge, "right": edge, "slope": rows, "done": 2 * edge, "out": rows}
    outs = pl.pallas_call(
        functools.partial(step_kernel, turn, lats if sides else None, part),
        out_shape=tuple(pltpu.VMEM((mb, tall[name], ch), BF) for name in names),
        in_specs=[VM] * len(args),
        out_specs=(VM,) * len(names),
        input_output_aliases={
            len(args) - len(known) + i: names.index(name) for i, name in enumerate(known)
        },
        scratch_shapes=[
            pltpu.VMEM((KB * max(GRP * BLK, 2 * MB * edge), ch), BF),
            pltpu.VMEM((rows + 2 * edge, ch), F32),
        ],
        compiler_params=params(),
        cost_estimate=cost(3 * MB * rows * KB * ch * ch * 2) if part == "bulk" else None,
    )(*args)
    state.update(zip(names, outs))


def weight_terms(hid_ref, slope_ref, acc_ref):
    size = GRP * BLK
    edge = HALO * BLK
    for k in range(KB):
        total = None
        for m in range(MB):
            for g in range(hid_ref.shape[1]):
                pairs = [hid_ref[m, g, i * edge : (i + 1) * edge, :] for i in (k, KB + k)]
                part = lax.dot_general(
                    jnp.concatenate(pairs, axis=0),
                    slope_ref[m, g * size : (g + 1) * size, :],
                    (((0,), (0,)), ((), ())),
                    preferred_element_type=F32,
                )
                total = part if total is None else total + part
        acc_ref[k * total.shape[0] : (k + 1) * total.shape[0], :] = total


def weight_call(hid, slope):
    ch = slope.shape[2]
    return pl.pallas_call(
        weight_terms,
        out_shape=pltpu.VMEM((KB * ch, ch), F32),
        in_specs=[VM] * 2,
        out_specs=VM,
        compiler_params=params(),
        name="weight",
    )(hid, slope)


def shared(ways, j, own):
    me, second = lax.axis_index("lat"), lax.axis_index("section") % 2 == 1
    ends = [partner_of(ways[2 * j + c], me) for c in range(2)]
    return jnp.where(second == own, ends[1], ends[0])


def lay_edges(even_ref, odd_ref):
    odd = lax.axis_index("lat") % 2 == 1
    return jnp.concatenate([jnp.where(odd, odd_ref[m], even_ref[m]) for m in range(MB)], axis=0)


def cut_kernel(way, ways, hid_ref, slope_ref, left_ref, right_ref, own_ref, ride_ref, keep_ref, give_ref, acc_ref):
    weight_terms(hid_ref, slope_ref, acc_ref)
    me = lax.axis_index("lat")
    piece = own_ref.shape[0]

    def cut(i):
        return acc_ref[pl.ds(pl.multiple_of(i * piece, piece), piece), :]

    own_ref[...] = cut(me)
    ride_ref[...] = cut(partner_of(way, me)).astype(BF)
    count = len(ways) // 2
    for j in range(count):
        keep_ref[j * piece : (j + 1) * piece, :] = cut(shared(ways, j, True)).astype(BF)
        give_ref[j * piece : (j + 1) * piece, :] = cut(shared(ways, j, False)).astype(BF)
    give_ref[count * piece :, :] = lay_edges(left_ref, right_ref)


def pack_kernel(keep_ref, got_ref, left_ref, right_ref, *out_refs):
    piece = out_refs[-1].shape[0] // 2
    for j, ref in enumerate(out_refs):
        ref[:piece, :] = keep_ref[j * piece : (j + 1) * piece, :]
        ref[piece : 2 * piece, :] = got_ref[j * piece : (j + 1) * piece, :]
    second = lax.axis_index("section") % 2 == 1
    rims = jnp.where(second, got_ref[len(out_refs) * piece :, :], lay_edges(right_ref, left_ref))
    out_refs[0][2 * piece :, :] = rims


def sum_kernel(own_ref, ride_ref, *refs):
    piece = own_ref.shape[0]
    mine, theirs = own_ref[...] + ride_ref[...].astype(F32), 0.0
    for ref in refs[:-1]:
        mine += ref[:piece, :].astype(F32)
        theirs += ref[piece : 2 * piece, :].astype(F32)
    refs[-1][:piece, :] = mine.astype(BF)
    refs[-1][piece:, :] = theirs.astype(BF)


def final_kernel(both_ref, got_ref, rims_ref, done_ref, pair_ref, ride_ref, aside_ref):
    piece = both_ref.shape[0] // 2
    mine = (both_ref[:piece, :].astype(F32) + got_ref[piece:, :].astype(F32)).astype(BF)
    theirs = (both_ref[piece:, :].astype(F32) + got_ref[:piece, :].astype(F32)).astype(BF)
    pair_ref[:piece, :] = mine
    pair_ref[piece:, :] = theirs
    ride_ref[...] = mine
    edges = rims_ref.shape[0] - 2 * piece
    aside_ref[:edges, :] = rims_ref[2 * piece :, :]
    rows = done_ref.shape[1]
    for m in range(MB):
        aside_ref[edges + m * rows : edges + (m + 1) * rows, :] = done_ref[m]


def split_kernel(*refs):
    piece = refs[0].shape[0] // 2
    for j, ref in enumerate(refs[:-1]):
        refs[-1][j * piece : (j + 1) * piece, :] = ref[piece:, :]


def join_kernel(way, ways, pair_ref, ride_ref, got_ref, *refs):
    met, weight_ref = refs[:-1], refs[-1]
    me = lax.axis_index("lat")
    piece = pair_ref.shape[0] // 2

    def place(i, value):
        weight_ref[pl.ds(pl.multiple_of(i * piece, piece), piece), :] = value.astype(F32)

    place(me, pair_ref[:piece, :])
    place(partner_of(way, me), ride_ref[...])
    for j, ref in enumerate(met):
        place(shared(ways, j, True), ref[:piece, :])
        place(shared(ways, j, False), got_ref[j * piece : (j + 1) * piece, :])


def small_call(kernel, shapes, *args, scratch=()):
    return pl.pallas_call(
        kernel,
        out_shape=tuple(shapes),
        in_specs=[VM] * len(args),
        out_specs=(VM,) * len(shapes),
        scratch_shapes=list(scratch),
        compiler_params=params(),
    )(*args)


def reduce_weight(lats, sections, hid, state):
    left, right, slope, done = (state[name] for name in PARTS["rims"])
    ch = slope.shape[2]
    near, far, way, *others = matchings(lats)
    ways = [near, far] + others
    count = len(ways) // 2
    piece = KB * ch // lats
    edges = MB * left.shape[1]
    swap = [(s, s ^ 1) for s in range(sections)]

    def vmem(rows, dtype=BF):
        return pltpu.VMEM((rows, ch), dtype)

    def meet(arrays):
        got = []
        for j, a in enumerate(arrays):
            pairs = [
                (i * sections + s, ways[2 * j + s % 2][i] * sections + s)
                for i in range(lats)
                for s in range(sections)
            ]
            got.append(lax.ppermute(a, ("lat", "section"), pairs))
        return got

    own, out, keep, give = small_call(
        functools.partial(cut_kernel, way, ways),
        (vmem(piece, F32), vmem(piece), vmem(count * piece), vmem(count * piece + edges)),
        hid,
        slope,
        left,
        right,
        scratch=(vmem(KB * ch, F32),),
    )
    straight = list(enumerate(way))
    ride = lax.ppermute(out, "lat", straight)
    got = lax.ppermute(give, "section", swap)
    shapes = [vmem(2 * piece + (0 if j else edges)) for j in range(count)]
    packs = small_call(pack_kernel, shapes, keep, got, left, right)
    met = meet(packs)
    rims = met[0]
    (both,) = small_call(sum_kernel, (vmem(2 * piece),), own, ride, *met)
    got = lax.ppermute(both, "section", swap)
    shapes = (vmem(2 * piece), vmem(piece), vmem(edges + MB * done.shape[1]))
    pair, out, aside = small_call(final_kernel, shapes, both, got, rims, done)
    met = meet([pair] * count)
    ride = lax.ppermute(out, "lat", straight)
    aside = lax.ppermute(aside, "section", swap)
    (give,) = small_call(split_kernel, (vmem(count * piece),), *met)
    got = lax.ppermute(give, "section", swap)
    (weight,) = small_call(
        functools.partial(join_kernel, way, ways),
        (jax.ShapeDtypeStruct((KB * ch, ch), F32),),
        pair,
        ride,
        got,
        *met,
    )
    return weight, rims, aside, 2 * piece


def grad_kernel(lats, skip, main_ref, near_ref, far_ref, grad_ref):
    rows = main_ref.shape[1]
    edge = HALO * BLK
    me = lax.axis_index("lat")
    odd = me % 2 == 1
    behind = far_ref.shape[0] > MB * edge
    finished = jnp.logical_and(lax.axis_index("section") % 2 == 1, behind)
    for m in range(MB):
        near = near_ref[skip + m * edge : skip + (m + 1) * edge, :].astype(F32)
        far = far_ref[m * edge : (m + 1) * edge, :].astype(F32)
        below = jnp.where(me > 0, jnp.where(odd, near, far), 0.0)
        above = jnp.where(me < lats - 1, jnp.where(odd, far, near), 0.0)
        low = (main_ref[m, :edge, :].astype(F32) + below).astype(BF)
        high = (main_ref[m, rows - edge :, :].astype(F32) + above).astype(BF)
        if behind:
            at = (MB + 2 * m) * edge
            low = jnp.where(finished, far_ref[at : at + edge, :], low)
            high = jnp.where(finished, far_ref[at + edge : at + 2 * edge, :], high)
        grad_ref[0, m, :edge, :] = low
        grad_ref[0, m, edge : rows - edge, :] = main_ref[m, edge : rows - edge, :]
        grad_ref[0, m, rows - edge :, :] = high


def grad_call(lats, skip, main, near, far):
    return pl.pallas_call(
        functools.partial(grad_kernel, lats, skip),
        out_shape=jax.ShapeDtypeStruct((1,) + main.shape, BF),
        in_specs=[VM] * 3,
        out_specs=VM,
        compiler_params=params(),
        name="grad",
    )(main, near, far)


def per_device(saved_input, cotangent, quad_values, block_index, block_mask, weights):
    sections = lax.axis_size("section")
    lats = lax.axis_size("lat")
    edge = HALO * BLK
    rows = saved_input.shape[2]
    both = ("lat", "section")
    odd = lax.axis_index("lat") % 2
    sides = [near_pairs(lats, sections, side) for side in range(2)]

    def rim(high):
        return lax.dynamic_slice_in_dim(saved_input[0], high * (rows - edge), edge, axis=1)

    far = lax.ppermute(rim(odd), both, sides[1])
    near = lax.ppermute(rim(1 - odd), both, sides[0])
    band, flip = band_call(block_index, block_mask, quad_values)
    hid, gp = hidden_call(saved_input, band, weights)
    hid, gp = hidden_call(saved_input, band, weights, near, far, hid, gp)

    state, main, terms = {}, cotangent, ()
    for turn in reversed(range(sections)):
        if turn % 2 or turn == 0:
            step_call(turn, lats, "edge" if turn else "rims", main, gp, terms, flip, weights, state)
            step_call(turn, lats, "bulk", main, state["slope"], terms, flip, weights, state)
        else:
            step_call(turn, lats, "whole", main, gp, terms, flip, weights, state)
        if turn > 0:
            low = lax.ppermute(state["right"], both, slant_pairs(lats, sections, turn, True))
            high = lax.ppermute(state["left"], both, slant_pairs(lats, sections, turn, False))
            main = lax.ppermute(state["out"], "section", hop_pairs(sections, turn))
            terms = (low, high)

    left, right, slope = (state[name] for name in PARTS["edge"])
    channels = saved_input.shape[3]
    if lats == 8 and sections % 2 == 0:
        weight, near, far, skip = reduce_weight(lats, sections, hid, state)
        grad = grad_call(lats, skip, state["out"], near, far)
    else:
        give = jnp.where(odd == 1, left, right), jnp.where(odd == 1, right, left)
        near, far = (lax.ppermute(g, both, p).reshape(-1, channels) for g, p in zip(give, sides))
        weight = lax.psum(weight_call(hid, slope), "lat")
        grad = grad_call(lats, 0, state["out"], near, far)
    return grad, weight.reshape(1, KB, channels, channels)


def solution(mesh):
    in_specs = (
        P("section", None, "lat", None),
        P(None, "lat", None),
        P(None, "lat", None, None, None),
        P("lat", None),
        P("lat", None),
        P("section", None, None, None),
    )
    out_specs = (P("section", None, "lat", None), P("section", None, None, None))
    return jax.shard_map(
        per_device, mesh=mesh, in_specs=in_specs, out_specs=out_specs, check_vma=False
    )
```

```python
import functools

import jax
import jax.numpy as jnp
from jax import lax
from jax.experimental import pallas as pl
from jax.experimental.pallas import tpu as pltpu
from jax.sharding import PartitionSpec as P


KB = 3
BLK = 64
HALO = 2
MB = 2
GRP = 4
SPAN = GRP + 2 * HALO
BF = jnp.bfloat16
F32 = jnp.float32
VM = pl.BlockSpec(memory_space=pltpu.VMEM)
ANY = pl.BlockSpec(memory_space=pl.ANY)
HB = pl.BlockSpec(memory_space=pltpu.HBM)


def gelu_slope(value):
    return (
        0.5 * (1.0 + lax.erf(value * 0.7071067811865476))
        + value * jnp.exp(-0.5 * value * value) * 0.3989422804014327
    )


def params(mib=24):
    return pltpu.CompilerParams(vmem_limit_bytes=mib << 20)


def near_pairs(lats, sections, side):
    pairs = []
    for i in range(lats):
        j = i ^ 1 if side == 0 else (i + 1 if i % 2 else i - 1)
        for s in range(sections):
            other = j * sections + s if 0 <= j < lats else i * sections + (s ^ 1)
            pairs.append((i * sections + s, other))
    return pairs


def edge_pairs(lats, sections):
    both = [near_pairs(lats, sections, side) for side in range(2)]
    pairs = []
    for i in range(lats):
        for s in range(sections):
            here = i * sections + s
            if s % 2 and (i == 0 or i == lats - 1):
                pairs.append((here, i * sections + (s + 2) % sections))
            else:
                pairs.append((here, dict(both[s % 2])[here]))
    return pairs


def hop_pairs(sections, turn):
    if turn % 2:
        return [(s, s ^ 1) for s in range(sections)]
    return [(s, (s - 1) % sections) for s in range(sections)]


def slant_pairs(lats, sections, turn, upward):
    last, low = lats - 1, turn - 1
    ways = {(i, turn): (i + 1, low) for i in range(last)}
    if turn % 2 and sections > 2:
        aside = (turn - 2) % sections
        ways[last, turn] = (last, aside)
        ways.update({(i, aside): (i - 1, aside) for i in range(1, lats)})
        ways[0, aside] = (0, low)
        ways.update({(i, low): (i, turn) for i in range(lats)})
        for i in range(lats):
            for s in range(sections):
                ways.setdefault((i, s), (i ^ 1, s))
        assert len(set(ways.values())) == lats * sections
    if not upward:
        ways = {(last - i, s): (last - j, r) for (i, s), (j, r) in ways.items()}
    return [(i * sections + s, j * sections + r) for (i, s), (j, r) in ways.items()]


def cost(flops):
    return pl.CostEstimate(flops=flops, bytes_accessed=flops // 256, transcendentals=0)


def dot(a, b):
    return jnp.dot(a, b, preferred_element_type=F32)


def band_kernel(
    blocks, index_in, mask_in, quad_in, band_ref, flip_ref, index_ref, mask_ref, quad_ref, table_ref, sems
):
    first = lax.axis_index("lat") * blocks
    small = [
        pltpu.make_async_copy(index_in, index_ref, sems.at[KB]),
        pltpu.make_async_copy(mask_in, mask_ref, sems.at[KB + 1]),
    ]
    large = [pltpu.make_async_copy(quad_in.at[k], quad_ref.at[k], sems.at[k]) for k in range(KB)]
    for c in small + large:
        c.start()
    for c in small:
        c.wait()
    for b in range(blocks):
        for d in range(2 * HALO + 2):
            table_ref[b, d] = 0
        for j in range(index_ref.shape[1]):
            d = index_ref[b, j] - (first + b) + HALO
            table_ref[b, jnp.where(mask_ref[b, j] != 0, d, 2 * HALO + 1)] = j + 1
    empty = jnp.zeros((BLK, BLK), BF)
    for k in range(KB):
        large[k].wait()
        for b in range(blocks):
            g, r = b // GRP, b % GRP
            tiles = [empty] * r
            for d in range(2 * HALO + 1):
                entry = table_ref[b, d]
                tile = quad_ref[k, b, jnp.maximum(entry - 1, 0)]
                tiles.append(jnp.where(entry > 0, tile, empty))
            tiles += [empty] * (GRP - 1 - r)
            half, rest = divmod(r * BLK, HALO * BLK)
            row = (half * KB + k) * HALO * BLK + rest
            band_ref[g, row : row + BLK, :] = jnp.concatenate(tiles, axis=1)
            if rest + BLK == HALO * BLK:
                part = slice(row - rest, row + BLK)
                flip_ref[g, :, part] = band_ref[g, part, :].T


def band_call(block_index, block_mask, quad):
    blocks = quad.shape[1]
    groups = blocks // GRP
    return pl.pallas_call(
        functools.partial(band_kernel, blocks),
        out_shape=(
            pltpu.VMEM((groups, KB * GRP * BLK, SPAN * BLK), BF),
            pltpu.VMEM((groups, SPAN * BLK, KB * GRP * BLK), BF),
        ),
        in_specs=[HB] * 3,
        out_specs=(VM, VM),
        scratch_shapes=[
            pltpu.SMEM(block_index.shape, jnp.int32),
            pltpu.SMEM(block_mask.shape, jnp.int32),
            pltpu.VMEM(quad.shape, BF),
            pltpu.SMEM((blocks, 2 * HALO + 2), jnp.int32),
            pltpu.SemaphoreType.DMA((KB + 2,)),
        ],
        compiler_params=params(),
        name="band",
    )(*(pltpu.with_memory_space_constraint(a, pltpu.HBM) for a in (block_index, block_mask, quad)))


def hidden_kernel(inner, x_ref, band_ref, w_ref, *refs):
    hid_ref, gp_ref = refs[-2:]
    pair = HALO * BLK
    deep = KB * pair
    groups = band_ref.shape[0]
    spots = [(g, h) for g in range(groups) for h in range(2)]
    spots = spots[1:-1] if inner else [spots[0], spots[-1]]
    odd = lax.axis_index("lat") % 2 == 1
    parts = []
    for m in range(MB):
        for g, h in spots:
            at = (2 * g + h - 1) * pair
            if inner:
                window = x_ref[0, m, at : at + 3 * pair, :]
            elif g == 0:
                rim = jnp.where(odd, refs[0][m], refs[1][m])
                window = jnp.concatenate([rim, x_ref[0, m, : 2 * pair, :]], axis=0)
            else:
                rim = jnp.where(odd, refs[1][m], refs[0][m])
                window = jnp.concatenate([x_ref[0, m, at:, :], rim], axis=0)
            band = band_ref[g, h * deep : (h + 1) * deep, h * pair : h * pair + 3 * pair]
            parts.append(dot(band, window).astype(BF))
            hid_ref[m, g, h * deep : (h + 1) * deep, :] = parts[-1]
    z = None
    for k in range(KB):
        rows = jnp.concatenate([p[k * pair : (k + 1) * pair] for p in parts], axis=0)
        new = dot(rows, w_ref[0, k])
        z = new if z is None else z + new
    gp = gelu_slope(z)
    for i, (m, g, h) in enumerate((m, g, h) for m in range(MB) for g, h in spots):
        gp_ref[m, (2 * g + h) * pair : (2 * g + h + 1) * pair, :] = gp[i * pair : (i + 1) * pair]


def hidden_call(x, band, weights, *rest):
    _, mb, rows, ch = x.shape
    args = (x, band, weights) + rest
    return pl.pallas_call(
        functools.partial(hidden_kernel, not rest),
        out_shape=(
            pltpu.VMEM((mb, band.shape[0], KB * GRP * BLK, ch), BF),
            pltpu.VMEM((mb, rows, ch), F32),
        ),
        in_specs=[VM] * len(args),
        out_specs=(VM, VM),
        input_output_aliases={5: 0, 6: 1} if rest else {},
        compiler_params=params(),
        cost_estimate=None if rest else cost(1 << 30),
        name="outer" if rest else "inner",
    )(*args)


PARTS = {
    "edge": ("left", "right", "slope"),
    "slope": ("slope", "done"),
    "tips": ("left", "right"),
    "bulk": ("out",),
    "head": ("slope", "done", "out", "sent0"),
    "tail": ("left", "right", "slope", "done", "out", "sent1"),
}
MICROS = {"head": (0,), "tail": (1,)}


def back_terms(slope, w_ref, stack_ref):
    pair = HALO * BLK
    for k in range(KB):
        back = lax.dot_general(
            slope, w_ref[0, k], (((1,), (1,)), ((), ())), preferred_element_type=F32
        ).astype(BF)
        for h in range(slope.shape[0] // pair):
            stack_ref[(h * KB + k) * pair : (h * KB + k + 1) * pair, :] = back[h * pair : (h + 1) * pair]


def step_kernel(turn, lats, part, form, *refs):
    outs, (stack_ref, term_ref) = dict(zip(PARTS[part], refs[-2 - len(PARTS[part]) :])), refs[-2:]
    (gp_ref, flip_ref, w_ref), rest = refs[:3], refs[3:]
    lat = lax.axis_index("lat")
    rows = gp_ref.shape[1]
    size = GRP * BLK
    edge = HALO * BLK
    lap = 2 * edge
    groups = rows // size

    micros = MICROS.get(part, range(MB))
    slope_ref = outs.get("slope", gp_ref)

    def grad_of(m, g):
        at = slice(g * size, (g + 1) * size)
        grad = (rest[m][at, :] if form == "micro" else rest[0][m, at, :]).astype(F32)
        if form == "whole":
            return grad
        below_ref, above_ref = rest[MB : MB + 2] if form == "micro" else rest[1:3]
        parts = [grad[i * edge : (i + 1) * edge] for i in range(size // edge)]
        if g == 0:
            parts[0] += jnp.where(lat > 0, below_ref[m].astype(F32), 0.0)
        if g == groups - 1:
            parts[-1] += jnp.where(lat < lats - 1, above_ref[m].astype(F32), 0.0)
        return jnp.concatenate(parts, axis=0).astype(BF).astype(F32)

    def tips():
        rims = [slope_ref[m, at : at + edge, :] for m in range(MB) for at in (0, rows - edge)]
        back_terms(jnp.concatenate(rims, axis=0), w_ref, stack_ref)
        deep = KB * edge
        for m in range(MB):
            low = stack_ref[2 * m * deep : (2 * m + 1) * deep, :]
            outs["left"][m] = dot(flip_ref[0, :edge, :deep], low).astype(BF)
            high = stack_ref[(2 * m + 1) * deep : (2 * m + 2) * deep, :]
            outs["right"][m] = dot(flip_ref[groups - 1, size + edge :, deep:], high).astype(BF)

    def slopes():
        for m in micros:
            for g in range(groups):
                grad = grad_of(m, g)
                at = slice(g * size, (g + 1) * size)
                outs["slope"][m, at, :] = (grad * gp_ref[m, at, :]).astype(BF)
                if "done" in outs and g == 0:
                    outs["done"][m, :edge, :] = grad[:edge].astype(BF)
                if "done" in outs and g == groups - 1:
                    outs["done"][m, edge:, :] = grad[size - edge :].astype(BF)

    def terms(m):
        for g in range(groups):
            grad = grad_of(m, g)
            back_terms(slope_ref[m, g * size : (g + 1) * size, :], w_ref, stack_ref)
            term = dot(flip_ref[g], stack_ref[: KB * size, :])
            low = g * size
            if g == 0:
                term_ref[low + edge : low + lap, :] = term[edge:lap] + grad[: lap - edge]
            else:
                term_ref[low : low + lap, :] += term[:lap]
                term_ref[low + edge : low + lap, :] += grad[: lap - edge]
            term_ref[low + lap : low + size + edge, :] = term[lap : size + edge] + grad[lap - edge :]
            if g < groups - 1:
                term_ref[low + size + edge : low + size + lap, :] = term[size + edge :]
        out = term_ref[edge : edge + rows, :].astype(BF)
        outs["out"][m] = out
        if part in MICROS:
            outs[f"sent{m}"][...] = out

    @pl.when(lax.axis_index("section") == turn)
    def _():
        if "slope" in outs:
            slopes()
        if "out" in outs:
            for m in micros:
                terms(m)
        if "left" in outs:
            tips()


def step_call(turn, lats, part, grads, flip, weights, state):
    mb, rows, ch = state["gp"].shape
    edge = HALO * BLK
    names = PARTS[part]
    known = [name for name in names if name in state]
    form = {1: "whole", 3: "summed", 4: "micro"}[len(grads)]
    factor = state["gp" if "slope" in names else "slope"]
    args = (factor, flip, weights) + grads + tuple(state[name] for name in known)
    tall = {"left": edge, "right": edge, "done": 2 * edge}
    shapes = {name: (mb, tall.get(name, rows), ch) for name in names}
    shapes.update({name: (rows, ch) for name in names if name.startswith("sent")})
    outs = pl.pallas_call(
        functools.partial(step_kernel, turn, lats, part, form),
        out_shape=tuple(pltpu.VMEM(shapes[name], BF) for name in names),
        in_specs=[VM] * len(args),
        out_specs=(VM,) * len(names),
        input_output_aliases={
            len(args) - len(known) + i: names.index(name) for i, name in enumerate(known)
        },
        scratch_shapes=[
            pltpu.VMEM((KB * max(GRP * BLK, 2 * MB * edge), ch), BF),
            pltpu.VMEM((rows + 2 * edge, ch), F32),
        ],
        compiler_params=params(),
    )(*args)
    state.update(zip(names, outs))


def weight_terms(hid_ref, slope_ref, acc_ref):
    size = GRP * BLK
    edge = HALO * BLK
    for k in range(KB):
        total = None
        for m in range(MB):
            for g in range(hid_ref.shape[1]):
                pairs = [hid_ref[m, g, i * edge : (i + 1) * edge, :] for i in (k, KB + k)]
                part = lax.dot_general(
                    jnp.concatenate(pairs, axis=0),
                    slope_ref[m, g * size : (g + 1) * size, :],
                    (((0,), (0,)), ((), ())),
                    preferred_element_type=F32,
                )
                total = part if total is None else total + part
        acc_ref[k * total.shape[0] : (k + 1) * total.shape[0], :] = total


def weight_call(hid, slope):
    ch = slope.shape[2]
    return pl.pallas_call(
        weight_terms,
        out_shape=pltpu.VMEM((KB * ch, ch), F32),
        in_specs=[VM] * 2,
        out_specs=VM,
        compiler_params=params(),
        name="weight",
    )(hid, slope)


def lay_edges(even_ref, odd_ref):
    odd = lax.axis_index("lat") % 2 == 1
    return jnp.concatenate([jnp.where(odd, odd_ref[m], even_ref[m]) for m in range(MB)], axis=0)


def cut_kernel(hid_ref, slope_ref, own_ref, one_ref, pair_ref, two_ref, three_ref, far_ref, acc_ref):
    weight_terms(hid_ref, slope_ref, acc_ref)
    me = lax.axis_index("lat")
    piece = own_ref.shape[0]

    def cut(bits):
        return acc_ref[pl.ds(pl.multiple_of((me ^ bits) * piece, piece), piece), :]

    own_ref[...] = cut(0)
    one_ref[...] = cut(1).astype(BF)
    for j, bits in enumerate((5, 7)):
        pair_ref[j * piece : (j + 1) * piece, :] = cut(bits).astype(BF)
    two_ref[...] = cut(2).astype(BF)
    three_ref[...] = cut(3).astype(BF)
    far_ref[:piece, :] = cut(4)
    far_ref[piece:, :] = cut(6)


def middle_kernel(far_ref, pair_ref, four_ref, six_ref):
    piece = four_ref.shape[0]
    four_ref[...] = (far_ref[:piece, :] + pair_ref[:piece, :].astype(F32)).astype(BF)
    six_ref[...] = (far_ref[piece:, :] + pair_ref[piece:, :].astype(F32)).astype(BF)


def give_kernel(left_ref, right_ref, out_ref):
    out_ref[...] = lay_edges(left_ref, right_ref)


def sum_kernel(own_ref, *refs):
    total = own_ref[...]
    for ref in refs[:-1]:
        total += ref[: total.shape[0], :].astype(F32)
    refs[-1][...] = total.astype(BF)


def pack_kernel(*refs):
    at = 0
    for ref in refs[:-1]:
        for value in [ref[...]] if len(ref.shape) == 2 else [ref[m] for m in range(ref.shape[0])]:
            refs[-1][at : at + value.shape[0], :] = value
            at += value.shape[0]


def rims_kernel(got_ref, left_ref, right_ref, out_ref):
    second = lax.axis_index("section") % 2 == 1
    out_ref[...] = jnp.where(second, got_ref[...], lay_edges(right_ref, left_ref))


def join_kernel(spots, piece, *refs):
    refs, (weight_ref, wide_ref, sems) = refs[: len(set(s[0] for s in spots))], refs[-3:]
    me = lax.axis_index("lat")
    copies = []
    for j, (source, part, bits) in enumerate(spots):
        wide_ref[j] = refs[source][part * piece : (part + 1) * piece, :].astype(F32)
        at = pl.multiple_of((me ^ bits) * piece, piece)
        copies.append(pltpu.make_async_copy(wide_ref.at[j], weight_ref.at[pl.ds(at, piece)], sems.at[j]))
        copies[-1].start()
    for c in copies:
        c.wait()


def join_call(lats, spots, sources, old=()):
    ch = sources[0].shape[1]
    piece = KB * ch // lats
    return pl.pallas_call(
        functools.partial(join_kernel, spots, piece),
        out_shape=jax.ShapeDtypeStruct((KB * ch, ch), F32),
        in_specs=[VM] * len(sources) + [ANY] * len(old),
        out_specs=ANY,
        input_output_aliases={len(sources): 0} if old else {},
        scratch_shapes=[
            pltpu.VMEM((len(spots), piece, ch), F32),
            pltpu.SemaphoreType.DMA((len(spots),)),
        ],
        compiler_params=params(),
    )(*sources, *old)


def small_call(kernel, shapes, *args, scratch=()):
    return pl.pallas_call(
        kernel,
        out_shape=tuple(shapes),
        in_specs=[VM] * len(args),
        out_specs=(VM,) * len(shapes),
        scratch_shapes=list(scratch),
        compiler_params=params(),
    )(*args)


def reduce_weight(lats, sections, hid, state):
    left, right, slope, done = (state[name] for name in ("left", "right", "slope", "done"))
    ch = slope.shape[2]
    piece = KB * ch // lats
    edges = MB * left.shape[1]
    swap = [(s, s ^ 1) for s in range(sections)]

    def vmem(rows, dtype=BF):
        return pltpu.VMEM((rows, ch), dtype)

    def meet(a, bits):
        return lax.ppermute(a, "lat", [(i, i ^ bits) for i in range(lats)])

    shapes = (vmem(piece, F32), vmem(piece), vmem(2 * piece), vmem(piece), vmem(piece), vmem(2 * piece, F32))
    own, one, pair, two, three, far = small_call(cut_kernel, shapes, hid, slope, scratch=(vmem(KB * ch, F32),))
    pair, two, three, one = meet(pair, 1), meet(two, 2), meet(three, 3), meet(one, 1)
    (give,) = small_call(give_kernel, (vmem(edges),), left, right)
    got = lax.ppermute(give, "section", swap)
    four, six = small_call(middle_kernel, (vmem(piece), vmem(piece)), far, pair)
    four, six = meet(four, 4), meet(six, 6)
    (rims,) = small_call(rims_kernel, (vmem(edges),), got, left, right)
    rims = lax.ppermute(rims, ("lat", "section"), edge_pairs(lats, sections))
    (mine,) = small_call(sum_kernel, (vmem(piece),), own, one, two, three, four, six)
    four, six = meet(mine, 4), meet(mine, 6)
    two, three = meet(mine, 2), meet(mine, 3)
    (one,) = small_call(pack_kernel, (vmem(3 * piece),), mine, four, six)
    one = meet(one, 1)
    (aside,) = small_call(pack_kernel, (vmem(edges + MB * done.shape[1]),), rims, done)
    aside = lax.ppermute(aside, "section", swap)
    spots = [(j, 0, bits) for j, bits in enumerate((0, 2, 3, 4, 6))]
    weight = join_call(lats, spots, (mine, two, three, four, six))
    spots = [(0, j, bits) for j, bits in enumerate((1, 5, 7))]
    weight = join_call(lats, spots, (one,), (weight,))
    return weight, rims, aside


def grad_kernel(lats, main_ref, near_ref, far_ref, grad_ref):
    rows = main_ref.shape[1]
    edge = HALO * BLK
    me = lax.axis_index("lat")
    odd = me % 2 == 1
    behind = far_ref.shape[0] > MB * edge
    finished = jnp.logical_and(lax.axis_index("section") % 2 == 1, behind)
    for m in range(MB):
        near = near_ref[m * edge : (m + 1) * edge, :].astype(F32)
        far = far_ref[m * edge : (m + 1) * edge, :].astype(F32)
        below = jnp.where(me > 0, jnp.where(odd, near, far), 0.0)
        above = jnp.where(me < lats - 1, jnp.where(odd, far, near), 0.0)
        low = (main_ref[m, :edge, :].astype(F32) + below).astype(BF)
        high = (main_ref[m, rows - edge :, :].astype(F32) + above).astype(BF)
        if behind:
            at = (MB + 2 * m) * edge
            low = jnp.where(finished, far_ref[at : at + edge, :], low)
            high = jnp.where(finished, far_ref[at + edge : at + 2 * edge, :], high)
        grad_ref[0, m, :edge, :] = low
        grad_ref[0, m, edge : rows - edge, :] = main_ref[m, edge : rows - edge, :]
        grad_ref[0, m, rows - edge :, :] = high


def grad_call(lats, main, near, far):
    return pl.pallas_call(
        functools.partial(grad_kernel, lats),
        out_shape=jax.ShapeDtypeStruct((1,) + main.shape, BF),
        in_specs=[VM] * 3,
        out_specs=VM,
        compiler_params=params(),
        name="grad",
    )(main, near, far)


def per_device(saved_input, cotangent, quad_values, block_index, block_mask, weights):
    sections = lax.axis_size("section")
    lats = lax.axis_size("lat")
    edge = HALO * BLK
    rows = saved_input.shape[2]
    both = ("lat", "section")
    odd = lax.axis_index("lat") % 2
    sides = [near_pairs(lats, sections, side) for side in range(2)]

    def rim(high):
        return lax.dynamic_slice_in_dim(saved_input[0], high * (rows - edge), edge, axis=1)

    far = lax.ppermute(rim(odd), both, sides[1])
    near = lax.ppermute(rim(1 - odd), both, sides[0])
    band, flip = band_call(block_index, block_mask, quad_values)
    hid, gp = hidden_call(saved_input, band, weights)
    hid, gp = hidden_call(saved_input, band, weights, near, far, hid, gp)

    state, grads = {"gp": gp}, (cotangent,)

    def send(array, pairs, axis=both):
        return lax.ppermute(array, axis, pairs)

    for turn in reversed(range(sections)):
        if turn == 0:
            step_call(turn, lats, "slope", grads, flip, weights, state)
            step_call(turn, lats, "tips", grads, flip, weights, state)
            step_call(turn, lats, "bulk", grads, flip, weights, state)
            continue
        if turn % 2:
            step_call(turn, lats, "edge", grads, flip, weights, state)
            step_call(turn, lats, "bulk", grads, flip, weights, state)
            sent = {"main": state["out"]}
        else:
            step_call(turn, lats, "head", grads, flip, weights, state)
            step_call(turn, lats, "tail", grads, flip, weights, state)
            sent = {"main0": state["sent0"], "main1": state["sent1"]}
        hop = hop_pairs(sections, turn)
        grads = tuple(send(array, hop, "section") for array in sent.values())
        low = send(state["right"], slant_pairs(lats, sections, turn, True))
        high = send(state["left"], slant_pairs(lats, sections, turn, False))
        grads += (low, high)

    left, right, slope = (state[name] for name in PARTS["edge"])
    channels = saved_input.shape[3]
    if lats == 8 and sections % 2 == 0:
        weight, near, far = reduce_weight(lats, sections, hid, state)
        grad = grad_call(lats, state["out"], near, far)
    else:
        give = jnp.where(odd == 1, left, right), jnp.where(odd == 1, right, left)
        near, far = (lax.ppermute(g, both, p).reshape(-1, channels) for g, p in zip(give, sides))
        weight = lax.psum(weight_call(hid, slope), "lat")
        grad = grad_call(lats, state["out"], near, far)
    return grad, weight.reshape(1, KB, channels, channels)


def solution(mesh):
    in_specs = (
        P("section", None, "lat", None),
        P(None, "lat", None),
        P(None, "lat", None, None, None),
        P("lat", None),
        P("lat", None),
        P("section", None, None, None),
    )
    out_specs = (P("section", None, "lat", None), P("section", None, None, None))
    return jax.shard_map(
        per_device, mesh=mesh, in_specs=in_specs, out_specs=out_specs, check_vma=False
    )
```

```python
import functools

import jax
import jax.numpy as jnp
from jax import lax
from jax.experimental import pallas as pl
from jax.experimental.pallas import tpu as pltpu
from jax.sharding import PartitionSpec as P


KB = 3
BLK = 64
HALO = 2
MB = 2
GRP = 4
SPAN = GRP + 2 * HALO
BF = jnp.bfloat16
F32 = jnp.float32
VM = pl.BlockSpec(memory_space=pltpu.VMEM)
ANY = pl.BlockSpec(memory_space=pl.ANY)
HB = pl.BlockSpec(memory_space=pltpu.HBM)


def gelu_slope(value):
    return (
        0.5 * (1.0 + lax.erf(value * 0.7071067811865476))
        + value * jnp.exp(-0.5 * value * value) * 0.3989422804014327
    )


def params(mib=24):
    return pltpu.CompilerParams(vmem_limit_bytes=mib << 20)


def near_pairs(lats, sections, side):
    pairs = []
    for i in range(lats):
        j = i ^ 1 if side == 0 else (i + 1 if i % 2 else i - 1)
        for s in range(sections):
            other = j * sections + s if 0 <= j < lats else i * sections + (s ^ 1)
            pairs.append((i * sections + s, other))
    return pairs


def edge_pairs(lats, sections):
    both = [near_pairs(lats, sections, side) for side in range(2)]
    pairs = []
    for i in range(lats):
        for s in range(sections):
            here = i * sections + s
            if s % 2 and (i == 0 or i == lats - 1):
                pairs.append((here, i * sections + (s + 2) % sections))
            else:
                pairs.append((here, dict(both[s % 2])[here]))
    return pairs


def hop_pairs(sections, turn):
    if turn % 2:
        return [(s, s ^ 1) for s in range(sections)]
    return [(s, (s - 1) % sections) for s in range(sections)]


def slant_pairs(lats, sections, turn, upward):
    last, low = lats - 1, turn - 1
    ways = {(i, turn): (i + 1, low) for i in range(last)}
    if sections > 2:
        aside = (turn - 2) % sections if turn % 2 else turn + 1
        ways[last, turn] = (last, aside)
        ways.update({(i, aside): (i - 1, aside) for i in range(1, lats)})
        ways[0, aside] = (0, low)
        ways.update({(i, low): (i, turn) for i in range(lats)})
        for i in range(lats):
            for s in range(sections):
                ways.setdefault((i, s), (i ^ 1, s))
        assert len(set(ways.values())) == lats * sections
    if not upward:
        ways = {(last - i, s): (last - j, r) for (i, s), (j, r) in ways.items()}
    return [(i * sections + s, j * sections + r) for (i, s), (j, r) in ways.items()]


def cost(flops):
    return pl.CostEstimate(flops=flops, bytes_accessed=flops // 256, transcendentals=0)


def dot(a, b):
    return jnp.dot(a, b, preferred_element_type=F32)


def band_kernel(
    blocks, index_in, mask_in, quad_in, band_ref, flip_ref, index_ref, mask_ref, quad_ref, table_ref, sems
):
    first = lax.axis_index("lat") * blocks
    small = [
        pltpu.make_async_copy(index_in, index_ref, sems.at[KB]),
        pltpu.make_async_copy(mask_in, mask_ref, sems.at[KB + 1]),
    ]
    large = [pltpu.make_async_copy(quad_in.at[k], quad_ref.at[k], sems.at[k]) for k in range(KB)]
    for c in small + large:
        c.start()
    for c in small:
        c.wait()
    for b in range(blocks):
        for d in range(2 * HALO + 2):
            table_ref[b, d] = 0
        for j in range(index_ref.shape[1]):
            d = index_ref[b, j] - (first + b) + HALO
            table_ref[b, jnp.where(mask_ref[b, j] != 0, d, 2 * HALO + 1)] = j + 1
    empty = jnp.zeros((BLK, BLK), BF)
    for k in range(KB):
        large[k].wait()
        for b in range(blocks):
            g, r = b // GRP, b % GRP
            tiles = [empty] * r
            for d in range(2 * HALO + 1):
                entry = table_ref[b, d]
                tile = quad_ref[k, b, jnp.maximum(entry - 1, 0)]
                tiles.append(jnp.where(entry > 0, tile, empty))
            tiles += [empty] * (GRP - 1 - r)
            half, rest = divmod(r * BLK, HALO * BLK)
            row = (half * KB + k) * HALO * BLK + rest
            band_ref[g, row : row + BLK, :] = jnp.concatenate(tiles, axis=1)
            if rest + BLK == HALO * BLK:
                part = slice(row - rest, row + BLK)
                flip_ref[g, :, part] = band_ref[g, part, :].T


def band_call(block_index, block_mask, quad):
    blocks = quad.shape[1]
    groups = blocks // GRP
    return pl.pallas_call(
        functools.partial(band_kernel, blocks),
        out_shape=(
            pltpu.VMEM((groups, KB * GRP * BLK, SPAN * BLK), BF),
            pltpu.VMEM((groups, SPAN * BLK, KB * GRP * BLK), BF),
        ),
        in_specs=[HB] * 3,
        out_specs=(VM, VM),
        scratch_shapes=[
            pltpu.SMEM(block_index.shape, jnp.int32),
            pltpu.SMEM(block_mask.shape, jnp.int32),
            pltpu.VMEM(quad.shape, BF),
            pltpu.SMEM((blocks, 2 * HALO + 2), jnp.int32),
            pltpu.SemaphoreType.DMA((KB + 2,)),
        ],
        compiler_params=params(),
        name="band",
    )(*(pltpu.with_memory_space_constraint(a, pltpu.HBM) for a in (block_index, block_mask, quad)))


def hidden_kernel(part, x_ref, band_ref, w_ref, *refs):
    hid_ref, gp_ref = refs[-2:]
    pair = HALO * BLK
    deep = KB * pair
    groups = band_ref.shape[0]
    spots = [(g, h) for g in range(groups) for h in range(2)]

    def fill(spots):
        parts = []
        for m in range(MB):
            for g, h in spots:
                at = (2 * g + h - 1) * pair
                if part == "inner":
                    window = x_ref[0, m, at : at + 3 * pair, :]
                elif g == 0:
                    window = jnp.concatenate([refs[0][m], x_ref[0, m, : 2 * pair, :]], axis=0)
                else:
                    window = jnp.concatenate([x_ref[0, m, at:, :], refs[0][m]], axis=0)
                band = band_ref[g, h * deep : (h + 1) * deep, h * pair : h * pair + 3 * pair]
                parts.append(dot(band, window).astype(BF))
                hid_ref[m, g, h * deep : (h + 1) * deep, :] = parts[-1]
        z = None
        for k in range(KB):
            rows = jnp.concatenate([p[k * pair : (k + 1) * pair] for p in parts], axis=0)
            new = dot(rows, w_ref[0, k])
            z = new if z is None else z + new
        gp = gelu_slope(z)
        for i, (m, g, h) in enumerate((m, g, h) for m in range(MB) for g, h in spots):
            gp_ref[m, (2 * g + h) * pair : (2 * g + h + 1) * pair, :] = gp[i * pair : (i + 1) * pair]

    if part == "inner":
        fill(spots[1:-1])
        return
    below = (lax.axis_index("lat") % 2 == 0) == (part == "far")
    pl.when(below)(lambda: fill(spots[:1]))
    pl.when(jnp.logical_not(below))(lambda: fill(spots[-1:]))


def hidden_call(part, x, band, weights, *rest):
    _, mb, rows, ch = x.shape
    args = (x, band, weights) + rest
    return pl.pallas_call(
        functools.partial(hidden_kernel, part),
        out_shape=(
            pltpu.VMEM((mb, band.shape[0], KB * GRP * BLK, ch), BF),
            pltpu.VMEM((mb, rows, ch), F32),
        ),
        in_specs=[VM] * len(args),
        out_specs=(VM, VM),
        input_output_aliases={4: 0, 5: 1} if rest else {},
        compiler_params=params(),
        cost_estimate=None if rest else cost(1 << 30),
    )(*args)


def rim_kernel(x_ref, far_ref, near_ref, sems):
    rows, edge = x_ref.shape[2], far_ref.shape[1]
    odd = lax.axis_index("lat") % 2
    copies = []
    for i, (high, ref) in enumerate(((odd, far_ref), (1 - odd, near_ref))):
        at = pl.multiple_of(high * (rows - edge), edge)
        copies.append(pltpu.make_async_copy(x_ref.at[0, :, pl.ds(at, edge)], ref, sems.at[i]))
        copies[-1].start()
    for c in copies:
        c.wait()


def rim_call(x):
    _, mb, _, ch = x.shape
    return pl.pallas_call(
        rim_kernel,
        out_shape=(pltpu.VMEM((mb, HALO * BLK, ch), BF),) * 2,
        in_specs=[HB],
        out_specs=(VM, VM),
        scratch_shapes=[pltpu.SemaphoreType.DMA((2,))],
        compiler_params=params(),
        name="rim",
    )(pltpu.with_memory_space_constraint(x, pltpu.HBM))


PARTS = {
    "edge": ("left", "right", "slope"),
    "slope": ("slope", "done"),
    "tips": ("left", "right"),
    "bulk": ("out",),
    "head": ("slope", "done", "out", "sent0"),
    "tail": ("left", "right", "slope", "done", "out", "sent1"),
}
MICROS = {"head": (0,), "tail": (1,)}


def back_terms(slope, w_ref, stack_ref):
    pair = HALO * BLK
    for k in range(KB):
        back = lax.dot_general(
            slope, w_ref[0, k], (((1,), (1,)), ((), ())), preferred_element_type=F32
        ).astype(BF)
        for h in range(slope.shape[0] // pair):
            stack_ref[(h * KB + k) * pair : (h * KB + k + 1) * pair, :] = back[h * pair : (h + 1) * pair]


def step_kernel(turn, lats, part, form, *refs):
    outs, (stack_ref, term_ref) = dict(zip(PARTS[part], refs[-2 - len(PARTS[part]) :])), refs[-2:]
    (gp_ref, flip_ref, w_ref), rest = refs[:3], refs[3:]
    lat = lax.axis_index("lat")
    rows = gp_ref.shape[1]
    size = GRP * BLK
    edge = HALO * BLK
    lap = 2 * edge
    groups = rows // size

    micros = MICROS.get(part, range(MB))
    slope_ref = outs.get("slope", gp_ref)

    def grad_of(m, g):
        at = slice(g * size, (g + 1) * size)
        grad = (rest[m][at, :] if form == "micro" else rest[0][m, at, :]).astype(F32)
        if form == "whole":
            return grad
        below_ref, above_ref = rest[MB : MB + 2] if form == "micro" else rest[1:3]
        parts = [grad[i * edge : (i + 1) * edge] for i in range(size // edge)]
        if g == 0:
            parts[0] += jnp.where(lat > 0, below_ref[m].astype(F32), 0.0)
        if g == groups - 1:
            parts[-1] += jnp.where(lat < lats - 1, above_ref[m].astype(F32), 0.0)
        return jnp.concatenate(parts, axis=0).astype(BF).astype(F32)

    def tips():
        rims = [slope_ref[m, at : at + edge, :] for m in range(MB) for at in (0, rows - edge)]
        back_terms(jnp.concatenate(rims, axis=0), w_ref, stack_ref)
        deep = KB * edge
        for m in range(MB):
            low = stack_ref[2 * m * deep : (2 * m + 1) * deep, :]
            outs["left"][m] = dot(flip_ref[0, :edge, :deep], low).astype(BF)
            high = stack_ref[(2 * m + 1) * deep : (2 * m + 2) * deep, :]
            outs["right"][m] = dot(flip_ref[groups - 1, size + edge :, deep:], high).astype(BF)

    def slopes():
        for m in micros:
            for g in range(groups):
                grad = grad_of(m, g)
                at = slice(g * size, (g + 1) * size)
                outs["slope"][m, at, :] = (grad * gp_ref[m, at, :]).astype(BF)
                if "done" in outs and g == 0:
                    outs["done"][m, :edge, :] = grad[:edge].astype(BF)
                if "done" in outs and g == groups - 1:
                    outs["done"][m, edge:, :] = grad[size - edge :].astype(BF)

    def terms(m):
        for g in range(groups):
            grad = grad_of(m, g)
            back_terms(slope_ref[m, g * size : (g + 1) * size, :], w_ref, stack_ref)
            term = dot(flip_ref[g], stack_ref[: KB * size, :])
            low = g * size
            if g == 0:
                term_ref[low + edge : low + lap, :] = term[edge:lap] + grad[: lap - edge]
            else:
                term_ref[low : low + lap, :] += term[:lap]
                term_ref[low + edge : low + lap, :] += grad[: lap - edge]
            term_ref[low + lap : low + size + edge, :] = term[lap : size + edge] + grad[lap - edge :]
            if g < groups - 1:
                term_ref[low + size + edge : low + size + lap, :] = term[size + edge :]
        out = term_ref[edge : edge + rows, :].astype(BF)
        outs["out"][m] = out
        if part in MICROS:
            outs[f"sent{m}"][...] = out

    @pl.when(lax.axis_index("section") == turn)
    def _():
        if "slope" in outs:
            slopes()
        if "out" in outs:
            for m in micros:
                terms(m)
        if "left" in outs:
            tips()


def step_call(turn, lats, part, grads, flip, weights, state):
    mb, rows, ch = state["gp"].shape
    edge = HALO * BLK
    names = PARTS[part]
    known = [name for name in names if name in state]
    form = {1: "whole", 3: "summed", 4: "micro"}[len(grads)]
    factor = state["gp" if "slope" in names else "slope"]
    args = (factor, flip, weights) + grads + tuple(state[name] for name in known)
    tall = {"left": edge, "right": edge, "done": 2 * edge}
    shapes = {name: (mb, tall.get(name, rows), ch) for name in names}
    shapes.update({name: (rows, ch) for name in names if name.startswith("sent")})
    outs = pl.pallas_call(
        functools.partial(step_kernel, turn, lats, part, form),
        out_shape=tuple(pltpu.VMEM(shapes[name], BF) for name in names),
        in_specs=[VM] * len(args),
        out_specs=(VM,) * len(names),
        input_output_aliases={
            len(args) - len(known) + i: names.index(name) for i, name in enumerate(known)
        },
        scratch_shapes=[
            pltpu.VMEM((KB * max(GRP * BLK, 2 * MB * edge), ch), BF),
            pltpu.VMEM((rows + 2 * edge, ch), F32),
        ],
        compiler_params=params(),
    )(*args)
    state.update(zip(names, outs))


def weight_terms(hid_ref, slope_ref, acc_ref):
    size = GRP * BLK
    edge = HALO * BLK
    for k in range(KB):
        total = None
        for m in range(MB):
            for g in range(hid_ref.shape[1]):
                pairs = [hid_ref[m, g, i * edge : (i + 1) * edge, :] for i in (k, KB + k)]
                part = lax.dot_general(
                    jnp.concatenate(pairs, axis=0),
                    slope_ref[m, g * size : (g + 1) * size, :],
                    (((0,), (0,)), ((), ())),
                    preferred_element_type=F32,
                )
                total = part if total is None else total + part
        acc_ref[k * total.shape[0] : (k + 1) * total.shape[0], :] = total


def weight_call(hid, slope):
    ch = slope.shape[2]
    return pl.pallas_call(
        weight_terms,
        out_shape=pltpu.VMEM((KB * ch, ch), F32),
        in_specs=[VM] * 2,
        out_specs=VM,
        compiler_params=params(),
        name="weight",
    )(hid, slope)


def lay_edges(even_ref, odd_ref):
    odd = lax.axis_index("lat") % 2 == 1
    return jnp.concatenate([jnp.where(odd, odd_ref[m], even_ref[m]) for m in range(MB)], axis=0)


def cut_kernel(hid_ref, slope_ref, own_ref, one_ref, pair_ref, two_ref, three_ref, far_ref, acc_ref):
    weight_terms(hid_ref, slope_ref, acc_ref)
    me = lax.axis_index("lat")
    piece = own_ref.shape[0]

    def cut(bits):
        return acc_ref[pl.ds(pl.multiple_of((me ^ bits) * piece, piece), piece), :]

    own_ref[...] = cut(0)
    one_ref[...] = cut(1).astype(BF)
    for j, bits in enumerate((5, 7)):
        pair_ref[j * piece : (j + 1) * piece, :] = cut(bits).astype(BF)
    two_ref[...] = cut(2).astype(BF)
    three_ref[...] = cut(3).astype(BF)
    far_ref[:piece, :] = cut(4)
    far_ref[piece:, :] = cut(6)


def middle_kernel(far_ref, pair_ref, four_ref, six_ref):
    piece = four_ref.shape[0]
    four_ref[...] = (far_ref[:piece, :] + pair_ref[:piece, :].astype(F32)).astype(BF)
    six_ref[...] = (far_ref[piece:, :] + pair_ref[piece:, :].astype(F32)).astype(BF)


def give_kernel(left_ref, right_ref, out_ref):
    out_ref[...] = lay_edges(left_ref, right_ref)


def sum_kernel(own_ref, *refs):
    total = own_ref[...]
    for ref in refs[:-1]:
        total += ref[: total.shape[0], :].astype(F32)
    refs[-1][...] = total.astype(BF)


def pack_kernel(*refs):
    at = 0
    for ref in refs[:-1]:
        for value in [ref[...]] if len(ref.shape) == 2 else [ref[m] for m in range(ref.shape[0])]:
            refs[-1][at : at + value.shape[0], :] = value
            at += value.shape[0]


def rims_kernel(got_ref, left_ref, right_ref, out_ref):
    second = lax.axis_index("section") % 2 == 1
    out_ref[...] = jnp.where(second, got_ref[...], lay_edges(right_ref, left_ref))


def join_kernel(spots, piece, *refs):
    refs, (weight_ref, wide_ref, sems) = refs[: len(set(s[0] for s in spots))], refs[-3:]
    me = lax.axis_index("lat")
    copies = []
    for j, (source, part, bits) in enumerate(spots):
        wide_ref[j] = refs[source][part * piece : (part + 1) * piece, :].astype(F32)
        at = pl.multiple_of((me ^ bits) * piece, piece)
        copies.append(pltpu.make_async_copy(wide_ref.at[j], weight_ref.at[pl.ds(at, piece)], sems.at[j]))
        copies[-1].start()
    for c in copies:
        c.wait()


def join_call(lats, spots, sources, old=()):
    ch = sources[0].shape[1]
    piece = KB * ch // lats
    return pl.pallas_call(
        functools.partial(join_kernel, spots, piece),
        out_shape=jax.ShapeDtypeStruct((KB * ch, ch), F32),
        in_specs=[VM] * len(sources) + [ANY] * len(old),
        out_specs=ANY,
        input_output_aliases={len(sources): 0} if old else {},
        scratch_shapes=[
            pltpu.VMEM((len(spots), piece, ch), F32),
            pltpu.SemaphoreType.DMA((len(spots),)),
        ],
        compiler_params=params(),
    )(*sources, *old)


def small_call(kernel, shapes, *args, scratch=()):
    return pl.pallas_call(
        kernel,
        out_shape=tuple(shapes),
        in_specs=[VM] * len(args),
        out_specs=(VM,) * len(shapes),
        scratch_shapes=list(scratch),
        compiler_params=params(),
    )(*args)


def reduce_weight(lats, sections, hid, state):
    left, right, slope, done = (state[name] for name in ("left", "right", "slope", "done"))
    ch = slope.shape[2]
    piece = KB * ch // lats
    edges = MB * left.shape[1]
    swap = [(s, s ^ 1) for s in range(sections)]

    def vmem(rows, dtype=BF):
        return pltpu.VMEM((rows, ch), dtype)

    def meet(a, bits):
        return lax.ppermute(a, "lat", [(i, i ^ bits) for i in range(lats)])

    shapes = (vmem(piece, F32), vmem(piece), vmem(2 * piece), vmem(piece), vmem(piece), vmem(2 * piece, F32))
    own, one, pair, two, three, far = small_call(cut_kernel, shapes, hid, slope, scratch=(vmem(KB * ch, F32),))
    pair, two, three, one = meet(pair, 1), meet(two, 2), meet(three, 3), meet(one, 1)
    (give,) = small_call(give_kernel, (vmem(edges),), left, right)
    got = lax.ppermute(give, "section", swap)
    four, six = small_call(middle_kernel, (vmem(piece), vmem(piece)), far, pair)
    four, six = meet(four, 4), meet(six, 6)
    (rims,) = small_call(rims_kernel, (vmem(edges),), got, left, right)
    rims = lax.ppermute(rims, ("lat", "section"), edge_pairs(lats, sections))
    (mine,) = small_call(sum_kernel, (vmem(piece),), own, one, two, three, four, six)
    four, six = meet(mine, 4), meet(mine, 6)
    two, three = meet(mine, 2), meet(mine, 3)
    (one,) = small_call(pack_kernel, (vmem(3 * piece),), mine, four, six)
    one = meet(one, 1)
    (aside,) = small_call(pack_kernel, (vmem(edges + MB * done.shape[1]),), rims, done)
    aside = lax.ppermute(aside, "section", swap)
    spots = [(j, 0, bits) for j, bits in enumerate((0, 2, 3, 4, 6))]
    weight = join_call(lats, spots, (mine, two, three, four, six))
    spots = [(0, j, bits) for j, bits in enumerate((1, 5, 7))]
    weight = join_call(lats, spots, (one,), (weight,))
    return weight, rims, aside


def grad_kernel(lats, main_ref, near_ref, far_ref, grad_ref):
    rows = main_ref.shape[1]
    edge = HALO * BLK
    me = lax.axis_index("lat")
    odd = me % 2 == 1
    behind = far_ref.shape[0] > MB * edge
    finished = jnp.logical_and(lax.axis_index("section") % 2 == 1, behind)
    for m in range(MB):
        near = near_ref[m * edge : (m + 1) * edge, :].astype(F32)
        far = far_ref[m * edge : (m + 1) * edge, :].astype(F32)
        below = jnp.where(me > 0, jnp.where(odd, near, far), 0.0)
        above = jnp.where(me < lats - 1, jnp.where(odd, far, near), 0.0)
        low = (main_ref[m, :edge, :].astype(F32) + below).astype(BF)
        high = (main_ref[m, rows - edge :, :].astype(F32) + above).astype(BF)
        if behind:
            at = (MB + 2 * m) * edge
            low = jnp.where(finished, far_ref[at : at + edge, :], low)
            high = jnp.where(finished, far_ref[at + edge : at + 2 * edge, :], high)
        grad_ref[0, m, :edge, :] = low
        grad_ref[0, m, edge : rows - edge, :] = main_ref[m, edge : rows - edge, :]
        grad_ref[0, m, rows - edge :, :] = high


def grad_call(lats, main, near, far):
    return pl.pallas_call(
        functools.partial(grad_kernel, lats),
        out_shape=jax.ShapeDtypeStruct((1,) + main.shape, BF),
        in_specs=[VM] * 3,
        out_specs=VM,
        compiler_params=params(),
        name="grad",
    )(main, near, far)


def per_device(saved_input, cotangent, quad_values, block_index, block_mask, weights):
    sections = lax.axis_size("section")
    lats = lax.axis_size("lat")
    both = ("lat", "section")
    odd = lax.axis_index("lat") % 2
    sides = [near_pairs(lats, sections, side) for side in range(2)]

    far, near = rim_call(saved_input)
    far = lax.ppermute(far, both, sides[1])
    near = lax.ppermute(near, both, sides[0])
    band, flip = band_call(block_index, block_mask, quad_values)
    hid, gp = hidden_call("inner", saved_input, band, weights)
    hid, gp = hidden_call("far", saved_input, band, weights, far, hid, gp)
    hid, gp = hidden_call("near", saved_input, band, weights, near, hid, gp)

    state, grads = {"gp": gp}, (cotangent,)

    def send(array, pairs, axis=both):
        return lax.ppermute(array, axis, pairs)

    for turn in reversed(range(sections)):
        if turn == 0:
            step_call(turn, lats, "slope", grads, flip, weights, state)
            step_call(turn, lats, "tips", grads, flip, weights, state)
            step_call(turn, lats, "bulk", grads, flip, weights, state)
            continue
        if turn % 2:
            step_call(turn, lats, "edge", grads, flip, weights, state)
            step_call(turn, lats, "bulk", grads, flip, weights, state)
            sent = {"main": state["out"]}
        else:
            step_call(turn, lats, "head", grads, flip, weights, state)
            step_call(turn, lats, "tail", grads, flip, weights, state)
            sent = {"main0": state["sent0"], "main1": state["sent1"]}
        hop = hop_pairs(sections, turn)
        grads = tuple(send(array, hop, "section") for array in sent.values())
        low = send(state["right"], slant_pairs(lats, sections, turn, True))
        high = send(state["left"], slant_pairs(lats, sections, turn, False))
        grads += (low, high)

    left, right, slope = (state[name] for name in PARTS["edge"])
    channels = saved_input.shape[3]
    if lats == 8 and sections % 2 == 0:
        weight, near, far = reduce_weight(lats, sections, hid, state)
        grad = grad_call(lats, state["out"], near, far)
    else:
        give = jnp.where(odd == 1, left, right), jnp.where(odd == 1, right, left)
        near, far = (lax.ppermute(g, both, p).reshape(-1, channels) for g, p in zip(give, sides))
        weight = lax.psum(weight_call(hid, slope), "lat")
        grad = grad_call(lats, state["out"], near, far)
    return grad, weight.reshape(1, KB, channels, channels)


def solution(mesh):
    in_specs = (
        P("section", None, "lat", None),
        P(None, "lat", None),
        P(None, "lat", None, None, None),
        P("lat", None),
        P("lat", None),
        P("section", None, None, None),
    )
    out_specs = (P("section", None, "lat", None), P("section", None, None, None))
    return jax.shard_map(
        per_device, mesh=mesh, in_specs=in_specs, out_specs=out_specs, check_vma=False
    )
```

```python
import functools

import jax
import jax.numpy as jnp
from jax import lax
from jax.experimental import pallas as pl
from jax.experimental.pallas import tpu as pltpu
from jax.sharding import PartitionSpec as P


KB = 3
BLK = 64
HALO = 2
MB = 2
GRP = 4
SPAN = GRP + 2 * HALO
BF = jnp.bfloat16
F32 = jnp.float32
VM = pl.BlockSpec(memory_space=pltpu.VMEM)
ANY = pl.BlockSpec(memory_space=pl.ANY)
HB = pl.BlockSpec(memory_space=pltpu.HBM)


def gelu_slope(value):
    return (
        0.5 * (1.0 + lax.erf(value * 0.7071067811865476))
        + value * jnp.exp(-0.5 * value * value) * 0.3989422804014327
    )


def params(mib=24):
    return pltpu.CompilerParams(vmem_limit_bytes=mib << 20)


def near_pairs(lats, sections, side):
    pairs = []
    for i in range(lats):
        j = i ^ 1 if side == 0 else (i + 1 if i % 2 else i - 1)
        for s in range(sections):
            other = j * sections + s if 0 <= j < lats else i * sections + (s ^ 1)
            pairs.append((i * sections + s, other))
    return pairs


def edge_pairs(lats, sections):
    both = [near_pairs(lats, sections, side) for side in range(2)]
    pairs = []
    for i in range(lats):
        for s in range(sections):
            here = i * sections + s
            if s % 2 and (i == 0 or i == lats - 1):
                pairs.append((here, i * sections + (s + 2) % sections))
            else:
                pairs.append((here, dict(both[s % 2])[here]))
    return pairs


def hop_pairs(sections, turn):
    if turn % 2:
        return [(s, s ^ 1) for s in range(sections)]
    return [(s, (s - 1) % sections) for s in range(sections)]


def mate_pairs(lats, sections, turn, side):
    pairs = []
    for i in range(lats):
        j = i ^ 1 if side == 0 else (i + 1 if i % 2 else i - 1)
        inside = 0 <= j < lats
        if turn % 2:
            pairs += [(i * sections + s, i * sections + (s ^ 1)) for s in range(sections) if s != turn]
        if turn % 2 or inside:
            pairs.append((i * sections + turn, (j if inside else i) * sections + turn - 1))
    return pairs


def cost(flops):
    return pl.CostEstimate(flops=flops, bytes_accessed=flops // 256, transcendentals=0)


def dot(a, b):
    return jnp.dot(a, b, preferred_element_type=F32)


def band_kernel(
    blocks, index_in, mask_in, quad_in, band_ref, flip_ref, index_ref, mask_ref, quad_ref, table_ref, sems
):
    first = lax.axis_index("lat") * blocks
    small = [
        pltpu.make_async_copy(index_in, index_ref, sems.at[KB]),
        pltpu.make_async_copy(mask_in, mask_ref, sems.at[KB + 1]),
    ]
    large = [pltpu.make_async_copy(quad_in.at[k], quad_ref.at[k], sems.at[k]) for k in range(KB)]
    for c in small + large:
        c.start()
    for c in small:
        c.wait()
    for b in range(blocks):
        for d in range(2 * HALO + 2):
            table_ref[b, d] = 0
        for j in range(index_ref.shape[1]):
            d = index_ref[b, j] - (first + b) + HALO
            table_ref[b, jnp.where(mask_ref[b, j] != 0, d, 2 * HALO + 1)] = j + 1
    empty = jnp.zeros((BLK, BLK), BF)
    for k in range(KB):
        large[k].wait()
        for b in range(blocks):
            g, r = b // GRP, b % GRP
            tiles = [empty] * r
            for d in range(2 * HALO + 1):
                entry = table_ref[b, d]
                tile = quad_ref[k, b, jnp.maximum(entry - 1, 0)]
                tiles.append(jnp.where(entry > 0, tile, empty))
            tiles += [empty] * (GRP - 1 - r)
            half, rest = divmod(r * BLK, HALO * BLK)
            row = (half * KB + k) * HALO * BLK + rest
            band_ref[g, row : row + BLK, :] = jnp.concatenate(tiles, axis=1)
            if rest + BLK == HALO * BLK:
                part = slice(row - rest, row + BLK)
                flip_ref[g, :, part] = band_ref[g, part, :].T


def band_call(block_index, block_mask, quad):
    blocks = quad.shape[1]
    groups = blocks // GRP
    return pl.pallas_call(
        functools.partial(band_kernel, blocks),
        out_shape=(
            pltpu.VMEM((groups, KB * GRP * BLK, SPAN * BLK), BF),
            pltpu.VMEM((groups, SPAN * BLK, KB * GRP * BLK), BF),
        ),
        in_specs=[HB] * 3,
        out_specs=(VM, VM),
        scratch_shapes=[
            pltpu.SMEM(block_index.shape, jnp.int32),
            pltpu.SMEM(block_mask.shape, jnp.int32),
            pltpu.VMEM(quad.shape, BF),
            pltpu.SMEM((blocks, 2 * HALO + 2), jnp.int32),
            pltpu.SemaphoreType.DMA((KB + 2,)),
        ],
        compiler_params=params(),
        name="band",
    )(*(pltpu.with_memory_space_constraint(a, pltpu.HBM) for a in (block_index, block_mask, quad)))


def hidden_kernel(part, x_ref, band_ref, w_ref, *refs):
    hid_ref, gp_ref = refs[-2:]
    pair = HALO * BLK
    deep = KB * pair
    groups = band_ref.shape[0]
    spots = [(g, h) for g in range(groups) for h in range(2)]

    def fill(spots):
        parts = []
        for m in range(MB):
            for g, h in spots:
                at = (2 * g + h - 1) * pair
                if part == "inner":
                    window = x_ref[0, m, at : at + 3 * pair, :]
                elif g == 0:
                    window = jnp.concatenate([refs[0][m], x_ref[0, m, : 2 * pair, :]], axis=0)
                else:
                    window = jnp.concatenate([x_ref[0, m, at:, :], refs[0][m]], axis=0)
                band = band_ref[g, h * deep : (h + 1) * deep, h * pair : h * pair + 3 * pair]
                parts.append(dot(band, window).astype(BF))
                hid_ref[m, g, h * deep : (h + 1) * deep, :] = parts[-1]
        z = None
        for k in range(KB):
            rows = jnp.concatenate([p[k * pair : (k + 1) * pair] for p in parts], axis=0)
            new = dot(rows, w_ref[0, k])
            z = new if z is None else z + new
        gp = gelu_slope(z)
        for i, (m, g, h) in enumerate((m, g, h) for m in range(MB) for g, h in spots):
            gp_ref[m, (2 * g + h) * pair : (2 * g + h + 1) * pair, :] = gp[i * pair : (i + 1) * pair]

    if part == "inner":
        fill(spots[1:-1])
        return
    below = (lax.axis_index("lat") % 2 == 0) == (part == "far")
    pl.when(below)(lambda: fill(spots[:1]))
    pl.when(jnp.logical_not(below))(lambda: fill(spots[-1:]))


def hidden_call(part, x, band, weights, *rest):
    _, mb, rows, ch = x.shape
    args = (x, band, weights) + rest
    return pl.pallas_call(
        functools.partial(hidden_kernel, part),
        out_shape=(
            pltpu.VMEM((mb, band.shape[0], KB * GRP * BLK, ch), BF),
            pltpu.VMEM((mb, rows, ch), F32),
        ),
        in_specs=[VM] * len(args),
        out_specs=(VM, VM),
        input_output_aliases={4: 0, 5: 1} if rest else {},
        compiler_params=params(),
        cost_estimate=None if rest else cost(1 << 30),
    )(*args)


def rim_kernel(x_ref, far_ref, near_ref, sems):
    rows, edge = x_ref.shape[2], far_ref.shape[1]
    odd = lax.axis_index("lat") % 2
    copies = []
    for i, (high, ref) in enumerate(((odd, far_ref), (1 - odd, near_ref))):
        at = pl.multiple_of(high * (rows - edge), edge)
        copies.append(pltpu.make_async_copy(x_ref.at[0, :, pl.ds(at, edge)], ref, sems.at[i]))
        copies[-1].start()
    for c in copies:
        c.wait()


def rim_call(x):
    _, mb, _, ch = x.shape
    return pl.pallas_call(
        rim_kernel,
        out_shape=(pltpu.VMEM((mb, HALO * BLK, ch), BF),) * 2,
        in_specs=[HB],
        out_specs=(VM, VM),
        scratch_shapes=[pltpu.SemaphoreType.DMA((2,))],
        compiler_params=params(),
        name="rim",
    )(pltpu.with_memory_space_constraint(x, pltpu.HBM))


PARTS = {
    "far": ("far", "slope"),
    "near": ("near", "slope"),
    "edge": ("near", "far", "slope"),
    "slope": ("slope", "done"),
    "tips": ("near", "far"),
    "bulk": ("out",),
    "head": ("slope", "done", "out", "sent0"),
    "tail": ("near", "far", "slope", "done", "out", "sent1"),
}
MICROS = {"head": (0,), "tail": (1,)}


def back_terms(slope, w_ref, stack_ref):
    pair = HALO * BLK
    for k in range(KB):
        back = lax.dot_general(
            slope, w_ref[0, k], (((1,), (1,)), ((), ())), preferred_element_type=F32
        ).astype(BF)
        for h in range(slope.shape[0] // pair):
            stack_ref[(h * KB + k) * pair : (h * KB + k + 1) * pair, :] = back[h * pair : (h + 1) * pair]


def step_kernel(turn, lats, part, form, *refs):
    outs, (stack_ref, term_ref) = dict(zip(PARTS[part], refs[-2 - len(PARTS[part]) :])), refs[-2:]
    (gp_ref, flip_ref, w_ref), rest = refs[:3], refs[3:]
    lat = lax.axis_index("lat")
    odd = lat % 2 == 1
    rows = gp_ref.shape[1]
    size = GRP * BLK
    edge = HALO * BLK
    lap = 2 * edge
    groups = rows // size

    micros = MICROS.get(part, range(MB))
    slope_ref = outs.get("slope", gp_ref)

    def grad_of(m, g):
        at = slice(g * size, (g + 1) * size)
        grad = (rest[m][at, :] if form == "micro" else rest[0][m, at, :]).astype(F32)
        if form == "whole":
            return grad
        near_ref, far_ref = rest[MB : MB + 2] if form == "micro" else rest[1:3]
        parts = [grad[i * edge : (i + 1) * edge] for i in range(size // edge)]
        if g == 0:
            below = jnp.where(odd, near_ref[m], far_ref[m]).astype(F32)
            parts[0] += jnp.where(lat > 0, below, 0.0)
        if g == groups - 1:
            above = jnp.where(odd, far_ref[m], near_ref[m]).astype(F32)
            parts[-1] += jnp.where(lat < lats - 1, above, 0.0)
        return jnp.concatenate(parts, axis=0).astype(BF).astype(F32)

    def tips(names):
        deep = KB * edge
        sides = [(name, above) for name, above in zip(names, (False, True)) if name]
        rims = [slope_ref[m, (rows - edge) * up : (rows - edge) * up + edge, :] for m in range(MB) for _, up in sides]
        back_terms(jnp.concatenate(rims, axis=0), w_ref, stack_ref)
        for m in range(MB):
            for i, (name, above) in enumerate(sides):
                at = (m * len(sides) + i) * deep
                band = flip_ref[groups - 1, size + edge :, deep:] if above else flip_ref[0, :edge, :deep]
                outs[name][m] = dot(band, stack_ref[at : at + deep, :]).astype(BF)

    def half(even_part):
        above = not even_part if part == "far" else even_part
        for m in range(MB):
            mine = slice(rows - edge, rows) if above else slice(0, edge)
            others = slice(edge, rows) if above else slice(0, rows - edge)
            at = mine if part == "far" else others
            grad = rest[0][m, at, :].astype(F32)
            outs["slope"][m, at, :] = (grad * gp_ref[m, at, :]).astype(BF)
        tips((None, part) if above else (part, None))

    def slopes():
        for m in micros:
            for g in range(groups):
                grad = grad_of(m, g)
                at = slice(g * size, (g + 1) * size)
                outs["slope"][m, at, :] = (grad * gp_ref[m, at, :]).astype(BF)
                if "done" in outs and g == 0:
                    outs["done"][m, :edge, :] = grad[:edge].astype(BF)
                if "done" in outs and g == groups - 1:
                    outs["done"][m, edge:, :] = grad[size - edge :].astype(BF)

    def terms(m):
        for g in range(groups):
            grad = grad_of(m, g)
            back_terms(slope_ref[m, g * size : (g + 1) * size, :], w_ref, stack_ref)
            term = dot(flip_ref[g], stack_ref[: KB * size, :])
            low = g * size
            if g == 0:
                term_ref[low + edge : low + lap, :] = term[edge:lap] + grad[: lap - edge]
            else:
                term_ref[low : low + lap, :] += term[:lap]
                term_ref[low + edge : low + lap, :] += grad[: lap - edge]
            term_ref[low + lap : low + size + edge, :] = term[lap : size + edge] + grad[lap - edge :]
            if g < groups - 1:
                term_ref[low + size + edge : low + size + lap, :] = term[size + edge :]
        out = term_ref[edge : edge + rows, :].astype(BF)
        outs["out"][m] = out
        if part in MICROS:
            outs[f"sent{m}"][...] = out

    @pl.when(lax.axis_index("section") == turn)
    def _():
        if part in ("far", "near"):
            pl.when(odd)(lambda: half(False))
            pl.when(jnp.logical_not(odd))(lambda: half(True))
            return
        if "slope" in outs:
            slopes()
        if "out" in outs:
            for m in micros:
                terms(m)
        if "near" in outs:
            pl.when(odd)(lambda: tips(("near", "far")))
            pl.when(jnp.logical_not(odd))(lambda: tips(("far", "near")))


def step_call(turn, lats, part, grads, flip, weights, state):
    mb, rows, ch = state["gp"].shape
    edge = HALO * BLK
    names = PARTS[part]
    known = [name for name in names if name in state]
    form = {1: "whole", 3: "summed", 4: "micro"}[len(grads)]
    factor = state["gp" if "slope" in names else "slope"]
    args = (factor, flip, weights) + grads + tuple(state[name] for name in known)
    tall = {"near": edge, "far": edge, "done": 2 * edge}
    shapes = {name: (mb, tall.get(name, rows), ch) for name in names}
    shapes.update({name: (rows, ch) for name in names if name.startswith("sent")})
    outs = pl.pallas_call(
        functools.partial(step_kernel, turn, lats, part, form),
        out_shape=tuple(pltpu.VMEM(shapes[name], BF) for name in names),
        in_specs=[VM] * len(args),
        out_specs=(VM,) * len(names),
        input_output_aliases={
            len(args) - len(known) + i: names.index(name) for i, name in enumerate(known)
        },
        scratch_shapes=[
            pltpu.VMEM((KB * max(GRP * BLK, 2 * MB * edge), ch), BF),
            pltpu.VMEM((rows + 2 * edge, ch), F32),
        ],
        compiler_params=params(),
    )(*args)
    state.update(zip(names, outs))


def weight_terms(hid_ref, slope_ref, acc_ref):
    size = GRP * BLK
    edge = HALO * BLK
    for k in range(KB):
        total = None
        for m in range(MB):
            for g in range(hid_ref.shape[1]):
                pairs = [hid_ref[m, g, i * edge : (i + 1) * edge, :] for i in (k, KB + k)]
                part = lax.dot_general(
                    jnp.concatenate(pairs, axis=0),
                    slope_ref[m, g * size : (g + 1) * size, :],
                    (((0,), (0,)), ((), ())),
                    preferred_element_type=F32,
                )
                total = part if total is None else total + part
        acc_ref[k * total.shape[0] : (k + 1) * total.shape[0], :] = total


def weight_call(hid, slope):
    ch = slope.shape[2]
    return pl.pallas_call(
        weight_terms,
        out_shape=pltpu.VMEM((KB * ch, ch), F32),
        in_specs=[VM] * 2,
        out_specs=VM,
        compiler_params=params(),
        name="weight",
    )(hid, slope)


def cut_kernel(hid_ref, slope_ref, own_ref, one_ref, pair_ref, two_ref, three_ref, far_ref, acc_ref):
    weight_terms(hid_ref, slope_ref, acc_ref)
    me = lax.axis_index("lat")
    piece = own_ref.shape[0]

    def cut(bits):
        return acc_ref[pl.ds(pl.multiple_of((me ^ bits) * piece, piece), piece), :]

    own_ref[...] = cut(0)
    one_ref[...] = cut(1).astype(BF)
    for j, bits in enumerate((5, 7)):
        pair_ref[j * piece : (j + 1) * piece, :] = cut(bits).astype(BF)
    two_ref[...] = cut(2).astype(BF)
    three_ref[...] = cut(3).astype(BF)
    far_ref[:piece, :] = cut(4)
    far_ref[piece:, :] = cut(6)


def middle_kernel(far_ref, pair_ref, four_ref, six_ref):
    piece = four_ref.shape[0]
    four_ref[...] = (far_ref[:piece, :] + pair_ref[:piece, :].astype(F32)).astype(BF)
    six_ref[...] = (far_ref[piece:, :] + pair_ref[piece:, :].astype(F32)).astype(BF)


def sum_kernel(own_ref, *refs):
    total = own_ref[...]
    for ref in refs[:-1]:
        total += ref[: total.shape[0], :].astype(F32)
    refs[-1][...] = total.astype(BF)


def pack_kernel(*refs):
    at = 0
    for ref in refs[:-1]:
        for value in [ref[...]] if len(ref.shape) == 2 else [ref[m] for m in range(ref.shape[0])]:
            refs[-1][at : at + value.shape[0], :] = value
            at += value.shape[0]


def rims_kernel(got_ref, near_ref, out_ref):
    second = lax.axis_index("section") % 2 == 1
    edge = near_ref.shape[1]
    for m in range(MB):
        out_ref[m * edge : (m + 1) * edge, :] = jnp.where(second, got_ref[m], near_ref[m])


def join_kernel(spots, piece, *refs):
    refs, (weight_ref, wide_ref, sems) = refs[: len(set(s[0] for s in spots))], refs[-3:]
    me = lax.axis_index("lat")
    copies = []
    for j, (source, part, bits) in enumerate(spots):
        wide_ref[j] = refs[source][part * piece : (part + 1) * piece, :].astype(F32)
        at = pl.multiple_of((me ^ bits) * piece, piece)
        copies.append(pltpu.make_async_copy(wide_ref.at[j], weight_ref.at[pl.ds(at, piece)], sems.at[j]))
        copies[-1].start()
    for c in copies:
        c.wait()


def join_call(lats, spots, sources, old=()):
    ch = sources[0].shape[1]
    piece = KB * ch // lats
    return pl.pallas_call(
        functools.partial(join_kernel, spots, piece),
        out_shape=jax.ShapeDtypeStruct((KB * ch, ch), F32),
        in_specs=[VM] * len(sources) + [ANY] * len(old),
        out_specs=ANY,
        input_output_aliases={len(sources): 0} if old else {},
        scratch_shapes=[
            pltpu.VMEM((len(spots), piece, ch), F32),
            pltpu.SemaphoreType.DMA((len(spots),)),
        ],
        compiler_params=params(),
    )(*sources, *old)


def small_call(kernel, shapes, *args, scratch=()):
    return pl.pallas_call(
        kernel,
        out_shape=tuple(shapes),
        in_specs=[VM] * len(args),
        out_specs=(VM,) * len(shapes),
        scratch_shapes=list(scratch),
        compiler_params=params(),
    )(*args)


def reduce_weight(lats, sections, hid, state):
    near, far, slope, done = (state[name] for name in ("near", "far", "slope", "done"))
    ch = slope.shape[2]
    piece = KB * ch // lats
    edges = MB * near.shape[1]
    swap = [(s, s ^ 1) for s in range(sections)]

    def vmem(rows, dtype=BF):
        return pltpu.VMEM((rows, ch), dtype)

    def meet(a, bits):
        return lax.ppermute(a, "lat", [(i, i ^ bits) for i in range(lats)])

    shapes = (vmem(piece, F32), vmem(piece), vmem(2 * piece), vmem(piece), vmem(piece), vmem(2 * piece, F32))
    own, one, pair, two, three, half = small_call(cut_kernel, shapes, hid, slope, scratch=(vmem(KB * ch, F32),))
    pair, two, three, one = meet(pair, 1), meet(two, 2), meet(three, 3), meet(one, 1)
    got = lax.ppermute(far, "section", swap)
    four, six = small_call(middle_kernel, (vmem(piece), vmem(piece)), half, pair)
    four, six = meet(four, 4), meet(six, 6)
    (rims,) = small_call(rims_kernel, (vmem(edges),), got, near)
    rims = lax.ppermute(rims, ("lat", "section"), edge_pairs(lats, sections))
    (mine,) = small_call(sum_kernel, (vmem(piece),), own, one, two, three, four, six)
    four, six = meet(mine, 4), meet(mine, 6)
    two, three = meet(mine, 2), meet(mine, 3)
    (one,) = small_call(pack_kernel, (vmem(3 * piece),), mine, four, six)
    one = meet(one, 1)
    (aside,) = small_call(pack_kernel, (vmem(edges + MB * done.shape[1]),), rims, done)
    aside = lax.ppermute(aside, "section", swap)
    spots = [(j, 0, bits) for j, bits in enumerate((0, 2, 3, 4, 6))]
    weight = join_call(lats, spots, (mine, two, three, four, six))
    spots = [(0, j, bits) for j, bits in enumerate((1, 5, 7))]
    weight = join_call(lats, spots, (one,), (weight,))
    return weight, rims, aside


def grad_kernel(lats, main_ref, near_ref, far_ref, grad_ref):
    rows = main_ref.shape[1]
    edge = HALO * BLK
    me = lax.axis_index("lat")
    odd = me % 2 == 1
    behind = far_ref.shape[0] > MB * edge
    finished = jnp.logical_and(lax.axis_index("section") % 2 == 1, behind)
    for m in range(MB):
        near = near_ref[m * edge : (m + 1) * edge, :].astype(F32)
        far = far_ref[m * edge : (m + 1) * edge, :].astype(F32)
        below = jnp.where(me > 0, jnp.where(odd, near, far), 0.0)
        above = jnp.where(me < lats - 1, jnp.where(odd, far, near), 0.0)
        low = (main_ref[m, :edge, :].astype(F32) + below).astype(BF)
        high = (main_ref[m, rows - edge :, :].astype(F32) + above).astype(BF)
        if behind:
            at = (MB + 2 * m) * edge
            low = jnp.where(finished, far_ref[at : at + edge, :], low)
            high = jnp.where(finished, far_ref[at + edge : at + 2 * edge, :], high)
        grad_ref[0, m, :edge, :] = low
        grad_ref[0, m, edge : rows - edge, :] = main_ref[m, edge : rows - edge, :]
        grad_ref[0, m, rows - edge :, :] = high


def grad_call(lats, main, near, far):
    return pl.pallas_call(
        functools.partial(grad_kernel, lats),
        out_shape=jax.ShapeDtypeStruct((1,) + main.shape, BF),
        in_specs=[VM] * 3,
        out_specs=VM,
        compiler_params=params(),
        name="grad",
    )(main, near, far)


def per_device(saved_input, cotangent, quad_values, block_index, block_mask, weights):
    sections = lax.axis_size("section")
    lats = lax.axis_size("lat")
    both = ("lat", "section")
    sides = [near_pairs(lats, sections, side) for side in range(2)]

    def send(array, pairs, axis=both):
        return lax.ppermute(array, axis, pairs)

    far, near = rim_call(saved_input)
    far = lax.ppermute(far, both, sides[1])
    near = lax.ppermute(near, both, sides[0])
    band, flip = band_call(block_index, block_mask, quad_values)
    hid, gp = hidden_call("inner", saved_input, band, weights)
    hid, gp = hidden_call("far", saved_input, band, weights, far, hid, gp)

    state, grads = {"gp": gp}, (cotangent,)
    for turn in reversed(range(sections)):
        if turn == sections - 1:
            step_call(turn, lats, "far", grads, flip, weights, state)
            hid, gp = hidden_call("near", saved_input, band, weights, near, hid, gp)
            state["gp"] = gp
            step_call(turn, lats, "near", grads, flip, weights, state)
        elif turn == 0:
            step_call(turn, lats, "slope", grads, flip, weights, state)
            step_call(turn, lats, "tips", grads, flip, weights, state)
        elif turn % 2:
            step_call(turn, lats, "edge", grads, flip, weights, state)
        if turn % 2 or turn == 0:
            step_call(turn, lats, "bulk", grads, flip, weights, state)
            sent = {"main": state["out"]}
        else:
            step_call(turn, lats, "head", grads, flip, weights, state)
            step_call(turn, lats, "tail", grads, flip, weights, state)
            sent = {"main0": state["sent0"], "main1": state["sent1"]}
        if turn > 0:
            hop = hop_pairs(sections, turn)
            grads = tuple(send(array, hop, "section") for array in sent.values())
            far = send(state["far"], mate_pairs(lats, sections, turn, 1))
            near = send(state["near"], mate_pairs(lats, sections, turn, 0))
            grads += (near, far)

    near, far, slope = (state[name] for name in PARTS["edge"])
    channels = saved_input.shape[3]
    if lats == 8 and sections % 2 == 0:
        weight, near, far = reduce_weight(lats, sections, hid, state)
        grad = grad_call(lats, state["out"], near, far)
    else:
        near, far = (
            lax.ppermute(a, both, p).reshape(-1, channels) for a, p in zip((near, far), sides)
        )
        weight = lax.psum(weight_call(hid, slope), "lat")
        grad = grad_call(lats, state["out"], near, far)
    return grad, weight.reshape(1, KB, channels, channels)


def solution(mesh):
    in_specs = (
        P("section", None, "lat", None),
        P(None, "lat", None),
        P(None, "lat", None, None, None),
        P("lat", None),
        P("lat", None),
        P("section", None, None, None),
    )
    out_specs = (P("section", None, "lat", None), P("section", None, None, None))
    return jax.shard_map(
        per_device, mesh=mesh, in_specs=in_specs, out_specs=out_specs, check_vma=False
    )
```

```python
import functools

import jax
import jax.numpy as jnp
from jax import lax
from jax.experimental import pallas as pl
from jax.experimental.pallas import tpu as pltpu
from jax.sharding import PartitionSpec as P


KB = 3
BLK = 64
HALO = 2
MB = 2
GRP = 4
SPAN = GRP + 2 * HALO
BF = jnp.bfloat16
F32 = jnp.float32
VM = pl.BlockSpec(memory_space=pltpu.VMEM)
ANY = pl.BlockSpec(memory_space=pl.ANY)
HB = pl.BlockSpec(memory_space=pltpu.HBM)


def gelu_slope(value):
    return (
        0.5 * (1.0 + lax.erf(value * 0.7071067811865476))
        + value * jnp.exp(-0.5 * value * value) * 0.3989422804014327
    )


def params(mib=24):
    return pltpu.CompilerParams(vmem_limit_bytes=mib << 20)


def near_pairs(lats, sections, side):
    pairs = []
    for i in range(lats):
        j = i ^ 1 if side == 0 else (i + 1 if i % 2 else i - 1)
        for s in range(sections):
            other = j * sections + s if 0 <= j < lats else i * sections + (s ^ 1)
            pairs.append((i * sections + s, other))
    return pairs


def edge_pairs(lats, sections):
    both = [near_pairs(lats, sections, side) for side in range(2)]
    pairs = []
    for i in range(lats):
        for s in range(sections):
            here = i * sections + s
            if s % 2 and (i == 0 or i == lats - 1):
                pairs.append((here, i * sections + (s + 2) % sections))
            else:
                pairs.append((here, dict(both[s % 2])[here]))
    return pairs


def hop_pairs(sections, turn):
    if turn % 2:
        return [(s, s ^ 1) for s in range(sections)]
    return [(s, (s - 1) % sections) for s in range(sections)]


def mate_pairs(lats, sections, turn, side):
    pairs = []
    for i in range(lats):
        j = i ^ 1 if side == 0 else (i + 1 if i % 2 else i - 1)
        inside = 0 <= j < lats
        if turn % 2:
            pairs += [(i * sections + s, i * sections + (s ^ 1)) for s in range(sections) if s != turn]
        if turn % 2 or inside:
            pairs.append((i * sections + turn, (j if inside else i) * sections + turn - 1))
    return pairs


def cost(flops):
    return pl.CostEstimate(flops=flops, bytes_accessed=flops // 256, transcendentals=0)


def dot(a, b):
    return jnp.dot(a, b, preferred_element_type=F32)


def band_kernel(
    blocks, index_in, mask_in, quad_in, band_ref, flip_ref, index_ref, mask_ref, quad_ref, table_ref, sems
):
    first = lax.axis_index("lat") * blocks
    small = [
        pltpu.make_async_copy(index_in, index_ref, sems.at[KB]),
        pltpu.make_async_copy(mask_in, mask_ref, sems.at[KB + 1]),
    ]
    large = [pltpu.make_async_copy(quad_in.at[k], quad_ref.at[k], sems.at[k]) for k in range(KB)]
    for c in small + large:
        c.start()
    for c in small:
        c.wait()
    for b in range(blocks):
        for d in range(2 * HALO + 2):
            table_ref[b, d] = 0
        for j in range(index_ref.shape[1]):
            d = index_ref[b, j] - (first + b) + HALO
            table_ref[b, jnp.where(mask_ref[b, j] != 0, d, 2 * HALO + 1)] = j + 1
    empty = jnp.zeros((BLK, BLK), BF)
    for k in range(KB):
        large[k].wait()
        for b in range(blocks):
            g, r = b // GRP, b % GRP
            tiles = [empty] * r
            for d in range(2 * HALO + 1):
                entry = table_ref[b, d]
                tile = quad_ref[k, b, jnp.maximum(entry - 1, 0)]
                tiles.append(jnp.where(entry > 0, tile, empty))
            tiles += [empty] * (GRP - 1 - r)
            half, rest = divmod(r * BLK, HALO * BLK)
            row = (half * KB + k) * HALO * BLK + rest
            band_ref[g, row : row + BLK, :] = jnp.concatenate(tiles, axis=1)
            if rest + BLK == HALO * BLK:
                part = slice(row - rest, row + BLK)
                flip_ref[g, :, part] = band_ref[g, part, :].T


def band_call(block_index, block_mask, quad):
    blocks = quad.shape[1]
    groups = blocks // GRP
    return pl.pallas_call(
        functools.partial(band_kernel, blocks),
        out_shape=(
            pltpu.VMEM((groups, KB * GRP * BLK, SPAN * BLK), BF),
            pltpu.VMEM((groups, SPAN * BLK, KB * GRP * BLK), BF),
        ),
        in_specs=[HB] * 3,
        out_specs=(VM, VM),
        scratch_shapes=[
            pltpu.SMEM(block_index.shape, jnp.int32),
            pltpu.SMEM(block_mask.shape, jnp.int32),
            pltpu.VMEM(quad.shape, BF),
            pltpu.SMEM((blocks, 2 * HALO + 2), jnp.int32),
            pltpu.SemaphoreType.DMA((KB + 2,)),
        ],
        compiler_params=params(),
        name="band",
    )(*(pltpu.with_memory_space_constraint(a, pltpu.HBM) for a in (block_index, block_mask, quad)))


def hidden_kernel(part, x_ref, band_ref, w_ref, *refs):
    hid_ref, gp_ref = refs[-2:]
    pair = HALO * BLK
    deep = KB * pair
    groups = band_ref.shape[0]
    spots = [(g, h) for g in range(groups) for h in range(2)]

    def fill(spots):
        parts = []
        for m in range(MB):
            for g, h in spots:
                at = (2 * g + h - 1) * pair
                if part == "inner":
                    window = x_ref[0, m, at : at + 3 * pair, :]
                elif g == 0:
                    window = jnp.concatenate([refs[0][m], x_ref[0, m, : 2 * pair, :]], axis=0)
                else:
                    window = jnp.concatenate([x_ref[0, m, at:, :], refs[0][m]], axis=0)
                band = band_ref[g, h * deep : (h + 1) * deep, h * pair : h * pair + 3 * pair]
                parts.append(dot(band, window).astype(BF))
                hid_ref[m, g, h * deep : (h + 1) * deep, :] = parts[-1]
        z = None
        for k in range(KB):
            rows = jnp.concatenate([p[k * pair : (k + 1) * pair] for p in parts], axis=0)
            new = dot(rows, w_ref[0, k])
            z = new if z is None else z + new
        gp = gelu_slope(z)
        for i, (m, g, h) in enumerate((m, g, h) for m in range(MB) for g, h in spots):
            gp_ref[m, (2 * g + h) * pair : (2 * g + h + 1) * pair, :] = gp[i * pair : (i + 1) * pair]

    if part == "inner":
        fill(spots[1:-1])
        return
    below = (lax.axis_index("lat") % 2 == 0) == (part == "far")
    pl.when(below)(lambda: fill(spots[:1]))
    pl.when(jnp.logical_not(below))(lambda: fill(spots[-1:]))


def hidden_call(part, x, band, weights, *rest):
    _, mb, rows, ch = x.shape
    args = (x, band, weights) + rest
    return pl.pallas_call(
        functools.partial(hidden_kernel, part),
        out_shape=(
            pltpu.VMEM((mb, band.shape[0], KB * GRP * BLK, ch), BF),
            pltpu.VMEM((mb, rows, ch), F32),
        ),
        in_specs=[VM] * len(args),
        out_specs=(VM, VM),
        input_output_aliases={4: 0, 5: 1} if rest else {},
        compiler_params=params(),
        cost_estimate=None if rest else cost(1 << 30),
    )(*args)


def rim_kernel(x_ref, far_ref, near_ref, sems):
    rows, edge = x_ref.shape[2], far_ref.shape[1]
    odd = lax.axis_index("lat") % 2
    copies = []
    for i, (high, ref) in enumerate(((odd, far_ref), (1 - odd, near_ref))):
        at = pl.multiple_of(high * (rows - edge), edge)
        copies.append(pltpu.make_async_copy(x_ref.at[0, :, pl.ds(at, edge)], ref, sems.at[i]))
        copies[-1].start()
    for c in copies:
        c.wait()


def rim_call(x):
    _, mb, _, ch = x.shape
    return pl.pallas_call(
        rim_kernel,
        out_shape=(pltpu.VMEM((mb, HALO * BLK, ch), BF),) * 2,
        in_specs=[HB],
        out_specs=(VM, VM),
        scratch_shapes=[pltpu.SemaphoreType.DMA((2,))],
        compiler_params=params(),
        name="rim",
    )(pltpu.with_memory_space_constraint(x, pltpu.HBM))


PARTS = {
    "far": ("far", "slope"),
    "near": ("near", "slope"),
    "edge": ("near", "far", "slope"),
    "slope": ("slope", "done"),
    "tips": ("near", "far"),
    "bulk": ("out",),
    "head": ("slope", "done", "out", "sent0"),
    "tail": ("near", "far", "slope", "done", "out", "sent1"),
}
MICROS = {"head": (0,), "tail": (1,)}


def back_terms(slope, w_ref, stack_ref):
    pair = HALO * BLK
    for k in range(KB):
        back = lax.dot_general(
            slope, w_ref[0, k], (((1,), (1,)), ((), ())), preferred_element_type=F32
        ).astype(BF)
        for h in range(slope.shape[0] // pair):
            stack_ref[(h * KB + k) * pair : (h * KB + k + 1) * pair, :] = back[h * pair : (h + 1) * pair]


def step_kernel(turn, lats, part, form, *refs):
    outs, stack_ref = dict(zip(PARTS[part], refs[-1 - len(PARTS[part]) :])), refs[-1]
    (gp_ref, flip_ref, w_ref), rest = refs[:3], refs[3:]
    lat = lax.axis_index("lat")
    odd = lat % 2 == 1
    rows = gp_ref.shape[1]
    size = GRP * BLK
    edge = HALO * BLK
    groups = rows // size

    micros = MICROS.get(part, range(MB))
    slope_ref = outs.get("slope", gp_ref)

    def grad_of(m, g):
        at = slice(g * size, (g + 1) * size)
        grad = (rest[m][at, :] if form == "micro" else rest[0][m, at, :]).astype(F32)
        if form == "whole":
            return grad
        near_ref, far_ref = rest[MB : MB + 2] if form == "micro" else rest[1:3]
        parts = [grad[i * edge : (i + 1) * edge] for i in range(size // edge)]
        if g == 0:
            below = jnp.where(odd, near_ref[m], far_ref[m]).astype(F32)
            parts[0] += jnp.where(lat > 0, below, 0.0)
        if g == groups - 1:
            above = jnp.where(odd, far_ref[m], near_ref[m]).astype(F32)
            parts[-1] += jnp.where(lat < lats - 1, above, 0.0)
        return jnp.concatenate(parts, axis=0).astype(BF).astype(F32)

    def tips(sides):
        deep = KB * edge
        rims = [slope_ref[m, (rows - edge) * up : (rows - edge) * up + edge, :] for m in range(MB) for up in sides]
        back_terms(jnp.concatenate(rims, axis=0), w_ref, stack_ref)
        found = []
        for i, up in enumerate(list(sides) * MB):
            band = flip_ref[groups - 1, size + edge :, deep:] if up else flip_ref[0, :edge, :deep]
            found.append(dot(band, stack_ref[i * deep : (i + 1) * deep, :]).astype(BF))
        return found

    def both_tips():
        found = tips((0, 1))
        for m in range(MB):
            below, above = found[2 * m : 2 * m + 2]
            outs["near"][m] = jnp.where(odd, below, above)
            outs["far"][m] = jnp.where(odd, above, below)

    def half(even_part):
        above = not even_part if part == "far" else even_part
        for m in range(MB):
            mine = slice(rows - edge, rows) if above else slice(0, edge)
            others = slice(edge, rows) if above else slice(0, rows - edge)
            at = mine if part == "far" else others
            grad = rest[0][m, at, :].astype(F32)
            outs["slope"][m, at, :] = (grad * gp_ref[m, at, :]).astype(BF)
        for m, found in enumerate(tips((int(above),))):
            outs[part][m] = found

    def slopes():
        for m in micros:
            for g in range(groups):
                grad = grad_of(m, g)
                at = slice(g * size, (g + 1) * size)
                outs["slope"][m, at, :] = (grad * gp_ref[m, at, :]).astype(BF)
                if "done" in outs and g == 0:
                    outs["done"][m, :edge, :] = grad[:edge].astype(BF)
                if "done" in outs and g == groups - 1:
                    outs["done"][m, edge:, :] = grad[size - edge :].astype(BF)

    def terms(m):
        deep = KB * size
        for g in range(groups):
            stack = stack_ref.at[pl.ds(g * deep, deep)]
            back_terms(slope_ref[m, g * size : (g + 1) * size, :], w_ref, stack)
        sums = [None] * (rows // edge)
        for g in range(groups):
            first = max(2 * g - 1, 0)
            last = min(2 * g + 3, len(sums))
            low = (first - (2 * g - 1)) * edge
            term = dot(flip_ref[g, low : low + (last - first) * edge, :], stack_ref[g * deep : (g + 1) * deep, :])
            for i in range(first, last):
                new = term[(i - first) * edge : (i - first + 1) * edge]
                sums[i] = new if sums[i] is None else sums[i] + new
        for i, value in enumerate(sums):
            at = slice(i * edge, (i + 1) * edge)
            grad = grad_of(m, i // 2)[(i % 2) * edge : (i % 2 + 1) * edge]
            out = (value + grad).astype(BF)
            outs["out"][m, at, :] = out
            if part in MICROS:
                outs[f"sent{m}"][at, :] = out

    @pl.when(lax.axis_index("section") == turn)
    def _():
        if part in ("far", "near"):
            pl.when(odd)(lambda: half(False))
            pl.when(jnp.logical_not(odd))(lambda: half(True))
            return
        if "slope" in outs:
            slopes()
        if "out" in outs:
            for m in micros:
                terms(m)
        if "near" in outs:
            both_tips()


def step_call(turn, lats, part, grads, flip, weights, state):
    mb, rows, ch = state["gp"].shape
    edge = HALO * BLK
    names = PARTS[part]
    known = [name for name in names if name in state]
    form = {1: "whole", 3: "summed", 4: "micro"}[len(grads)]
    factor = state["gp" if "slope" in names else "slope"]
    args = (factor, flip, weights) + grads + tuple(state[name] for name in known)
    tall = {"near": edge, "far": edge, "done": 2 * edge}
    shapes = {name: (mb, tall.get(name, rows), ch) for name in names}
    shapes.update({name: (rows, ch) for name in names if name.startswith("sent")})
    outs = pl.pallas_call(
        functools.partial(step_kernel, turn, lats, part, form),
        out_shape=tuple(pltpu.VMEM(shapes[name], BF) for name in names),
        in_specs=[VM] * len(args),
        out_specs=(VM,) * len(names),
        input_output_aliases={
            len(args) - len(known) + i: names.index(name) for i, name in enumerate(known)
        },
        scratch_shapes=[
            pltpu.VMEM((KB * max(rows, 2 * MB * edge), ch), BF),
        ],
        compiler_params=params(),
    )(*args)
    state.update(zip(names, outs))


def weight_terms(hid_ref, slope_ref, acc_ref):
    size = GRP * BLK
    edge = HALO * BLK
    for k in range(KB):
        total = None
        for m in range(MB):
            for g in range(hid_ref.shape[1]):
                pairs = [hid_ref[m, g, i * edge : (i + 1) * edge, :] for i in (k, KB + k)]
                part = lax.dot_general(
                    jnp.concatenate(pairs, axis=0),
                    slope_ref[m, g * size : (g + 1) * size, :],
                    (((0,), (0,)), ((), ())),
                    preferred_element_type=F32,
                )
                total = part if total is None else total + part
        acc_ref[k * total.shape[0] : (k + 1) * total.shape[0], :] = total


def weight_call(hid, slope):
    ch = slope.shape[2]
    return pl.pallas_call(
        weight_terms,
        out_shape=pltpu.VMEM((KB * ch, ch), F32),
        in_specs=[VM] * 2,
        out_specs=VM,
        compiler_params=params(),
        name="weight",
    )(hid, slope)


def cut_kernel(hid_ref, slope_ref, own_ref, one_ref, pair_ref, two_ref, three_ref, far_ref, acc_ref):
    weight_terms(hid_ref, slope_ref, acc_ref)
    me = lax.axis_index("lat")
    piece = own_ref.shape[0]

    def cut(bits):
        return acc_ref[pl.ds(pl.multiple_of((me ^ bits) * piece, piece), piece), :]

    own_ref[...] = cut(0)
    one_ref[...] = cut(1).astype(BF)
    for j, bits in enumerate((5, 7)):
        pair_ref[j * piece : (j + 1) * piece, :] = cut(bits).astype(BF)
    two_ref[...] = cut(2).astype(BF)
    three_ref[...] = cut(3).astype(BF)
    far_ref[:piece, :] = cut(4)
    far_ref[piece:, :] = cut(6)


def middle_kernel(far_ref, pair_ref, four_ref, six_ref):
    piece = four_ref.shape[0]
    four_ref[...] = (far_ref[:piece, :] + pair_ref[:piece, :].astype(F32)).astype(BF)
    six_ref[...] = (far_ref[piece:, :] + pair_ref[piece:, :].astype(F32)).astype(BF)


def sum_kernel(own_ref, *refs):
    total = own_ref[...]
    for ref in refs[:-1]:
        total += ref[: total.shape[0], :].astype(F32)
    refs[-1][...] = total.astype(BF)


def pack_kernel(*refs):
    at = 0
    for ref in refs[:-1]:
        for value in [ref[...]] if len(ref.shape) == 2 else [ref[m] for m in range(ref.shape[0])]:
            refs[-1][at : at + value.shape[0], :] = value
            at += value.shape[0]


def rims_kernel(got_ref, near_ref, out_ref):
    second = lax.axis_index("section") % 2 == 1
    edge = near_ref.shape[1]
    for m in range(MB):
        out_ref[m * edge : (m + 1) * edge, :] = jnp.where(second, got_ref[m], near_ref[m])


def join_kernel(spots, piece, *refs):
    refs, (weight_ref, wide_ref, sems) = refs[: len(set(s[0] for s in spots))], refs[-3:]
    me = lax.axis_index("lat")
    copies = []
    for j, (source, part, bits) in enumerate(spots):
        wide_ref[j] = refs[source][part * piece : (part + 1) * piece, :].astype(F32)
        at = pl.multiple_of((me ^ bits) * piece, piece)
        copies.append(pltpu.make_async_copy(wide_ref.at[j], weight_ref.at[pl.ds(at, piece)], sems.at[j]))
        copies[-1].start()
    for c in copies:
        c.wait()


def join_call(lats, spots, sources, old=()):
    ch = sources[0].shape[1]
    piece = KB * ch // lats
    return pl.pallas_call(
        functools.partial(join_kernel, spots, piece),
        out_shape=jax.ShapeDtypeStruct((KB * ch, ch), F32),
        in_specs=[VM] * len(sources) + [ANY] * len(old),
        out_specs=ANY,
        input_output_aliases={len(sources): 0} if old else {},
        scratch_shapes=[
            pltpu.VMEM((len(spots), piece, ch), F32),
            pltpu.SemaphoreType.DMA((len(spots),)),
        ],
        compiler_params=params(),
    )(*sources, *old)


def small_call(kernel, shapes, *args, scratch=()):
    return pl.pallas_call(
        kernel,
        out_shape=tuple(shapes),
        in_specs=[VM] * len(args),
        out_specs=(VM,) * len(shapes),
        scratch_shapes=list(scratch),
        compiler_params=params(),
    )(*args)


def reduce_weight(lats, sections, hid, state):
    near, far, slope, done = (state[name] for name in ("near", "far", "slope", "done"))
    ch = slope.shape[2]
    piece = KB * ch // lats
    edges = MB * near.shape[1]
    swap = [(s, s ^ 1) for s in range(sections)]

    def vmem(rows, dtype=BF):
        return pltpu.VMEM((rows, ch), dtype)

    def meet(a, bits):
        return lax.ppermute(a, "lat", [(i, i ^ bits) for i in range(lats)])

    shapes = (vmem(piece, F32), vmem(piece), vmem(2 * piece), vmem(piece), vmem(piece), vmem(2 * piece, F32))
    own, one, pair, two, three, half = small_call(cut_kernel, shapes, hid, slope, scratch=(vmem(KB * ch, F32),))
    pair, two, three, one = meet(pair, 1), meet(two, 2), meet(three, 3), meet(one, 1)
    got = lax.ppermute(far, "section", swap)
    four, six = small_call(middle_kernel, (vmem(piece), vmem(piece)), half, pair)
    four, six = meet(four, 4), meet(six, 6)
    (rims,) = small_call(rims_kernel, (vmem(edges),), got, near)
    rims = lax.ppermute(rims, ("lat", "section"), edge_pairs(lats, sections))
    (mine,) = small_call(sum_kernel, (vmem(piece),), own, one, two, three, four, six)
    four, six = meet(mine, 4), meet(mine, 6)
    two, three = meet(mine, 2), meet(mine, 3)
    (one,) = small_call(pack_kernel, (vmem(3 * piece),), mine, four, six)
    one = meet(one, 1)
    (aside,) = small_call(pack_kernel, (vmem(edges + MB * done.shape[1]),), rims, done)
    aside = lax.ppermute(aside, "section", swap)
    spots = [(j, 0, bits) for j, bits in enumerate((0, 2, 3, 4, 6))]
    weight = join_call(lats, spots, (mine, two, three, four, six))
    spots = [(0, j, bits) for j, bits in enumerate((1, 5, 7))]
    weight = join_call(lats, spots, (one,), (weight,))
    return weight, rims, aside


def grad_kernel(lats, main_ref, near_ref, far_ref, grad_ref):
    rows = main_ref.shape[1]
    edge = HALO * BLK
    me = lax.axis_index("lat")
    odd = me % 2 == 1
    behind = far_ref.shape[0] > MB * edge
    finished = jnp.logical_and(lax.axis_index("section") % 2 == 1, behind)
    for m in range(MB):
        near = near_ref[m * edge : (m + 1) * edge, :].astype(F32)
        far = far_ref[m * edge : (m + 1) * edge, :].astype(F32)
        below = jnp.where(me > 0, jnp.where(odd, near, far), 0.0)
        above = jnp.where(me < lats - 1, jnp.where(odd, far, near), 0.0)
        low = (main_ref[m, :edge, :].astype(F32) + below).astype(BF)
        high = (main_ref[m, rows - edge :, :].astype(F32) + above).astype(BF)
        if behind:
            at = (MB + 2 * m) * edge
            low = jnp.where(finished, far_ref[at : at + edge, :], low)
            high = jnp.where(finished, far_ref[at + edge : at + 2 * edge, :], high)
        grad_ref[0, m, :edge, :] = low
        grad_ref[0, m, edge : rows - edge, :] = main_ref[m, edge : rows - edge, :]
        grad_ref[0, m, rows - edge :, :] = high


def grad_call(lats, main, near, far):
    return pl.pallas_call(
        functools.partial(grad_kernel, lats),
        out_shape=jax.ShapeDtypeStruct((1,) + main.shape, BF),
        in_specs=[VM] * 3,
        out_specs=VM,
        compiler_params=params(),
        name="grad",
    )(main, near, far)


def per_device(saved_input, cotangent, quad_values, block_index, block_mask, weights):
    sections = lax.axis_size("section")
    lats = lax.axis_size("lat")
    both = ("lat", "section")
    sides = [near_pairs(lats, sections, side) for side in range(2)]

    def send(array, pairs, axis=both):
        return lax.ppermute(array, axis, pairs)

    far, near = rim_call(saved_input)
    far = lax.ppermute(far, both, sides[1])
    near = lax.ppermute(near, both, sides[0])
    band, flip = band_call(block_index, block_mask, quad_values)
    hid, gp = hidden_call("inner", saved_input, band, weights)
    hid, gp = hidden_call("far", saved_input, band, weights, far, hid, gp)

    state, grads = {"gp": gp}, (cotangent,)
    for turn in reversed(range(sections)):
        if turn == sections - 1:
            step_call(turn, lats, "far", grads, flip, weights, state)
            hid, gp = hidden_call("near", saved_input, band, weights, near, hid, gp)
            state["gp"] = gp
            step_call(turn, lats, "near", grads, flip, weights, state)
        elif turn == 0:
            step_call(turn, lats, "slope", grads, flip, weights, state)
            step_call(turn, lats, "tips", grads, flip, weights, state)
        elif turn % 2:
            step_call(turn, lats, "edge", grads, flip, weights, state)
        if turn % 2 or turn == 0:
            step_call(turn, lats, "bulk", grads, flip, weights, state)
            sent = {"main": state["out"]}
        else:
            step_call(turn, lats, "head", grads, flip, weights, state)
            step_call(turn, lats, "tail", grads, flip, weights, state)
            sent = {"main0": state["sent0"], "main1": state["sent1"]}
        if turn > 0:
            hop = hop_pairs(sections, turn)
            grads = tuple(send(array, hop, "section") for array in sent.values())
            far = send(state["far"], mate_pairs(lats, sections, turn, 1))
            near = send(state["near"], mate_pairs(lats, sections, turn, 0))
            grads += (near, far)

    near, far, slope = (state[name] for name in PARTS["edge"])
    channels = saved_input.shape[3]
    if lats == 8 and sections % 2 == 0:
        weight, near, far = reduce_weight(lats, sections, hid, state)
        grad = grad_call(lats, state["out"], near, far)
    else:
        near, far = (
            lax.ppermute(a, both, p).reshape(-1, channels) for a, p in zip((near, far), sides)
        )
        weight = lax.psum(weight_call(hid, slope), "lat")
        grad = grad_call(lats, state["out"], near, far)
    return grad, weight.reshape(1, KB, channels, channels)


def solution(mesh):
    in_specs = (
        P("section", None, "lat", None),
        P(None, "lat", None),
        P(None, "lat", None, None, None),
        P("lat", None),
        P("lat", None),
        P("section", None, None, None),
    )
    out_specs = (P("section", None, "lat", None), P("section", None, None, None))
    return jax.shard_map(
        per_device, mesh=mesh, in_specs=in_specs, out_specs=out_specs, check_vma=False
    )
```

```python
import functools

import jax
import jax.numpy as jnp
from jax import lax
from jax.experimental import pallas as pl
from jax.experimental.pallas import tpu as pltpu
from jax.sharding import PartitionSpec as P


KB = 3
BLK = 64
HALO = 2
MB = 2
GRP = 4
SPAN = GRP + 2 * HALO
BF = jnp.bfloat16
F32 = jnp.float32
VM = pl.BlockSpec(memory_space=pltpu.VMEM)
ANY = pl.BlockSpec(memory_space=pl.ANY)
HB = pl.BlockSpec(memory_space=pltpu.HBM)


def gelu_slope(value):
    return (
        0.5 * (1.0 + lax.erf(value * 0.7071067811865476))
        + value * jnp.exp(-0.5 * value * value) * 0.3989422804014327
    )


def params(mib=24):
    return pltpu.CompilerParams(vmem_limit_bytes=mib << 20)


def near_pairs(lats, sections, side):
    pairs = []
    for i in range(lats):
        j = i ^ 1 if side == 0 else (i + 1 if i % 2 else i - 1)
        for s in range(sections):
            other = j * sections + s if 0 <= j < lats else i * sections + (s ^ 1)
            pairs.append((i * sections + s, other))
    return pairs


def edge_pairs(lats, sections):
    both = [near_pairs(lats, sections, side) for side in range(2)]
    pairs = []
    for i in range(lats):
        for s in range(sections):
            here = i * sections + s
            if s % 2 and (i == 0 or i == lats - 1):
                pairs.append((here, i * sections + (s + 2) % sections))
            else:
                pairs.append((here, dict(both[s % 2])[here]))
    return pairs


def hop_pairs(sections, turn):
    if turn % 2:
        return [(s, s ^ 1) for s in range(sections)]
    return [(s, (s - 1) % sections) for s in range(sections)]


def mate_pairs(lats, sections, turn, side):
    pairs = []
    for i in range(lats):
        j = i ^ 1 if side == 0 else (i + 1 if i % 2 else i - 1)
        inside = 0 <= j < lats
        if turn % 2:
            p, q = (turn - 3) % sections, (turn - 2) % sections
            ways = {s: s ^ 1 for s in range(sections) if s != turn}
            if sections > 2:
                ways.update({turn - 1: p, p: q, q: turn})
            pairs += [(i * sections + s, i * sections + r) for s, r in ways.items()]
        if turn % 2 or inside:
            pairs.append((i * sections + turn, (j if inside else i) * sections + turn - 1))
    return pairs


def cost(flops):
    return pl.CostEstimate(flops=flops, bytes_accessed=flops // 256, transcendentals=0)


def dot(a, b):
    return jnp.dot(a, b, preferred_element_type=F32)


def band_kernel(
    blocks, index_in, mask_in, quad_in, band_ref, flip_ref, index_ref, mask_ref, quad_ref, table_ref, sems
):
    first = lax.axis_index("lat") * blocks
    small = [
        pltpu.make_async_copy(index_in, index_ref, sems.at[KB]),
        pltpu.make_async_copy(mask_in, mask_ref, sems.at[KB + 1]),
    ]
    large = [pltpu.make_async_copy(quad_in.at[k], quad_ref.at[k], sems.at[k]) for k in range(KB)]
    for c in small + large:
        c.start()
    for c in small:
        c.wait()
    for b in range(blocks):
        for d in range(2 * HALO + 2):
            table_ref[b, d] = 0
        for j in range(index_ref.shape[1]):
            d = index_ref[b, j] - (first + b) + HALO
            table_ref[b, jnp.where(mask_ref[b, j] != 0, d, 2 * HALO + 1)] = j + 1
    empty = jnp.zeros((BLK, BLK), BF)
    for k in range(KB):
        large[k].wait()
        for b in range(blocks):
            g, r = b // GRP, b % GRP
            tiles = [empty] * r
            for d in range(2 * HALO + 1):
                entry = table_ref[b, d]
                tile = quad_ref[k, b, jnp.maximum(entry - 1, 0)]
                tiles.append(jnp.where(entry > 0, tile, empty))
            tiles += [empty] * (GRP - 1 - r)
            half, rest = divmod(r * BLK, HALO * BLK)
            row = (half * KB + k) * HALO * BLK + rest
            band_ref[g, row : row + BLK, :] = jnp.concatenate(tiles, axis=1)
            if rest + BLK == HALO * BLK:
                part = slice(row - rest, row + BLK)
                flip_ref[g, :, part] = band_ref[g, part, :].T


def band_call(block_index, block_mask, quad):
    blocks = quad.shape[1]
    groups = blocks // GRP
    return pl.pallas_call(
        functools.partial(band_kernel, blocks),
        out_shape=(
            pltpu.VMEM((groups, KB * GRP * BLK, SPAN * BLK), BF),
            pltpu.VMEM((groups, SPAN * BLK, KB * GRP * BLK), BF),
        ),
        in_specs=[HB] * 3,
        out_specs=(VM, VM),
        scratch_shapes=[
            pltpu.SMEM(block_index.shape, jnp.int32),
            pltpu.SMEM(block_mask.shape, jnp.int32),
            pltpu.VMEM(quad.shape, BF),
            pltpu.SMEM((blocks, 2 * HALO + 2), jnp.int32),
            pltpu.SemaphoreType.DMA((KB + 2,)),
        ],
        compiler_params=params(),
        name="band",
    )(*(pltpu.with_memory_space_constraint(a, pltpu.HBM) for a in (block_index, block_mask, quad)))


def hidden_kernel(part, x_ref, band_ref, w_ref, *refs):
    hid_ref, gp_ref = refs[-2:]
    pair = HALO * BLK
    deep = KB * pair
    groups = band_ref.shape[0]
    spots = [(g, h) for g in range(groups) for h in range(2)]

    def fill(spots):
        parts = []
        for m in range(MB):
            for g, h in spots:
                at = (2 * g + h - 1) * pair
                if part == "inner":
                    window = x_ref[0, m, at : at + 3 * pair, :]
                elif g == 0:
                    window = jnp.concatenate([refs[0][m], x_ref[0, m, : 2 * pair, :]], axis=0)
                else:
                    window = jnp.concatenate([x_ref[0, m, at:, :], refs[0][m]], axis=0)
                band = band_ref[g, h * deep : (h + 1) * deep, h * pair : h * pair + 3 * pair]
                parts.append(dot(band, window).astype(BF))
                hid_ref[m, g, h * deep : (h + 1) * deep, :] = parts[-1]
        z = None
        for k in range(KB):
            rows = jnp.concatenate([p[k * pair : (k + 1) * pair] for p in parts], axis=0)
            new = dot(rows, w_ref[0, k])
            z = new if z is None else z + new
        gp = gelu_slope(z)
        for i, (m, g, h) in enumerate((m, g, h) for m in range(MB) for g, h in spots):
            gp_ref[m, (2 * g + h) * pair : (2 * g + h + 1) * pair, :] = gp[i * pair : (i + 1) * pair]

    if part == "inner":
        fill(spots[1:-1])
        return
    below = (lax.axis_index("lat") % 2 == 0) == (part == "far")
    pl.when(below)(lambda: fill(spots[:1]))
    pl.when(jnp.logical_not(below))(lambda: fill(spots[-1:]))


def hidden_call(part, x, band, weights, *rest):
    _, mb, rows, ch = x.shape
    args = (x, band, weights) + rest
    return pl.pallas_call(
        functools.partial(hidden_kernel, part),
        out_shape=(
            pltpu.VMEM((mb, band.shape[0], KB * GRP * BLK, ch), BF),
            pltpu.VMEM((mb, rows, ch), F32),
        ),
        in_specs=[VM] * len(args),
        out_specs=(VM, VM),
        input_output_aliases={4: 0, 5: 1} if rest else {},
        compiler_params=params(),
        cost_estimate=None if rest else cost(1 << 30),
    )(*args)


def rim_kernel(x_ref, far_ref, near_ref, sems):
    rows, edge = x_ref.shape[2], far_ref.shape[1]
    odd = lax.axis_index("lat") % 2
    copies = []
    for i, (high, ref) in enumerate(((odd, far_ref), (1 - odd, near_ref))):
        at = pl.multiple_of(high * (rows - edge), edge)
        copies.append(pltpu.make_async_copy(x_ref.at[0, :, pl.ds(at, edge)], ref, sems.at[i]))
        copies[-1].start()
    for c in copies:
        c.wait()


def rim_call(x):
    _, mb, _, ch = x.shape
    return pl.pallas_call(
        rim_kernel,
        out_shape=(pltpu.VMEM((mb, HALO * BLK, ch), BF),) * 2,
        in_specs=[HB],
        out_specs=(VM, VM),
        scratch_shapes=[pltpu.SemaphoreType.DMA((2,))],
        compiler_params=params(),
        name="rim",
    )(pltpu.with_memory_space_constraint(x, pltpu.HBM))


PARTS = {
    "far": ("far", "slope"),
    "near": ("near", "slope"),
    "edge": ("near", "far", "slope"),
    "slope": ("slope", "done"),
    "tips": ("near", "far"),
    "bulk": ("out",),
    "head": ("slope", "done", "out", "sent0"),
    "tail": ("near", "far", "slope", "done", "out", "sent1"),
}
MICROS = {"head": (0,), "tail": (1,)}


def back_terms(slope, w_ref, stack_ref):
    pair = HALO * BLK
    for k in range(KB):
        back = lax.dot_general(
            slope, w_ref[0, k], (((1,), (1,)), ((), ())), preferred_element_type=F32
        ).astype(BF)
        for h in range(slope.shape[0] // pair):
            stack_ref[(h * KB + k) * pair : (h * KB + k + 1) * pair, :] = back[h * pair : (h + 1) * pair]


def step_kernel(turn, lats, part, form, *refs):
    outs, stack_ref = dict(zip(PARTS[part], refs[-1 - len(PARTS[part]) :])), refs[-1]
    (gp_ref, flip_ref, w_ref), rest = refs[:3], refs[3:]
    lat = lax.axis_index("lat")
    odd = lat % 2 == 1
    rows = gp_ref.shape[1]
    size = GRP * BLK
    edge = HALO * BLK
    groups = rows // size

    micros = MICROS.get(part, range(MB))
    slope_ref = outs.get("slope", gp_ref)

    def grad_of(m, g):
        at = slice(g * size, (g + 1) * size)
        grad = (rest[m][at, :] if form == "micro" else rest[0][m, at, :]).astype(F32)
        if form == "whole":
            return grad
        near_ref, far_ref = rest[MB : MB + 2] if form == "micro" else rest[1:3]
        parts = [grad[i * edge : (i + 1) * edge] for i in range(size // edge)]
        if g == 0:
            below = jnp.where(odd, near_ref[m], far_ref[m]).astype(F32)
            parts[0] += jnp.where(lat > 0, below, 0.0)
        if g == groups - 1:
            above = jnp.where(odd, far_ref[m], near_ref[m]).astype(F32)
            parts[-1] += jnp.where(lat < lats - 1, above, 0.0)
        return jnp.concatenate(parts, axis=0).astype(BF).astype(F32)

    def tips(sides):
        deep = KB * edge
        rims = [slope_ref[m, (rows - edge) * up : (rows - edge) * up + edge, :] for m in range(MB) for up in sides]
        back_terms(jnp.concatenate(rims, axis=0), w_ref, stack_ref)
        found = []
        for i, up in enumerate(list(sides) * MB):
            band = flip_ref[groups - 1, size + edge :, deep:] if up else flip_ref[0, :edge, :deep]
            found.append(dot(band, stack_ref[i * deep : (i + 1) * deep, :]).astype(BF))
        return found

    def both_tips():
        found = tips((0, 1))
        for m in range(MB):
            below, above = found[2 * m : 2 * m + 2]
            outs["near"][m] = jnp.where(odd, below, above)
            outs["far"][m] = jnp.where(odd, above, below)

    def half(even_part):
        above = not even_part if part == "far" else even_part
        for m in range(MB):
            mine = slice(rows - edge, rows) if above else slice(0, edge)
            others = slice(edge, rows) if above else slice(0, rows - edge)
            at = mine if part == "far" else others
            grad = rest[0][m, at, :].astype(F32)
            outs["slope"][m, at, :] = (grad * gp_ref[m, at, :]).astype(BF)
        for m, found in enumerate(tips((int(above),))):
            outs[part][m] = found

    def slopes():
        for m in micros:
            for g in range(groups):
                grad = grad_of(m, g)
                at = slice(g * size, (g + 1) * size)
                outs["slope"][m, at, :] = (grad * gp_ref[m, at, :]).astype(BF)
                if "done" in outs and g == 0:
                    outs["done"][m, :edge, :] = grad[:edge].astype(BF)
                if "done" in outs and g == groups - 1:
                    outs["done"][m, edge:, :] = grad[size - edge :].astype(BF)

    def terms(m):
        deep = KB * size
        for g in range(groups):
            stack = stack_ref.at[pl.ds(g * deep, deep)]
            back_terms(slope_ref[m, g * size : (g + 1) * size, :], w_ref, stack)
        sums = [None] * (rows // edge)
        for g in range(groups):
            first = max(2 * g - 1, 0)
            last = min(2 * g + 3, len(sums))
            low = (first - (2 * g - 1)) * edge
            term = dot(flip_ref[g, low : low + (last - first) * edge, :], stack_ref[g * deep : (g + 1) * deep, :])
            for i in range(first, last):
                new = term[(i - first) * edge : (i - first + 1) * edge]
                sums[i] = new if sums[i] is None else sums[i] + new
        for i, value in enumerate(sums):
            at = slice(i * edge, (i + 1) * edge)
            grad = grad_of(m, i // 2)[(i % 2) * edge : (i % 2 + 1) * edge]
            out = (value + grad).astype(BF)
            outs["out"][m, at, :] = out
            if part in MICROS:
                outs[f"sent{m}"][at, :] = out

    @pl.when(lax.axis_index("section") == turn)
    def _():
        if part in ("far", "near"):
            pl.when(odd)(lambda: half(False))
            pl.when(jnp.logical_not(odd))(lambda: half(True))
            return
        if "slope" in outs:
            slopes()
        if "out" in outs:
            for m in micros:
                terms(m)
        if "near" in outs:
            both_tips()


def step_call(turn, lats, part, grads, flip, weights, state):
    mb, rows, ch = state["gp"].shape
    edge = HALO * BLK
    names = PARTS[part]
    known = [name for name in names if name in state]
    form = {1: "whole", 3: "summed", 4: "micro"}[len(grads)]
    factor = state["gp" if "slope" in names else "slope"]
    args = (factor, flip, weights) + grads + tuple(state[name] for name in known)
    tall = {"near": edge, "far": edge, "done": 2 * edge}
    shapes = {name: (mb, tall.get(name, rows), ch) for name in names}
    shapes.update({name: (rows, ch) for name in names if name.startswith("sent")})
    outs = pl.pallas_call(
        functools.partial(step_kernel, turn, lats, part, form),
        out_shape=tuple(pltpu.VMEM(shapes[name], BF) for name in names),
        in_specs=[VM] * len(args),
        out_specs=(VM,) * len(names),
        input_output_aliases={
            len(args) - len(known) + i: names.index(name) for i, name in enumerate(known)
        },
        scratch_shapes=[
            pltpu.VMEM((KB * max(rows, 2 * MB * edge), ch), BF),
        ],
        compiler_params=params(),
    )(*args)
    state.update(zip(names, outs))


def weight_terms(hid_ref, slope_ref, acc_ref):
    size = GRP * BLK
    edge = HALO * BLK
    for k in range(KB):
        total = None
        for m in range(MB):
            for g in range(hid_ref.shape[1]):
                pairs = [hid_ref[m, g, i * edge : (i + 1) * edge, :] for i in (k, KB + k)]
                part = lax.dot_general(
                    jnp.concatenate(pairs, axis=0),
                    slope_ref[m, g * size : (g + 1) * size, :],
                    (((0,), (0,)), ((), ())),
                    preferred_element_type=F32,
                )
                total = part if total is None else total + part
        acc_ref[k * total.shape[0] : (k + 1) * total.shape[0], :] = total


def weight_call(hid, slope):
    ch = slope.shape[2]
    return pl.pallas_call(
        weight_terms,
        out_shape=pltpu.VMEM((KB * ch, ch), F32),
        in_specs=[VM] * 2,
        out_specs=VM,
        compiler_params=params(),
        name="weight",
    )(hid, slope)


def cut_kernel(hid_ref, slope_ref, own_ref, one_ref, pair_ref, two_ref, three_ref, far_ref, acc_ref):
    weight_terms(hid_ref, slope_ref, acc_ref)
    me = lax.axis_index("lat")
    piece = own_ref.shape[0]

    def cut(bits):
        return acc_ref[pl.ds(pl.multiple_of((me ^ bits) * piece, piece), piece), :]

    own_ref[...] = cut(0)
    one_ref[...] = cut(1).astype(BF)
    for j, bits in enumerate((5, 7)):
        pair_ref[j * piece : (j + 1) * piece, :] = cut(bits).astype(BF)
    two_ref[...] = cut(2).astype(BF)
    three_ref[...] = cut(3).astype(BF)
    far_ref[:piece, :] = cut(4)
    far_ref[piece:, :] = cut(6)


def middle_kernel(far_ref, pair_ref, four_ref, six_ref):
    piece = four_ref.shape[0]
    four_ref[...] = (far_ref[:piece, :] + pair_ref[:piece, :].astype(F32)).astype(BF)
    six_ref[...] = (far_ref[piece:, :] + pair_ref[piece:, :].astype(F32)).astype(BF)


def sum_kernel(own_ref, *refs):
    total = own_ref[...]
    for ref in refs[:-1]:
        total += ref[: total.shape[0], :].astype(F32)
    refs[-1][...] = total.astype(BF)


def pack_kernel(*refs):
    at = 0
    for ref in refs[:-1]:
        for value in [ref[...]] if len(ref.shape) == 2 else [ref[m] for m in range(ref.shape[0])]:
            refs[-1][at : at + value.shape[0], :] = value
            at += value.shape[0]


def rims_kernel(got_ref, near_ref, out_ref):
    second = lax.axis_index("section") % 2 == 1
    edge = near_ref.shape[1]
    for m in range(MB):
        out_ref[m * edge : (m + 1) * edge, :] = jnp.where(second, got_ref[m], near_ref[m])


def join_kernel(spots, piece, *refs):
    refs, (weight_ref, wide_ref, sems) = refs[: len(set(s[0] for s in spots))], refs[-3:]
    me = lax.axis_index("lat")
    copies = []
    for j, (source, part, bits) in enumerate(spots):
        wide_ref[j] = refs[source][part * piece : (part + 1) * piece, :].astype(F32)
        at = pl.multiple_of((me ^ bits) * piece, piece)
        copies.append(pltpu.make_async_copy(wide_ref.at[j], weight_ref.at[pl.ds(at, piece)], sems.at[j]))
        copies[-1].start()
    for c in copies:
        c.wait()


def join_call(lats, spots, sources, old=()):
    ch = sources[0].shape[1]
    piece = KB * ch // lats
    return pl.pallas_call(
        functools.partial(join_kernel, spots, piece),
        out_shape=jax.ShapeDtypeStruct((KB * ch, ch), F32),
        in_specs=[VM] * len(sources) + [ANY] * len(old),
        out_specs=ANY,
        input_output_aliases={len(sources): 0} if old else {},
        scratch_shapes=[
            pltpu.VMEM((len(spots), piece, ch), F32),
            pltpu.SemaphoreType.DMA((len(spots),)),
        ],
        compiler_params=params(),
    )(*sources, *old)


def small_call(kernel, shapes, *args, scratch=()):
    return pl.pallas_call(
        kernel,
        out_shape=tuple(shapes),
        in_specs=[VM] * len(args),
        out_specs=(VM,) * len(shapes),
        scratch_shapes=list(scratch),
        compiler_params=params(),
    )(*args)


def reduce_weight(lats, sections, hid, state):
    near, far, slope, done = (state[name] for name in ("near", "far", "slope", "done"))
    ch = slope.shape[2]
    piece = KB * ch // lats
    edges = MB * near.shape[1]
    swap = [(s, s ^ 1) for s in range(sections)]

    def vmem(rows, dtype=BF):
        return pltpu.VMEM((rows, ch), dtype)

    def meet(a, bits):
        return lax.ppermute(a, "lat", [(i, i ^ bits) for i in range(lats)])

    shapes = (vmem(piece, F32), vmem(piece), vmem(2 * piece), vmem(piece), vmem(piece), vmem(2 * piece, F32))
    own, one, pair, two, three, half = small_call(cut_kernel, shapes, hid, slope, scratch=(vmem(KB * ch, F32),))
    pair, two, three, one = meet(pair, 1), meet(two, 2), meet(three, 3), meet(one, 1)
    got = lax.ppermute(far, "section", swap)
    four, six = small_call(middle_kernel, (vmem(piece), vmem(piece)), half, pair)
    four, six = meet(four, 4), meet(six, 6)
    (rims,) = small_call(rims_kernel, (vmem(edges),), got, near)
    rims = lax.ppermute(rims, ("lat", "section"), edge_pairs(lats, sections))
    (mine,) = small_call(sum_kernel, (vmem(piece),), own, one, two, three, four, six)
    four, six = meet(mine, 4), meet(mine, 6)
    two, three = meet(mine, 2), meet(mine, 3)
    (one,) = small_call(pack_kernel, (vmem(3 * piece),), mine, four, six)
    one = meet(one, 1)
    (aside,) = small_call(pack_kernel, (vmem(edges + MB * done.shape[1]),), rims, done)
    aside = lax.ppermute(aside, "section", swap)
    spots = [(j, 0, bits) for j, bits in enumerate((0, 2, 3, 4, 6))]
    weight = join_call(lats, spots, (mine, two, three, four, six))
    spots = [(0, j, bits) for j, bits in enumerate((1, 5, 7))]
    weight = join_call(lats, spots, (one,), (weight,))
    return weight, rims, aside


def grad_kernel(lats, main_ref, near_ref, far_ref, grad_ref):
    rows = main_ref.shape[1]
    edge = HALO * BLK
    me = lax.axis_index("lat")
    odd = me % 2 == 1
    behind = far_ref.shape[0] > MB * edge
    finished = jnp.logical_and(lax.axis_index("section") % 2 == 1, behind)
    for m in range(MB):
        near = near_ref[m * edge : (m + 1) * edge, :].astype(F32)
        far = far_ref[m * edge : (m + 1) * edge, :].astype(F32)
        below = jnp.where(me > 0, jnp.where(odd, near, far), 0.0)
        above = jnp.where(me < lats - 1, jnp.where(odd, far, near), 0.0)
        low = (main_ref[m, :edge, :].astype(F32) + below).astype(BF)
        high = (main_ref[m, rows - edge :, :].astype(F32) + above).astype(BF)
        if behind:
            at = (MB + 2 * m) * edge
            low = jnp.where(finished, far_ref[at : at + edge, :], low)
            high = jnp.where(finished, far_ref[at + edge : at + 2 * edge, :], high)
        grad_ref[0, m, :edge, :] = low
        grad_ref[0, m, edge : rows - edge, :] = main_ref[m, edge : rows - edge, :]
        grad_ref[0, m, rows - edge :, :] = high


def grad_call(lats, main, near, far):
    return pl.pallas_call(
        functools.partial(grad_kernel, lats),
        out_shape=jax.ShapeDtypeStruct((1,) + main.shape, BF),
        in_specs=[VM] * 3,
        out_specs=VM,
        compiler_params=params(),
        name="grad",
    )(main, near, far)


def per_device(saved_input, cotangent, quad_values, block_index, block_mask, weights):
    sections = lax.axis_size("section")
    lats = lax.axis_size("lat")
    both = ("lat", "section")
    sides = [near_pairs(lats, sections, side) for side in range(2)]

    def send(array, pairs, axis=both):
        return lax.ppermute(array, axis, pairs)

    far, near = rim_call(saved_input)
    far = lax.ppermute(far, both, sides[1])
    near = lax.ppermute(near, both, sides[0])
    band, flip = band_call(block_index, block_mask, quad_values)
    hid, gp = hidden_call("inner", saved_input, band, weights)
    hid, gp = hidden_call("far", saved_input, band, weights, far, hid, gp)

    state, grads = {"gp": gp}, (cotangent,)
    for turn in reversed(range(sections)):
        if turn == sections - 1:
            step_call(turn, lats, "far", grads, flip, weights, state)
            hid, gp = hidden_call("near", saved_input, band, weights, near, hid, gp)
            state["gp"] = gp
            step_call(turn, lats, "near", grads, flip, weights, state)
        elif turn == 0:
            step_call(turn, lats, "slope", grads, flip, weights, state)
            step_call(turn, lats, "tips", grads, flip, weights, state)
        elif turn % 2:
            step_call(turn, lats, "edge", grads, flip, weights, state)
        if turn % 2 or turn == 0:
            step_call(turn, lats, "bulk", grads, flip, weights, state)
            sent = {"main": state["out"]}
        else:
            step_call(turn, lats, "head", grads, flip, weights, state)
            step_call(turn, lats, "tail", grads, flip, weights, state)
            sent = {"main0": state["sent0"], "main1": state["sent1"]}
        if turn > 0:
            hop = hop_pairs(sections, turn)
            grads = tuple(send(array, hop, "section") for array in sent.values())
            far = send(state["far"], mate_pairs(lats, sections, turn, 1))
            near = send(state["near"], mate_pairs(lats, sections, turn, 0))
            grads += (near, far)

    near, far, slope = (state[name] for name in PARTS["edge"])
    channels = saved_input.shape[3]
    if lats == 8 and sections % 2 == 0:
        weight, near, far = reduce_weight(lats, sections, hid, state)
        grad = grad_call(lats, state["out"], near, far)
    else:
        near, far = (
            lax.ppermute(a, both, p).reshape(-1, channels) for a, p in zip((near, far), sides)
        )
        weight = lax.psum(weight_call(hid, slope), "lat")
        grad = grad_call(lats, state["out"], near, far)
    return grad, weight.reshape(1, KB, channels, channels)


def solution(mesh):
    in_specs = (
        P("section", None, "lat", None),
        P(None, "lat", None),
        P(None, "lat", None, None, None),
        P("lat", None),
        P("lat", None),
        P("section", None, None, None),
    )
    out_specs = (P("section", None, "lat", None), P("section", None, None, None))
    return jax.shard_map(
        per_device, mesh=mesh, in_specs=in_specs, out_specs=out_specs, check_vma=False
    )
```

```python
import functools

import jax
import jax.numpy as jnp
from jax import lax
from jax.experimental import pallas as pl
from jax.experimental.pallas import tpu as pltpu
from jax.sharding import PartitionSpec as P


KB = 3
BLK = 64
HALO = 2
MB = 2
GRP = 4
SPAN = GRP + 2 * HALO
BF = jnp.bfloat16
F32 = jnp.float32
VM = pl.BlockSpec(memory_space=pltpu.VMEM)
ANY = pl.BlockSpec(memory_space=pl.ANY)
HB = pl.BlockSpec(memory_space=pltpu.HBM)


def gelu_slope(value):
    return (
        0.5 * (1.0 + lax.erf(value * 0.7071067811865476))
        + value * jnp.exp(-0.5 * value * value) * 0.3989422804014327
    )


def params(mib=24):
    return pltpu.CompilerParams(vmem_limit_bytes=mib << 20)


def near_pairs(lats, sections, side):
    pairs = []
    for i in range(lats):
        j = i ^ 1 if side == 0 else (i + 1 if i % 2 else i - 1)
        for s in range(sections):
            other = j * sections + s if 0 <= j < lats else i * sections + (s ^ 1)
            pairs.append((i * sections + s, other))
    return pairs


def edge_pairs(lats, sections):
    both = [near_pairs(lats, sections, side) for side in range(2)]
    pairs = []
    for i in range(lats):
        for s in range(sections):
            here = i * sections + s
            if s % 2 and (i == 0 or i == lats - 1):
                pairs.append((here, i * sections + (s + 2) % sections))
            else:
                pairs.append((here, dict(both[s % 2])[here]))
    return pairs


def hop_pairs(sections, turn):
    if turn % 2:
        return [(s, s ^ 1) for s in range(sections)]
    return [(s, (s - 1) % sections) for s in range(sections)]


def mate_pairs(lats, sections, turn, side):
    pairs = []
    for i in range(lats):
        j = i ^ 1 if side == 0 else (i + 1 if i % 2 else i - 1)
        inside = 0 <= j < lats
        if turn % 2:
            p, q = (turn - 3) % sections, (turn - 2) % sections
            ways = {s: s ^ 1 for s in range(sections) if s != turn}
            if sections > 2:
                ways.update({turn - 1: p, p: q, q: turn})
            pairs += [(i * sections + s, i * sections + r) for s, r in ways.items()]
        elif sections > 2:
            ways = {s: s ^ 1 for s in range(sections) if s != turn}
            ways.update({turn - 1: turn - 2, turn - 2: turn + 1, turn + 1: turn})
            pairs += [(i * sections + s, i * sections + r) for s, r in ways.items()]
        if sections > 2 or turn % 2 or inside:
            pairs.append((i * sections + turn, (j if inside else i) * sections + turn - 1))
    return pairs


def cost(flops):
    return pl.CostEstimate(flops=flops, bytes_accessed=flops // 256, transcendentals=0)


def dot(a, b):
    return jnp.dot(a, b, preferred_element_type=F32)


def band_kernel(
    blocks, index_in, mask_in, quad_in, band_ref, flip_ref, index_ref, mask_ref, quad_ref, table_ref, sems
):
    first = lax.axis_index("lat") * blocks
    small = [
        pltpu.make_async_copy(index_in, index_ref, sems.at[KB]),
        pltpu.make_async_copy(mask_in, mask_ref, sems.at[KB + 1]),
    ]
    large = [pltpu.make_async_copy(quad_in.at[k], quad_ref.at[k], sems.at[k]) for k in range(KB)]
    for c in small + large:
        c.start()
    for c in small:
        c.wait()
    for b in range(blocks):
        for d in range(2 * HALO + 2):
            table_ref[b, d] = 0
        for j in range(index_ref.shape[1]):
            d = index_ref[b, j] - (first + b) + HALO
            table_ref[b, jnp.where(mask_ref[b, j] != 0, d, 2 * HALO + 1)] = j + 1
    empty = jnp.zeros((BLK, BLK), BF)
    for k in range(KB):
        large[k].wait()
        for b in range(blocks):
            g, r = b // GRP, b % GRP
            tiles = [empty] * r
            for d in range(2 * HALO + 1):
                entry = table_ref[b, d]
                tile = quad_ref[k, b, jnp.maximum(entry - 1, 0)]
                tiles.append(jnp.where(entry > 0, tile, empty))
            tiles += [empty] * (GRP - 1 - r)
            half, rest = divmod(r * BLK, HALO * BLK)
            row = (half * KB + k) * HALO * BLK + rest
            band_ref[g, row : row + BLK, :] = jnp.concatenate(tiles, axis=1)
            if rest + BLK == HALO * BLK:
                part = slice(row - rest, row + BLK)
                flip_ref[g, :, part] = band_ref[g, part, :].T


def band_call(block_index, block_mask, quad):
    blocks = quad.shape[1]
    groups = blocks // GRP
    return pl.pallas_call(
        functools.partial(band_kernel, blocks),
        out_shape=(
            pltpu.VMEM((groups, KB * GRP * BLK, SPAN * BLK), BF),
            pltpu.VMEM((groups, SPAN * BLK, KB * GRP * BLK), BF),
        ),
        in_specs=[HB] * 3,
        out_specs=(VM, VM),
        scratch_shapes=[
            pltpu.SMEM(block_index.shape, jnp.int32),
            pltpu.SMEM(block_mask.shape, jnp.int32),
            pltpu.VMEM(quad.shape, BF),
            pltpu.SMEM((blocks, 2 * HALO + 2), jnp.int32),
            pltpu.SemaphoreType.DMA((KB + 2,)),
        ],
        compiler_params=params(),
        name="band",
    )(*(pltpu.with_memory_space_constraint(a, pltpu.HBM) for a in (block_index, block_mask, quad)))


def hidden_kernel(part, x_ref, band_ref, w_ref, *refs):
    hid_ref, gp_ref = refs[-2:]
    pair = HALO * BLK
    deep = KB * pair
    groups = band_ref.shape[0]
    spots = [(g, h) for g in range(groups) for h in range(2)]

    def fill(spots):
        parts = []
        for m in range(MB):
            for g, h in spots:
                at = (2 * g + h - 1) * pair
                if part == "inner":
                    window = x_ref[0, m, at : at + 3 * pair, :]
                elif g == 0:
                    window = jnp.concatenate([refs[0][m], x_ref[0, m, : 2 * pair, :]], axis=0)
                else:
                    window = jnp.concatenate([x_ref[0, m, at:, :], refs[0][m]], axis=0)
                band = band_ref[g, h * deep : (h + 1) * deep, h * pair : h * pair + 3 * pair]
                parts.append(dot(band, window).astype(BF))
                hid_ref[m, g, h * deep : (h + 1) * deep, :] = parts[-1]
        z = None
        for k in range(KB):
            rows = jnp.concatenate([p[k * pair : (k + 1) * pair] for p in parts], axis=0)
            new = dot(rows, w_ref[0, k])
            z = new if z is None else z + new
        gp = gelu_slope(z)
        for i, (m, g, h) in enumerate((m, g, h) for m in range(MB) for g, h in spots):
            gp_ref[m, (2 * g + h) * pair : (2 * g + h + 1) * pair, :] = gp[i * pair : (i + 1) * pair]

    if part == "inner":
        fill(spots[1:-1])
        return
    below = (lax.axis_index("lat") % 2 == 0) == (part == "far")
    pl.when(below)(lambda: fill(spots[:1]))
    pl.when(jnp.logical_not(below))(lambda: fill(spots[-1:]))


def hidden_call(part, x, band, weights, *rest):
    _, mb, rows, ch = x.shape
    args = (x, band, weights) + rest
    return pl.pallas_call(
        functools.partial(hidden_kernel, part),
        out_shape=(
            pltpu.VMEM((mb, band.shape[0], KB * GRP * BLK, ch), BF),
            pltpu.VMEM((mb, rows, ch), F32),
        ),
        in_specs=[VM] * len(args),
        out_specs=(VM, VM),
        input_output_aliases={4: 0, 5: 1} if rest else {},
        compiler_params=params(),
        cost_estimate=None if rest else cost(1 << 30),
    )(*args)


def rim_kernel(x_ref, far_ref, near_ref, sems):
    rows, edge = x_ref.shape[2], far_ref.shape[1]
    odd = lax.axis_index("lat") % 2
    copies = []
    for i, (high, ref) in enumerate(((odd, far_ref), (1 - odd, near_ref))):
        at = pl.multiple_of(high * (rows - edge), edge)
        copies.append(pltpu.make_async_copy(x_ref.at[0, :, pl.ds(at, edge)], ref, sems.at[i]))
        copies[-1].start()
    for c in copies:
        c.wait()


def rim_call(x):
    _, mb, _, ch = x.shape
    return pl.pallas_call(
        rim_kernel,
        out_shape=(pltpu.VMEM((mb, HALO * BLK, ch), BF),) * 2,
        in_specs=[HB],
        out_specs=(VM, VM),
        scratch_shapes=[pltpu.SemaphoreType.DMA((2,))],
        compiler_params=params(),
        name="rim",
    )(pltpu.with_memory_space_constraint(x, pltpu.HBM))


PARTS = {
    "far": ("far", "slope"),
    "near": ("near", "slope"),
    "edge": ("near", "far", "slope"),
    "slope": ("slope", "done"),
    "tips": ("near", "far"),
    "bulk": ("out",),
    "head": ("slope", "done", "out", "sent0"),
    "tail": ("near", "far", "slope", "done", "out", "sent1"),
}
MICROS = {"head": (0,), "tail": (1,)}


def back_terms(slope, w_ref, stack_ref):
    pair = HALO * BLK
    for k in range(KB):
        back = lax.dot_general(
            slope, w_ref[0, k], (((1,), (1,)), ((), ())), preferred_element_type=F32
        ).astype(BF)
        for h in range(slope.shape[0] // pair):
            stack_ref[(h * KB + k) * pair : (h * KB + k + 1) * pair, :] = back[h * pair : (h + 1) * pair]


def step_kernel(turn, lats, part, form, *refs):
    outs, stack_ref = dict(zip(PARTS[part], refs[-1 - len(PARTS[part]) :])), refs[-1]
    (gp_ref, flip_ref, w_ref), rest = refs[:3], refs[3:]
    lat = lax.axis_index("lat")
    odd = lat % 2 == 1
    rows = gp_ref.shape[1]
    size = GRP * BLK
    edge = HALO * BLK
    groups = rows // size

    micros = MICROS.get(part, range(MB))
    slope_ref = outs.get("slope", gp_ref)

    def grad_of(m, g):
        at = slice(g * size, (g + 1) * size)
        grad = (rest[m][at, :] if form == "micro" else rest[0][m, at, :]).astype(F32)
        if form == "whole":
            return grad
        near_ref, far_ref = rest[MB : MB + 2] if form == "micro" else rest[1:3]
        parts = [grad[i * edge : (i + 1) * edge] for i in range(size // edge)]
        if g == 0:
            below = jnp.where(odd, near_ref[m], far_ref[m]).astype(F32)
            parts[0] += jnp.where(lat > 0, below, 0.0)
        if g == groups - 1:
            above = jnp.where(odd, far_ref[m], near_ref[m]).astype(F32)
            parts[-1] += jnp.where(lat < lats - 1, above, 0.0)
        return jnp.concatenate(parts, axis=0).astype(BF).astype(F32)

    def tips(sides):
        deep = KB * edge
        rims = [slope_ref[m, (rows - edge) * up : (rows - edge) * up + edge, :] for m in range(MB) for up in sides]
        back_terms(jnp.concatenate(rims, axis=0), w_ref, stack_ref)
        found = []
        for i, up in enumerate(list(sides) * MB):
            band = flip_ref[groups - 1, size + edge :, deep:] if up else flip_ref[0, :edge, :deep]
            found.append(dot(band, stack_ref[i * deep : (i + 1) * deep, :]).astype(BF))
        return found

    def both_tips():
        found = tips((0, 1))
        for m in range(MB):
            below, above = found[2 * m : 2 * m + 2]
            outs["near"][m] = jnp.where(odd, below, above)
            outs["far"][m] = jnp.where(odd, above, below)

    def half(even_part):
        above = not even_part if part == "far" else even_part
        for m in range(MB):
            mine = slice(rows - edge, rows) if above else slice(0, edge)
            others = slice(edge, rows) if above else slice(0, rows - edge)
            at = mine if part == "far" else others
            grad = rest[0][m, at, :].astype(F32)
            outs["slope"][m, at, :] = (grad * gp_ref[m, at, :]).astype(BF)
        for m, found in enumerate(tips((int(above),))):
            outs[part][m] = found

    def slopes():
        for m in micros:
            for g in range(groups):
                grad = grad_of(m, g)
                at = slice(g * size, (g + 1) * size)
                outs["slope"][m, at, :] = (grad * gp_ref[m, at, :]).astype(BF)
                if "done" in outs and g == 0:
                    outs["done"][m, :edge, :] = grad[:edge].astype(BF)
                if "done" in outs and g == groups - 1:
                    outs["done"][m, edge:, :] = grad[size - edge :].astype(BF)

    def terms(m):
        deep = KB * size
        for g in range(groups):
            stack = stack_ref.at[pl.ds(g * deep, deep)]
            back_terms(slope_ref[m, g * size : (g + 1) * size, :], w_ref, stack)
        sums = [None] * (rows // edge)
        for g in range(groups):
            first = max(2 * g - 1, 0)
            last = min(2 * g + 3, len(sums))
            low = (first - (2 * g - 1)) * edge
            term = dot(flip_ref[g, low : low + (last - first) * edge, :], stack_ref[g * deep : (g + 1) * deep, :])
            for i in range(first, last):
                new = term[(i - first) * edge : (i - first + 1) * edge]
                sums[i] = new if sums[i] is None else sums[i] + new
        for i, value in enumerate(sums):
            at = slice(i * edge, (i + 1) * edge)
            grad = grad_of(m, i // 2)[(i % 2) * edge : (i % 2 + 1) * edge]
            out = (value + grad).astype(BF)
            outs["out"][m, at, :] = out
            if part in MICROS:
                outs[f"sent{m}"][at, :] = out

    @pl.when(lax.axis_index("section") == turn)
    def _():
        if part in ("far", "near"):
            pl.when(odd)(lambda: half(False))
            pl.when(jnp.logical_not(odd))(lambda: half(True))
            return
        if "slope" in outs:
            slopes()
        if "out" in outs:
            for m in micros:
                terms(m)
        if "near" in outs:
            both_tips()


def step_call(turn, lats, part, grads, flip, weights, state):
    mb, rows, ch = state["gp"].shape
    edge = HALO * BLK
    names = PARTS[part]
    known = [name for name in names if name in state]
    form = {1: "whole", 3: "summed", 4: "micro"}[len(grads)]
    factor = state["gp" if "slope" in names else "slope"]
    args = (factor, flip, weights) + grads + tuple(state[name] for name in known)
    tall = {"near": edge, "far": edge, "done": 2 * edge}
    shapes = {name: (mb, tall.get(name, rows), ch) for name in names}
    shapes.update({name: (rows, ch) for name in names if name.startswith("sent")})
    outs = pl.pallas_call(
        functools.partial(step_kernel, turn, lats, part, form),
        out_shape=tuple(pltpu.VMEM(shapes[name], BF) for name in names),
        in_specs=[VM] * len(args),
        out_specs=(VM,) * len(names),
        input_output_aliases={
            len(args) - len(known) + i: names.index(name) for i, name in enumerate(known)
        },
        scratch_shapes=[
            pltpu.VMEM((KB * max(rows, 2 * MB * edge), ch), BF),
        ],
        compiler_params=params(),
    )(*args)
    state.update(zip(names, outs))


def weight_terms(hid_ref, slope_ref, acc_ref):
    size = GRP * BLK
    edge = HALO * BLK
    for k in range(KB):
        total = None
        for m in range(MB):
            for g in range(hid_ref.shape[1]):
                pairs = [hid_ref[m, g, i * edge : (i + 1) * edge, :] for i in (k, KB + k)]
                part = lax.dot_general(
                    jnp.concatenate(pairs, axis=0),
                    slope_ref[m, g * size : (g + 1) * size, :],
                    (((0,), (0,)), ((), ())),
                    preferred_element_type=F32,
                )
                total = part if total is None else total + part
        acc_ref[k * total.shape[0] : (k + 1) * total.shape[0], :] = total


def weight_call(hid, slope):
    ch = slope.shape[2]
    return pl.pallas_call(
        weight_terms,
        out_shape=pltpu.VMEM((KB * ch, ch), F32),
        in_specs=[VM] * 2,
        out_specs=VM,
        compiler_params=params(),
        name="weight",
    )(hid, slope)


def cut_kernel(hid_ref, slope_ref, own_ref, one_ref, pair_ref, two_ref, three_ref, far_ref, acc_ref):
    weight_terms(hid_ref, slope_ref, acc_ref)
    me = lax.axis_index("lat")
    piece = own_ref.shape[0]

    def cut(bits):
        return acc_ref[pl.ds(pl.multiple_of((me ^ bits) * piece, piece), piece), :]

    own_ref[...] = cut(0)
    one_ref[...] = cut(1).astype(BF)
    for j, bits in enumerate((5, 7)):
        pair_ref[j * piece : (j + 1) * piece, :] = cut(bits).astype(BF)
    two_ref[...] = cut(2).astype(BF)
    three_ref[...] = cut(3).astype(BF)
    far_ref[:piece, :] = cut(4)
    far_ref[piece:, :] = cut(6)


def middle_kernel(far_ref, pair_ref, four_ref, six_ref):
    piece = four_ref.shape[0]
    four_ref[...] = (far_ref[:piece, :] + pair_ref[:piece, :].astype(F32)).astype(BF)
    six_ref[...] = (far_ref[piece:, :] + pair_ref[piece:, :].astype(F32)).astype(BF)


def sum_kernel(own_ref, *refs):
    total = own_ref[...]
    for ref in refs[:-1]:
        total += ref[: total.shape[0], :].astype(F32)
    refs[-1][...] = total.astype(BF)


def pack_kernel(*refs):
    at = 0
    for ref in refs[:-1]:
        for value in [ref[...]] if len(ref.shape) == 2 else [ref[m] for m in range(ref.shape[0])]:
            refs[-1][at : at + value.shape[0], :] = value
            at += value.shape[0]


def rims_kernel(got_ref, near_ref, out_ref):
    second = lax.axis_index("section") % 2 == 1
    edge = near_ref.shape[1]
    for m in range(MB):
        out_ref[m * edge : (m + 1) * edge, :] = jnp.where(second, got_ref[m], near_ref[m])


def join_kernel(spots, piece, *refs):
    refs, (weight_ref, wide_ref, sems) = refs[: len(set(s[0] for s in spots))], refs[-3:]
    me = lax.axis_index("lat")
    copies = []
    for j, (source, part, bits) in enumerate(spots):
        wide_ref[j] = refs[source][part * piece : (part + 1) * piece, :].astype(F32)
        at = pl.multiple_of((me ^ bits) * piece, piece)
        copies.append(pltpu.make_async_copy(wide_ref.at[j], weight_ref.at[pl.ds(at, piece)], sems.at[j]))
        copies[-1].start()
    for c in copies:
        c.wait()


def join_call(lats, spots, sources, old=()):
    ch = sources[0].shape[1]
    piece = KB * ch // lats
    return pl.pallas_call(
        functools.partial(join_kernel, spots, piece),
        out_shape=jax.ShapeDtypeStruct((KB * ch, ch), F32),
        in_specs=[VM] * len(sources) + [ANY] * len(old),
        out_specs=ANY,
        input_output_aliases={len(sources): 0} if old else {},
        scratch_shapes=[
            pltpu.VMEM((len(spots), piece, ch), F32),
            pltpu.SemaphoreType.DMA((len(spots),)),
        ],
        compiler_params=params(),
    )(*sources, *old)


def small_call(kernel, shapes, *args, scratch=()):
    return pl.pallas_call(
        kernel,
        out_shape=tuple(shapes),
        in_specs=[VM] * len(args),
        out_specs=(VM,) * len(shapes),
        scratch_shapes=list(scratch),
        compiler_params=params(),
    )(*args)


def reduce_weight(lats, sections, hid, state):
    near, far, slope, done = (state[name] for name in ("near", "far", "slope", "done"))
    ch = slope.shape[2]
    piece = KB * ch // lats
    edges = MB * near.shape[1]
    swap = [(s, s ^ 1) for s in range(sections)]

    def vmem(rows, dtype=BF):
        return pltpu.VMEM((rows, ch), dtype)

    def meet(a, bits):
        return lax.ppermute(a, "lat", [(i, i ^ bits) for i in range(lats)])

    shapes = (vmem(piece, F32), vmem(piece), vmem(2 * piece), vmem(piece), vmem(piece), vmem(2 * piece, F32))
    own, one, pair, two, three, half = small_call(cut_kernel, shapes, hid, slope, scratch=(vmem(KB * ch, F32),))
    pair, two, three, one = meet(pair, 1), meet(two, 2), meet(three, 3), meet(one, 1)
    got = lax.ppermute(far, "section", swap)
    four, six = small_call(middle_kernel, (vmem(piece), vmem(piece)), half, pair)
    four, six = meet(four, 4), meet(six, 6)
    (rims,) = small_call(rims_kernel, (vmem(edges),), got, near)
    rims = lax.ppermute(rims, ("lat", "section"), edge_pairs(lats, sections))
    (mine,) = small_call(sum_kernel, (vmem(piece),), own, one, two, three, four, six)
    four, six = meet(mine, 4), meet(mine, 6)
    two, three = meet(mine, 2), meet(mine, 3)
    (one,) = small_call(pack_kernel, (vmem(3 * piece),), mine, four, six)
    one = meet(one, 1)
    (aside,) = small_call(pack_kernel, (vmem(edges + MB * done.shape[1]),), rims, done)
    aside = lax.ppermute(aside, "section", swap)
    spots = [(j, 0, bits) for j, bits in enumerate((0, 2, 3, 4, 6))]
    weight = join_call(lats, spots, (mine, two, three, four, six))
    spots = [(0, j, bits) for j, bits in enumerate((1, 5, 7))]
    weight = join_call(lats, spots, (one,), (weight,))
    return weight, rims, aside


def grad_kernel(lats, main_ref, near_ref, far_ref, grad_ref):
    rows = main_ref.shape[1]
    edge = HALO * BLK
    me = lax.axis_index("lat")
    odd = me % 2 == 1
    behind = far_ref.shape[0] > MB * edge
    finished = jnp.logical_and(lax.axis_index("section") % 2 == 1, behind)
    for m in range(MB):
        near = near_ref[m * edge : (m + 1) * edge, :].astype(F32)
        far = far_ref[m * edge : (m + 1) * edge, :].astype(F32)
        below = jnp.where(me > 0, jnp.where(odd, near, far), 0.0)
        above = jnp.where(me < lats - 1, jnp.where(odd, far, near), 0.0)
        low = (main_ref[m, :edge, :].astype(F32) + below).astype(BF)
        high = (main_ref[m, rows - edge :, :].astype(F32) + above).astype(BF)
        if behind:
            at = (MB + 2 * m) * edge
            low = jnp.where(finished, far_ref[at : at + edge, :], low)
            high = jnp.where(finished, far_ref[at + edge : at + 2 * edge, :], high)
        grad_ref[0, m, :edge, :] = low
        grad_ref[0, m, edge : rows - edge, :] = main_ref[m, edge : rows - edge, :]
        grad_ref[0, m, rows - edge :, :] = high


def grad_call(lats, main, near, far):
    return pl.pallas_call(
        functools.partial(grad_kernel, lats),
        out_shape=jax.ShapeDtypeStruct((1,) + main.shape, BF),
        in_specs=[VM] * 3,
        out_specs=VM,
        compiler_params=params(),
        name="grad",
    )(main, near, far)


def per_device(saved_input, cotangent, quad_values, block_index, block_mask, weights):
    sections = lax.axis_size("section")
    lats = lax.axis_size("lat")
    both = ("lat", "section")
    sides = [near_pairs(lats, sections, side) for side in range(2)]

    def send(array, pairs, axis=both):
        return lax.ppermute(array, axis, pairs)

    far, near = rim_call(saved_input)
    far = lax.ppermute(far, both, sides[1])
    near = lax.ppermute(near, both, sides[0])
    band, flip = band_call(block_index, block_mask, quad_values)
    hid, gp = hidden_call("inner", saved_input, band, weights)
    hid, gp = hidden_call("far", saved_input, band, weights, far, hid, gp)

    state, grads = {"gp": gp}, (cotangent,)
    for turn in reversed(range(sections)):
        if turn == sections - 1:
            step_call(turn, lats, "far", grads, flip, weights, state)
            hid, gp = hidden_call("near", saved_input, band, weights, near, hid, gp)
            state["gp"] = gp
            step_call(turn, lats, "near", grads, flip, weights, state)
        elif turn == 0:
            step_call(turn, lats, "slope", grads, flip, weights, state)
            step_call(turn, lats, "tips", grads, flip, weights, state)
        elif turn % 2:
            step_call(turn, lats, "edge", grads, flip, weights, state)
        if turn % 2 or turn == 0:
            step_call(turn, lats, "bulk", grads, flip, weights, state)
            sent = {"main": state["out"]}
        else:
            step_call(turn, lats, "head", grads, flip, weights, state)
            step_call(turn, lats, "tail", grads, flip, weights, state)
            sent = {"main0": state["sent0"], "main1": state["sent1"]}
        if turn > 0:
            hop = hop_pairs(sections, turn)
            grads = tuple(send(array, hop, "section") for array in sent.values())
            far = send(state["far"], mate_pairs(lats, sections, turn, 1))
            near = send(state["near"], mate_pairs(lats, sections, turn, 0))
            grads += (near, far)

    near, far, slope = (state[name] for name in PARTS["edge"])
    channels = saved_input.shape[3]
    if lats == 8 and sections % 2 == 0:
        weight, near, far = reduce_weight(lats, sections, hid, state)
        grad = grad_call(lats, state["out"], near, far)
    else:
        near, far = (
            lax.ppermute(a, both, p).reshape(-1, channels) for a, p in zip((near, far), sides)
        )
        weight = lax.psum(weight_call(hid, slope), "lat")
        grad = grad_call(lats, state["out"], near, far)
    return grad, weight.reshape(1, KB, channels, channels)


def solution(mesh):
    in_specs = (
        P("section", None, "lat", None),
        P(None, "lat", None),
        P(None, "lat", None, None, None),
        P("lat", None),
        P("lat", None),
        P("section", None, None, None),
    )
    out_specs = (P("section", None, "lat", None), P("section", None, None, None))
    return jax.shard_map(
        per_device, mesh=mesh, in_specs=in_specs, out_specs=out_specs, check_vma=False
    )
```
